256 devices in a mesh: group: 4 (over x), leaf: 64 (over z, y, core).
Axes of the slice: x: 4, y: 4, z: 8, core: 2. Of those that a mesh axis runs over, the one named last changes fastest.
Arguments:
- right_sides: float32 [16, 1048576], P(None, ('group', 'leaf')), may hold values from -6 to 6
- near_blocks: float32 [16384, 8, 4096], P(('group', 'leaf')), may hold values from -0.375 to 0.375
- near_source: int32 [16384, 8], P(('group', 'leaf')), may hold values from 0 to 16383, as said below
- near_count: int32 [16384], P(('group', 'leaf')), may hold values from 1 to 8
- basis: float32 [16384, 2048], P(('group', 'leaf')), may hold values from -0.75 to 0.75
- leaf_source: int32 [16384, 8], P(('group', 'leaf')), may hold values from 0 to 16383
- leaf_coupling: float32 [16384, 8, 1024], P(('group', 'leaf')), may hold values from -0.375 to 0.375
- leaf_transfer: float32 [16384, 1024], P(('group', 'leaf')), may hold values from -1 to 1
- cluster_source: int32 [1024, 8], P(('group', 'leaf')), may hold values from 0 to 255
- cluster_coupling: float32 [1024, 8, 1024], P(('group', 'leaf')), may hold values from -0.09375 to 0.09375
- cluster_transfer: float32 [1024, 1024], P(('group', 'leaf')), may hold values from -1 to 1
- group_coupling: float32 [4, 4, 1024], P('group'), may hold values from -0.0078125 to 0.0078125
Outputs:
- applied: float32 [16, 1048576], P(None, ('group', 'leaf'))
The draws below stay inside these ranges and needn't reach their ends.
Inputs may be any that keep to these rules, and one draw needn't show every extreme that they name: near_source[t, j] and leaf_source[t, j] name a leaf held by the same device as t or by the device just before or after it in the order of devices.
All inputs are finite; a program needn't handle non-finite values.
Results may differ from the reference program's by a relative error of at most 0.0001.
Values sent between devices are 32-bit elements; how exact they have to be, the bound alone decides.
No kernel may reach another device: no remote copies, remote signals or barrier semaphores. Data moves between devices by JAX's collectives and lax.ppermute only.
A program may use at most 128 MiB of HBM per device.

```python
import jax
import jax.numpy as jnp
from jax import lax

LEAF = 64
K = 32
RHS = 16
LPD = 64
CPD = 4
NEAR = 8
FAR0 = 8
FAR1 = 8
DEVS = 256
GROUPS = 4
LEAVES = 16384
POINTS = 1048576
CLUSTERS_ALL = 1024
GROUP_CLUSTERS = 256


def window_sources(key, slots):
    leaf_ids = jnp.arange(LEAVES, dtype=jnp.int32)
    first_leaf = leaf_ids // LPD * LPD
    offsets = jax.random.randint(key, (LEAVES, slots), -LPD, 2 * LPD)
    chosen = jnp.clip(first_leaf[:, None] + offsets, 0, LEAVES - 1)
    chosen = chosen.at[0, 0].set(0)
    chosen = chosen.at[LEAVES - 1, slots - 1].set(LEAVES - 1)
    return chosen.astype(jnp.int32)


def draw_near_source(key, part):
    return window_sources(jax.random.fold_in(key, 11), NEAR)


def draw_leaf_source(key, part):
    return window_sources(jax.random.fold_in(key, 12), FAR0)


def draw_near_count(key, part):
    first_key = jax.random.fold_in(key, 21)
    second_key = jax.random.fold_in(key, 22)
    ceilings = jax.random.randint(first_key, (DEVS,), 1, NEAR + 1).at[0].set(NEAR)
    per_leaf = jnp.repeat(ceilings, LPD)
    raw_values = jax.random.randint(second_key, (LEAVES,), 0, 1048576)
    counts = raw_values % per_leaf + 1
    counts = counts.at[0].set(NEAR)
    return counts.astype(jnp.int32)


def plant(entries, rng, least, high):
    shape = entries.shape
    place = [jax.random.randint(jax.random.fold_in(rng, axis), (), 0, shape[axis]) for axis in range(len(shape))]
    entries = entries.at[tuple(place)].set(least)
    longest = shape.index(max(shape))
    place[longest] = (place[longest] + 1) % shape[longest]
    return entries.at[tuple(place)].set(high)


def levels(key, shape, pieces, low, top_value):
    factor_of, own = 1.0, jax.random.fold_in(key, 6)
    for position, blocks in pieces:
        steps = jnp.exp(jax.random.uniform(jax.random.fold_in(own, position), (blocks,), jnp.float32, low / len(pieces), top_value / len(pieces)))
        factor_of = factor_of * jnp.repeat(steps, shape[position] // blocks).reshape([-1 if axis == position else 1 for axis in range(len(shape))])
    return factor_of


def centred(stream_key, dims, deviation, reach, split=(), held_as=jnp.bfloat16):
    result = jax.random.normal(stream_key, dims, jnp.float32) * deviation
    if len(split) > 0:
        result = levels(stream_key, dims, split, -0.22, 0.18) * result
    return jnp.clip(result, min=-reach, max=reach).astype(held_as)


def setup_inputs(seed: int = 0) -> dict:
    key_of = jax.random.split(jax.random.key(seed), 13)
    right_sides = centred(key_of[0], (RHS, POINTS), 1.0, 6.0, ((1, 256),), jnp.float32)
    near_blocks = centred(key_of[1], (LEAVES, NEAR, LEAF * LEAF), (LEAF * NEAR // 2) ** -0.5, 0.375, ((0, 256),), jnp.float32)
    near_source = draw_near_source(jax.random.fold_in(key_of[12], 71), 0)
    near_count = draw_near_count(jax.random.fold_in(key_of[12], 71), 0)
    basis = centred(key_of[4], (LEAVES, K * LEAF), LEAF ** -0.5, 0.75, ((0, 256),), jnp.float32)
    leaf_source = draw_leaf_source(jax.random.fold_in(key_of[12], 71), 0)
    leaf_coupling = centred(key_of[6], (LEAVES, FAR0, K * K), (K * FAR0) ** -0.5, 0.375, ((0, 256),), jnp.float32)
    leaf_transfer = centred(key_of[7], (LEAVES, K * K), K ** -0.5, 1.0, ((0, 256),), jnp.float32)
    cluster_source = plant(jax.random.randint(key_of[8], (CLUSTERS_ALL, FAR1), 0, GROUP_CLUSTERS), jax.random.fold_in(key_of[8], 1), 0, GROUP_CLUSTERS - 1).astype(jnp.int32)
    cluster_coupling = centred(key_of[9], (CLUSTERS_ALL, FAR1, K * K), (K * FAR1 * LPD // CPD) ** -0.5, 0.09375, ((0, 256),), jnp.float32)
    cluster_transfer = centred(key_of[10], (CLUSTERS_ALL, K * K), K ** -0.5, 1.0, ((0, 256),), jnp.float32)
    group_coupling = centred(key_of[11], (GROUPS, GROUPS, K * K), (K * GROUPS * LPD * GROUP_CLUSTERS // CPD) ** -0.5, 0.0078125, ((0, 4),), jnp.float32)
    return {"right_sides": right_sides, "near_blocks": near_blocks, "near_source": near_source, "near_count": near_count, "basis": basis, "leaf_source": leaf_source, "leaf_coupling": leaf_coupling, "leaf_transfer": leaf_transfer, "cluster_source": cluster_source, "cluster_coupling": cluster_coupling, "cluster_transfer": cluster_transfer, "group_coupling": group_coupling}


highest_precision = lax.Precision.HIGHEST


def reference(right_sides, near_blocks, near_source, near_count, basis, leaf_source, leaf_coupling, leaf_transfer, cluster_source, cluster_coupling, cluster_transfer, group_coupling):
    blocks = right_sides.reshape(RHS, LEAVES, LEAF).transpose(1, 0, 2)
    bases = basis.reshape(LEAVES, K, LEAF)
    leaf_coef = jnp.einsum('tka,tra->tkr', bases, blocks, precision=highest_precision)

    def near_step(slot_index, running):
        picked = jnp.take(blocks, near_source[:, slot_index], axis=0)
        slab = lax.dynamic_index_in_dim(near_blocks, slot_index, axis=1, keepdims=False).reshape(LEAVES, LEAF, LEAF)
        live = (near_count > slot_index).astype(jnp.float32)
        term = jnp.einsum('tab,trb->tra', slab, picked, precision=highest_precision)
        return running + term * live[:, None, None]

    near_total = lax.fori_loop(0, NEAR, near_step, jnp.zeros((LEAVES, RHS, LEAF), jnp.float32))

    picked_coef = jnp.take(leaf_coef, leaf_source, axis=0)
    leaf_far = jnp.einsum('tjkl,tjlr->tkr', leaf_coupling.reshape(LEAVES, FAR0, K, K), picked_coef, precision=highest_precision)

    transfers = leaf_transfer.reshape(LEAVES, K, K)
    lifted = jnp.einsum('tkl,tlr->tkr', transfers, leaf_coef, precision=highest_precision)
    cluster_coef = lifted.reshape(CLUSTERS_ALL, LPD // CPD, K, RHS).sum(axis=1)
    upper = cluster_transfer.reshape(CLUSTERS_ALL, K, K)
    projected = jnp.einsum('ukl,ulr->ukr', upper, cluster_coef, precision=highest_precision)
    group_coef = projected.reshape(GROUPS, GROUP_CLUSTERS, K, RHS).sum(axis=1)
    group_field = jnp.einsum('ghkl,hlr->gkr', group_coupling.reshape(GROUPS, GROUPS, K, K), group_coef, precision=highest_precision)

    owners = (jnp.arange(CLUSTERS_ALL, dtype=jnp.int32) // GROUP_CLUSTERS) * GROUP_CLUSTERS
    global_source = owners[:, None] + cluster_source
    picked_cluster = jnp.take(cluster_coef, global_source, axis=0)
    cluster_far = jnp.einsum('ujkl,ujlr->ukr', cluster_coupling.reshape(CLUSTERS_ALL, FAR1, K, K), picked_cluster, precision=highest_precision)
    spread_top = jnp.repeat(group_field, GROUP_CLUSTERS, axis=0)
    cluster_field = cluster_far + jnp.einsum('ulk,ulr->ukr', upper, spread_top, precision=highest_precision)
    spread_cluster = jnp.repeat(cluster_field, LPD // CPD, axis=0)
    leaf_field = leaf_far + jnp.einsum('tlk,tlr->tkr', transfers, spread_cluster, precision=highest_precision)
    total = near_total + jnp.einsum('tka,tkr->tra', bases, leaf_field, precision=highest_precision)
    return total.transpose(1, 0, 2).reshape(RHS, POINTS)
```

```python
import jax
import jax.numpy as jnp
from jax import lax
from jax.experimental import pallas as pl
from jax.experimental.pallas import tpu as pltpu
from jax.sharding import PartitionSpec as P

LEAF=64;K=32;RHS=16
f32=jnp.float32; bf16=jnp.bfloat16
NT=(((1,),(1,)),((),()))
def split(a):
    h=a.astype(bf16)
    return h,(a-h.astype(f32)).astype(bf16)
def dotnt(a,b): return lax.dot_general(a,b,NT,preferred_element_type=f32)
def dotnn(a,b): return lax.dot_general(a,b,(((1,),(0,)),((),())),preferred_element_type=f32)

def point_pairs(x_ref, first, pairs, hi, lo):
    lane=lax.broadcasted_iota(jnp.int32,(RHS,128),1)
    left=lane<LEAF
    zero=jnp.zeros((RHS,128),f32)
    def body(q,_):
        x=x_ref[:,pl.ds(pl.multiple_of(q*128,128),128)]
        y=pltpu.roll(x,LEAF,1)
        for n,(a,b) in enumerate(((x,y),(y,x))):
            blk=jnp.concatenate([jnp.where(left,a,zero),jnp.where(left,zero,b)],axis=0)
            h,l=split(blk)
            hi[first+2*q+n]=h
            lo[first+2*q+n]=l
        return 0
    lax.fori_loop(0,pairs,body,0,unroll=4)

def near_kernel(base, src, cnt, xb, xo, xa, nb, out, hi, lo, weave):
    g=pl.program_id(0)
    n=xo.shape[1]//LEAF
    @pl.when(g==0)
    def _():
        point_pairs(xb,0,n//2,hi,lo)
        point_pairs(xo,n,n//2,hi,lo)
        point_pairs(xa,2*n,n//2,hi,lo)
        hi[3*n]=jnp.zeros((2*RHS,128),bf16)
        lo[3*n]=jnp.zeros((2*RHS,128),bf16)
        row=lax.broadcasted_iota(jnp.int32,(256,256),0)
        col=lax.broadcasted_iota(jnp.int32,(256,256),1)
        a=lax.rem(col,64)
        want=lax.rem(a,2)*128+(col//64)*32+a//2
        weave[...]=(row==want).astype(f32).astype(bf16)
    per=nb.shape[0]//256
    for quad in range(per//4):
        parts=[]
        for m in range(4):
            i=quad*4+m
            a=jnp.concatenate([nb[pl.ds(i*256+j,32,stride=8),:] for j in range(8)],axis=1)
            ah,al=split(a)
            t=g*per+i
            live=cnt[t]
            at=[jnp.where(j<live,src[t,j]-base[0],3*n) for j in range(8)]
            xh=jnp.concatenate([hi[s] for s in at],axis=1)
            xl=jnp.concatenate([lo[s] for s in at],axis=1)
            d=dotnt(jnp.concatenate([xh,xl],axis=0),ah)
            parts.append(d[:2*RHS]+d[2*RHS:]+dotnt(xh,al))
        m4=jnp.concatenate(parts,axis=1)
        m4=jnp.concatenate([m4[:RHS],m4[RHS:]],axis=1)
        h,l=split(m4)
        out[:,pl.ds(pl.multiple_of((g*per+quad*4)*LEAF,256),256)]=dotnn(h,weave[...])+dotnn(l,weave[...])

def near(base,src,cnt,xb,xo,xa,nb,steps=8):
    leaves=nb.shape[0]
    view=nb.reshape(leaves,8,32,128).transpose(0,2,1,3).reshape(leaves*256,128)
    blk=leaves*256//steps
    full=lambda g,*_:(0,0)
    return pl.pallas_call(near_kernel,
        out_shape=jax.ShapeDtypeStruct(xo.shape,f32),
        grid_spec=pltpu.PrefetchScalarGridSpec(num_scalar_prefetch=3,grid=(steps,),
            in_specs=[pl.BlockSpec(xb.shape,full)]*3+[pl.BlockSpec((blk,128),lambda g,*_:(g,0))],
            out_specs=pl.BlockSpec(xo.shape,full),
            scratch_shapes=[pltpu.VMEM((3*leaves+1,32,128),bf16)]*2+[pltpu.VMEM((256,256),bf16)]),
        compiler_params=pltpu.CompilerParams(vmem_limit_bytes=40<<20),
        name="near")(base,src,cnt,xb,xo,xa,view)


def iota(shape,d): return lax.broadcasted_iota(jnp.int32,shape,d)
def onehot(cond): return cond.astype(f32).astype(bf16)
def exact(v,m):
    h,l=split(v)
    return dotnn(h,m)+dotnn(l,m)
def spread4(tile,m):
    block=jnp.where(iota(tile.shape,1)//K==m,tile,0.0)
    block=block+pltpu.roll(block,64,1)
    return block+pltpu.roll(block,32,1)
def masked4(rows):
    lane=lax.rem(iota(rows.shape,1),128)//K
    both=jnp.concatenate([jnp.where(lane==m,rows,0.0) for m in range(4)],axis=0)
    return split(both)
def mul3(v,w):
    h,l=split(v)
    d=dotnt(jnp.concatenate([h,l],axis=0),w[0])
    return d[:RHS]+d[RHS:]+dotnt(h,w[1])

def up_kernel(x,bas,tra,upt,coef,pay,fs):
    lane=iota((RHS,128),1)
    left=lane<LEAF
    n=x.shape[1]//LEAF
    row=iota((256,256),0); col=iota((256,256),1)
    k2=lax.rem(row,128)//8
    s2=onehot(col==lax.rem(row,8)*32+2*k2+row//128)
    same=(iota((256,128),0)//32==lax.rem(iota((256,128),1),8))
    v4=[]
    for g in range(n//8):
        blks=[]
        for q in range(4):
            t=x[:,pl.ds((g*4+q)*128,128)]
            y=pltpu.roll(t,LEAF,1)
            for a,b in ((t,y),(y,t)):
                blks+= [jnp.where(left,a,0.0),jnp.where(left,0.0,b)]
        xh,xl=split(jnp.concatenate(blks,axis=0))
        bh,bl=split(bas[pl.ds(g*128,128),:])
        d=dotnt(xh,bh)+dotnt(xl,bh)+dotnt(xh,bl)
        d=jnp.where(same,d,0.0).reshape(8,32,128).sum(axis=0)
        c=exact(jnp.concatenate([d[:RHS],d[RHS:]],axis=1),s2)
        coef[:,pl.ds(g*256,256)]=c
        for i in range(8):
            v4.append(spread4(c[:,(i//4)*128:(i//4)*128+128],i%4))
    nc=upt.shape[0]
    per=n//nc
    outs=[]
    for u in range(nc):
        e=jnp.concatenate([tra[pl.ds(((u*per+i)//8)*64+(u*per+i)%8,8,stride=8),:] for i in range(per)],axis=1)
        outs.append(mul3(jnp.concatenate(v4[u*per:(u+1)*per],axis=1),masked4(e)))
    row=iota((128,128),0); col=iota((128,128),1)
    s3=onehot(col==row//32*32+lax.rem(row,8)*4+lax.rem(row,32)//8)
    cc=exact(jnp.concatenate(outs,axis=1),s3)
    pay[0:RHS,:]=cc
    for q in range(8):
        fs[pl.ds(q*nc,nc),:]=upt[:,pl.ds(q*128,128)]
    f=jnp.concatenate([fs[pl.ds(u,8,stride=nc),:] for u in range(nc)],axis=1)
    pr=mul3(jnp.concatenate([spread4(cc,u) for u in range(nc)],axis=1),masked4(f))
    pay[RHS:,:]=jnp.concatenate([jnp.concatenate([pr[0:8],pr[8:16]],axis=1),jnp.zeros((8,64),f32)],axis=1)

def up(x,basis,transfer,upper):
    n=basis.shape[0]
    bas=basis.reshape(n//8,8,16,128).transpose(0,2,1,3).reshape(n*16,128)
    tra=transfer.reshape(n//8,8,8,128).transpose(0,2,1,3).reshape(n*8,128)
    return pl.pallas_call(up_kernel,
        out_shape=(jax.ShapeDtypeStruct((RHS,n*K),f32),jax.ShapeDtypeStruct((24,128),f32)),
        scratch_shapes=[pltpu.VMEM((8*upper.shape[0],128),f32)],
        compiler_params=pltpu.CompilerParams(vmem_limit_bytes=24<<20),name="up")(x,bas,tra,upper)

def far_kernel(base,src,cb,co,ca,cpl,out,hi,lo):
    g=pl.program_id(0)
    tiles=co.shape[1]//128
    @pl.when(g==0)
    def _():
        for w,ref in enumerate((cb,co,ca)):
            def body(q,_):
                t=ref[:,pl.ds(pl.multiple_of(q*128,128),128)]
                for m in range(4):
                    h,l=split(spread4(t,m))
                    hi[(w*tiles+q)*4+m]=h
                    lo[(w*tiles+q)*4+m]=l
                return 0
            lax.fori_loop(0,tiles,body,0,unroll=4)
    per=cpl.shape[0]//64
    for i in range(per):
        c=jnp.concatenate([cpl[pl.ds(i*64+j,8,stride=8),:] for j in range(8)],axis=1)
        wh,wl=masked4(c)
        at=[src[g*per+i,j]-base[0] for j in range(8)]
        vh=jnp.concatenate([hi[s] for s in at],axis=1)
        vl=jnp.concatenate([lo[s] for s in at],axis=1)
        d=dotnt(jnp.concatenate([vh,vl],axis=0),wh)
        out[pl.ds(i*RHS,RHS),:]=d[:RHS]+d[RHS:]+dotnt(vh,wl)

def far(base,src,cb,co,ca,coupling,steps=8):
    n=coupling.shape[0]
    view=coupling.reshape(n,8,8,128).transpose(0,2,1,3).reshape(n*64,128)
    full=lambda g,*_:(0,0)
    return pl.pallas_call(far_kernel,
        out_shape=jax.ShapeDtypeStruct((n*RHS,K),f32),
        grid_spec=pltpu.PrefetchScalarGridSpec(num_scalar_prefetch=2,grid=(steps,),
            in_specs=[pl.BlockSpec(co.shape,full)]*3+[pl.BlockSpec((n*64//steps,128),lambda g,*_:(g,0))],
            out_specs=pl.BlockSpec((n*RHS//steps,K),lambda g,*_:(g,0)),
            scratch_shapes=[pltpu.VMEM((3*n,RHS,128),bf16)]*2),
        compiler_params=pltpu.CompilerParams(vmem_limit_bytes=24<<20),name="far")(base,src,cb,co,ca,view)

def down_kernel(csrc,pays,sums,gcp,ccp,upt,tra,bas,lf,near_ref,out,gs,fs):
    nc=upt.shape[0]; ng=gcp.shape[0]
    n=lf.shape[0]//RHS
    devs=pays.shape[0]//24
    row=iota((K,128),0); col=lax.rem(iota((K,128),1),K)
    s4=onehot(col==lax.rem(row,8)*4+row//8)
    for q in range(8):
        fs[pl.ds(q*nc,nc),:]=upt[:,pl.ds(q*128,128)]
        gs[pl.ds(q*ng,ng),:]=gcp[:,pl.ds(q*128,128)]
    gv=[]
    for h in range(ng):
        t=sums[pl.ds(h*8,8),:]
        gv.append(exact(jnp.concatenate([t[:,0:K],t[:,K:2*K]],axis=0),s4))
    gw=jnp.concatenate([gs[pl.ds(h,8,stride=ng),:] for h in range(ng)],axis=1)
    gf=mul3(jnp.concatenate(gv,axis=1),masked4(gw))
    fw=jnp.concatenate([fs[pl.ds(u,8,stride=nc),:] for u in range(nc)],axis=1)
    wh,wl=masked4(fw)
    gh,gl=split(gf)
    down=dotnn(gh,wh)+dotnn(gl,wh)+dotnn(gh,wl)
    row=lax.rem(iota((128,K),0),K); col=iota((128,K),1)
    s5=onehot(row==lax.rem(col,8)*4+col//8)
    down=jnp.concatenate([down[:,u*128:(u+1)*128] for u in range(nc)],axis=0)
    down=exact(down,s5)
    row=lax.rem(iota((128,256),0),K); col=iota((128,256),1)
    p1=onehot(row==2*(lax.rem(col,128)//8)+col//128)
    row=iota((K,256),0); col=iota((K,256),1)
    nat=2*(lax.rem(col,128)//8)+col//128
    p2=onehot(row==lax.rem(nat,4)*8+nat//4)
    left=iota((RHS,128),1)<LEAF
    per=n//nc
    for u in range(nc):
        w=jnp.concatenate([ccp[pl.ds(u*64+j,8,stride=8),:] for j in range(8)],axis=1)
        vs=[]
        for j in range(8):
            s=csrc[u,j]
            place=lax.rem(s//nc,2)*(devs//2)+s//(2*nc)
            vs.append(spread4(pays[pl.ds(pl.multiple_of(place*24,8),RHS),:],lax.rem(s,nc)))
        cf=mul3(jnp.concatenate(vs,axis=1),masked4(w))+down[u*RHS:(u+1)*RHS]
        e=jnp.concatenate([tra[pl.ds(((u*per+i)//8)*64+(u*per+i)%8,8,stride=8),:] for i in range(per)],axis=1)
        eh,el=masked4(e)
        ch,cl=split(cf)
        d=dotnn(jnp.concatenate([ch,cl,ch],axis=1),jnp.concatenate([eh,eh,el],axis=0))
        d=jnp.concatenate([d[:,i*128:(i+1)*128] for i in range(per)],axis=0)
        q=exact(d,p1)+exact(lf[pl.ds(u*per*RHS,per*RHS),:],p2)
        for b in range(per//8):
            g=(u*per)//8+b
            z=q[b*128:(b+1)*128].reshape(8,RHS,256)
            z=jnp.stack([z[:,:,:128],z[:,:,128:]],axis=1).reshape(256,128)
            same=(iota((256,128),0)//32==lax.rem(iota((256,128),1),8))
            zh,zl=split(jnp.where(same,z,0.0))
            bh,bl=split(bas[pl.ds(g*128,128),:])
            o=(dotnn(zh,bh)+dotnn(zl,bh)+dotnn(zh,bl)).reshape(8,2,RHS,128)
            for m in range(4):
                a=jnp.where(left,o[2*m,0],o[2*m,1])
                c=jnp.where(left,o[2*m+1,0],o[2*m+1,1])
                r=jnp.where(left,a,c)+pltpu.roll(jnp.where(left,c,a),LEAF,1)
                at=pl.ds(g*512+m*128,128)
                out[:,at]=near_ref[:,at]+r

def down(csrc,pays,sums,gcp,ccp,upper,transfer,basis,lf,nearv):
    n=basis.shape[0]; nc=upper.shape[0]; ng=gcp.shape[0]
    bas=basis.reshape(n//8,8,16,128).transpose(0,2,1,3).reshape(n*16,128)
    tra=transfer.reshape(n//8,8,8,128).transpose(0,2,1,3).reshape(n*8,128)
    ccv=ccp.reshape(nc,8,8,128).transpose(0,2,1,3).reshape(nc*64,128)
    vm=pl.BlockSpec(memory_space=pltpu.VMEM)
    return pl.pallas_call(down_kernel,
        out_shape=jax.ShapeDtypeStruct((RHS,n*LEAF),f32),
        in_specs=[pl.BlockSpec(memory_space=pltpu.SMEM)]+[vm]*9,
        scratch_shapes=[pltpu.VMEM((8*ng,128),f32),pltpu.VMEM((8*nc,128),f32)],
        compiler_params=pltpu.CompilerParams(vmem_limit_bytes=24<<20),name="down")(csrc,pays,sums,gcp,ccv,upper,tra,bas,lf,nearv)

def across(sizes):
    z,y,c=sizes
    return [[(a*y+b)*c+k for a in range(z) for b in range(y)] for k in range(c)]

def per_device(right_sides,near_blocks,near_source,near_count,basis,leaf_source,leaf_coupling,leaf_transfer,cluster_source,cluster_coupling,cluster_transfer,group_coupling):
    both=("group","leaf")
    leaves=near_blocks.shape[0]
    devs=lax.axis_size("leaf")
    every=lax.axis_size(both)
    base=((lax.axis_index(both)-1)*leaves).reshape(1).astype(jnp.int32)
    up_pairs=[(i,i+1) for i in range(every-1)]
    down_pairs=[(i+1,i) for i in range(every-1)]
    xb=lax.ppermute(right_sides,both,up_pairs)
    xa=lax.ppermute(right_sides,both,down_pairs)
    coef,pay=up(right_sides,basis,leaf_transfer,cluster_transfer)
    cb=lax.ppermute(coef,both,up_pairs)
    ca=lax.ppermute(coef,both,down_pairs)
    groups=across((devs//8,4,2))
    some=lax.all_to_all(jnp.broadcast_to(pay[None],(devs//2,)+pay.shape),"leaf",0,0,tiled=True,axis_index_groups=groups)
    pays=lax.all_gather(some,"leaf",axis=0,tiled=True,axis_index_groups=[[2*i,2*i+1] for i in range(devs//2)])
    total=pays[:,RHS:,:].sum(axis=0)
    sums=lax.all_gather(total,"group",axis=0,tiled=True)
    nearv=near(base,near_source,near_count,xb,right_sides,xa,near_blocks)
    lf=far(base,leaf_source,cb,coef,ca,leaf_coupling)
    return down(cluster_source,pays.reshape(devs*24,128),sums,group_coupling.reshape(-1,1024),cluster_coupling,cluster_transfer,leaf_transfer,basis,lf,nearv)

def solution(mesh):
    both=("group","leaf")
    one=P(both)
    two=P(both,None)
    three=P(both,None,None)
    return jax.shard_map(per_device,mesh=mesh,
        in_specs=(P(None,both),three,two,one,two,two,three,two,two,three,two,P("group",None,None)),
        out_specs=P(None,both),check_vma=False)
```

```python
import functools

import jax
import jax.numpy as jnp
from jax import lax
from jax.experimental import pallas as pl
from jax.experimental.pallas import tpu as pltpu
from jax.sharding import PartitionSpec as P

LEAF=64;K=32;RHS=16
f32=jnp.float32; bf16=jnp.bfloat16
NT=(((1,),(1,)),((),()))
def split(a):
    h=a.astype(bf16)
    return h,(a-h.astype(f32)).astype(bf16)
def dotnt(a,b): return lax.dot_general(a,b,NT,preferred_element_type=f32)
def dotnn(a,b): return lax.dot_general(a,b,(((1,),(0,)),((),())),preferred_element_type=f32)

HBM=pltpu.HBM
def in_hbm(v): return pltpu.with_memory_space_constraint(v,HBM)

def point_table(x_ref, first, leaves, hi, lo):
    left=lax.broadcasted_iota(jnp.int32,(RHS,128),1)<LEAF
    def body(q,_):
        x=x_ref[:,pl.ds(pl.multiple_of(q*128,128),128)]
        y=pltpu.roll(x,LEAF,1)
        for n,(a,b) in enumerate(((x,y),(y,x))):
            h,l=split(jnp.where(left,a,b))
            hi[first+2*q+n]=h
            lo[first+2*q+n]=l
        return 0
    lax.fori_loop(0,leaves//2,body,0,unroll=4)

def near_kernel(var, base, src_h, cnt_h, nb_h, xb, xo, xa, out, hi, lo, weave, nb, src, cnt, sem, sem2):
    n=out.shape[1]//LEAF
    chunks=sem.shape[0]
    size=nb.shape[0]//chunks
    def chunk(c): return pltpu.make_async_copy(nb_h.at[pl.ds(c*size,size),:],nb.at[pl.ds(c*size,size),:],sem.at[c])
    ca=pltpu.make_async_copy(src_h,src,sem2.at[0]); cb=pltpu.make_async_copy(cnt_h,cnt,sem2.at[1])
    ca.start(); cb.start()
    for c in range(chunks): chunk(c).start()
    point_table(xb,0,n,hi,lo)
    point_table(xo,n,n,hi,lo)
    point_table(xa,2*n,n,hi,lo)
    hi[3*n]=jnp.zeros((RHS,128),bf16)
    lo[3*n]=jnp.zeros((RHS,128),bf16)
    row=lax.broadcasted_iota(jnp.int32,(256,256),0)
    col=lax.broadcasted_iota(jnp.int32,(256,256),1)
    a=lax.rem(col,64)
    weave[...]=(row==col-a+lax.rem(a,2)*32+a//2).astype(f32).astype(bf16)
    ca.wait(); cb.wait()
    per=n//chunks
    first=base[0]
    left=lax.broadcasted_iota(jnp.int32,(RHS,128),1)<LEAF
    left32=lax.broadcasted_iota(jnp.int32,(32,128),1)<LEAF
    def join(table,at): return jnp.concatenate([jnp.where(left,table[at[2*p]],table[at[2*p+1]]) for p in range(4)],axis=1)
    def step(c,_):
        chunk(c).wait()
        for quad in range(per//4):
            parts=[]
            for m in range(4):
                t=c*per+quad*4+m
                off=pl.multiple_of(t*256,256)
                even=[];odd=[]
                for p in range(4):
                    a=nb[pl.ds(off+2*p,32,stride=8),:]
                    b=nb[pl.ds(off+2*p+1,32,stride=8),:]
                    if var=="f32":
                        even.append(jnp.where(left32,a,pltpu.roll(b,LEAF,1)))
                        odd.append(jnp.where(left32,pltpu.roll(a,LEAF,1),b))
                    else:
                        even.append((a,b))
                if var=="f32":
                    w=jnp.concatenate([jnp.concatenate(even,axis=1),jnp.concatenate(odd,axis=1)],axis=0)
                    ah,al=split(w)
                else:
                    res=[]
                    es=[(split(a),split(b)) for a,b in even]
                    for k in range(2):
                        e=jnp.concatenate([jnp.concatenate([a[k][:,:64],b[k][:,:64]],axis=1) for a,b in es],axis=1)
                        o=jnp.concatenate([jnp.concatenate([a[k][:,64:],b[k][:,64:]],axis=1) for a,b in es],axis=1)
                        res.append(jnp.concatenate([e,o],axis=0))
                    ah,al=res
                live=cnt[t]
                at=[jnp.where(j<live,src[j,t]-first,3*n) for j in range(8)]
                xh=join(hi,at); xl=join(lo,at)
                if var=="n128":
                    d=dotnt(jnp.concatenate([xh,xl],axis=0),jnp.concatenate([ah,al],axis=0))
                    parts.append(d[:RHS,:64]+d[RHS:,:64]+d[:RHS,64:])
                else:
                    d=dotnt(jnp.concatenate([xh,xl],axis=0),ah)
                    parts.append(d[:RHS]+d[RHS:]+dotnt(xh,al))
            h,l=split(jnp.concatenate(parts,axis=1))
            d=dotnn(jnp.concatenate([h,l],axis=0),weave[...])
            out[:,pl.ds(pl.multiple_of((c*per+quad*4)*LEAF,256),256)]=d[:RHS]+d[RHS:]
        return 0
    lax.fori_loop(0,chunks,step,0)

def near(base,src,cnt,xb,xo,xa,nb,chunks=4,var="f32"):
    leaves=nb.shape[0]
    view=nb.reshape(leaves,8,32,128).transpose(0,2,1,3).reshape(leaves*256,128)
    pts=leaves*LEAF
    blk=pl.BlockSpec((RHS,pts),lambda g:(0,0))
    hbm=pl.BlockSpec(memory_space=HBM)
    return pl.pallas_call(functools.partial(near_kernel,var),
        out_shape=jax.ShapeDtypeStruct((RHS,pts),f32),grid=(1,),
        in_specs=[pl.BlockSpec(memory_space=pltpu.SMEM),hbm,hbm,hbm,blk,blk,blk],
        out_specs=blk,
        scratch_shapes=[pltpu.VMEM((3*leaves+1,RHS,128),bf16)]*2+[pltpu.VMEM((256,256),bf16),pltpu.VMEM((leaves*256,128),f32),
            pltpu.SMEM((8,leaves),jnp.int32),pltpu.SMEM((leaves,),jnp.int32),pltpu.SemaphoreType.DMA((chunks,)),pltpu.SemaphoreType.DMA((2,))],
        compiler_params=pltpu.CompilerParams(vmem_limit_bytes=24<<20),
        name="near")(base,in_hbm(src.T),in_hbm(cnt),in_hbm(view),xb,xo,xa)

def iota(shape,d): return lax.broadcasted_iota(jnp.int32,shape,d)
def onehot(cond): return cond.astype(f32).astype(bf16)
def exact(v,m):
    h,l=split(v)
    return dotnn(h,m)+dotnn(l,m)
def spread4(tile,m):
    block=jnp.where(iota(tile.shape,1)//K==m,tile,0.0)
    block=block+pltpu.roll(block,64,1)
    return block+pltpu.roll(block,32,1)
def masked4(rows):
    lane=lax.rem(iota(rows.shape,1),128)//K
    both=jnp.concatenate([jnp.where(lane==m,rows,0.0) for m in range(4)],axis=0)
    return split(both)
def mul3(v,w):
    h,l=split(v)
    d=dotnt(jnp.concatenate([h,l],axis=0),w[0])
    return d[:RHS]+d[RHS:]+dotnt(h,w[1])

def up_kernel(x_h,bas_h,tra_h,upt_h,ext,rep,fs,x,bas,tra,upt,sem):
    moves=[pltpu.make_async_copy(s,d,sem.at[i]) for i,(s,d) in enumerate(((x_h,x),(bas_h,bas),(tra_h,tra),(upt_h,upt)))]
    for m in moves: m.start()
    pts=x.shape[1]
    lane=iota((RHS,128),1)
    left=lane<LEAF
    n=x.shape[1]//LEAF
    row=iota((256,256),0); col=iota((256,256),1)
    k2=lax.rem(row,128)//8
    s2=onehot(col==lax.rem(row,8)*32+2*k2+row//128)
    same=(iota((256,128),0)//32==lax.rem(iota((256,128),1),8))
    v4=[]
    moves[0].wait()
    moves[1].wait()
    ext[:,:pts]=x[...]
    for g in range(n//8):
        blks=[]
        for q in range(4):
            t=x[:,pl.ds((g*4+q)*128,128)]
            y=pltpu.roll(t,LEAF,1)
            for a,b in ((t,y),(y,t)):
                blks+= [jnp.where(left,a,0.0),jnp.where(left,0.0,b)]
        xh,xl=split(jnp.concatenate(blks,axis=0))
        bh,bl=split(bas[pl.ds(g*128,128),:])
        d=dotnt(xh,bh)+dotnt(xl,bh)+dotnt(xh,bl)
        d=jnp.where(same,d,0.0).reshape(8,32,128).sum(axis=0)
        c=exact(jnp.concatenate([d[:RHS],d[RHS:]],axis=1),s2)
        ext[:,pl.ds(pts+g*256,256)]=c
        for i in range(8):
            v4.append(spread4(c[:,(i//4)*128:(i//4)*128+128],i%4))
    nc=upt.shape[0]
    per=n//nc
    moves[2].wait()
    moves[3].wait()
    outs=[]
    for u in range(nc):
        e=jnp.concatenate([tra[pl.ds(((u*per+i)//8)*64+(u*per+i)%8,8,stride=8),:] for i in range(per)],axis=1)
        outs.append(mul3(jnp.concatenate(v4[u*per:(u+1)*per],axis=1),masked4(e)))
    row=iota((128,128),0); col=iota((128,128),1)
    s3=onehot(col==row//32*32+lax.rem(row,8)*4+lax.rem(row,32)//8)
    cc=exact(jnp.concatenate(outs,axis=1),s3)
    for q in range(8):
        fs[pl.ds(q*nc,nc),:]=upt[:,pl.ds(q*128,128)]
    f=jnp.concatenate([fs[pl.ds(u,8,stride=nc),:] for u in range(nc)],axis=1)
    pr=mul3(jnp.concatenate([spread4(cc,u) for u in range(nc)],axis=1),masked4(f))
    pay=jnp.concatenate([cc,jnp.concatenate([pr[0:8],pr[8:16],jnp.zeros((8,64),f32)],axis=1)],axis=0)
    for c in range(rep.shape[0]//24): rep[pl.ds(c*24,24),:]=pay

def up(x,basis,transfer,upper,copies):
    n=basis.shape[0]
    bas=basis.reshape(n//8,8,16,128).transpose(0,2,1,3).reshape(n*16,128)
    tra=transfer.reshape(n//8,8,8,128).transpose(0,2,1,3).reshape(n*8,128)
    args=(x,bas,tra,upper)
    return pl.pallas_call(up_kernel,
        out_shape=(jax.ShapeDtypeStruct((RHS,n*(LEAF+K)),f32),jax.ShapeDtypeStruct((copies*24,128),f32)),
        in_specs=[pl.BlockSpec(memory_space=HBM)]*4,
        scratch_shapes=[pltpu.VMEM((8*upper.shape[0],128),f32)]+[pltpu.VMEM(v.shape,f32) for v in args]+[pltpu.SemaphoreType.DMA((4,))],
        compiler_params=pltpu.CompilerParams(vmem_limit_bytes=24<<20),name="up")(*[in_hbm(v) for v in args])

def far_kernel(base,src_h,cpl_h,cb,co,ca,out,hi,lo,cpl,src,sem,sem2):
    tiles=co.shape[1]//128
    n=src.shape[1]
    chunks=sem.shape[0]
    size=cpl.shape[0]//chunks
    def chunk(c): return pltpu.make_async_copy(cpl_h.at[pl.ds(c*size,size),:],cpl.at[pl.ds(c*size,size),:],sem.at[c])
    idx=pltpu.make_async_copy(src_h,src,sem2.at[0])
    idx.start()
    for c in range(chunks): chunk(c).start()
    for w,ref in enumerate((cb,co,ca)):
        def body(q,_):
            t=ref[:,pl.ds(pl.multiple_of(q*128,128),128)]
            for m in range(4):
                h,l=split(spread4(t,m))
                hi[(w*tiles+q)*4+m]=h
                lo[(w*tiles+q)*4+m]=l
            return 0
        lax.fori_loop(0,tiles,body,0,unroll=4)
    idx.wait()
    per=n//chunks
    first=base[0]
    def step(c,_):
        chunk(c).wait()
        for i in range(per):
            t=c*per+i
            off=pl.multiple_of(t*64,64)
            w=jnp.concatenate([cpl[pl.ds(off+j,8,stride=8),:] for j in range(8)],axis=1)
            wh,wl=masked4(w)
            at=[src[j,t]-first for j in range(8)]
            vh=jnp.concatenate([hi[s] for s in at],axis=1)
            vl=jnp.concatenate([lo[s] for s in at],axis=1)
            d=dotnt(jnp.concatenate([vh,vl],axis=0),wh)
            out[pl.ds(pl.multiple_of(t*RHS,RHS),RHS),:]=d[:RHS]+d[RHS:]+dotnt(vh,wl)
        return 0
    lax.fori_loop(0,chunks,step,0)

def far(base,src,eb,eo,ea,coupling,chunks=4):
    n=coupling.shape[0]
    view=coupling.reshape(n,8,8,128).transpose(0,2,1,3).reshape(n*64,128)
    blk=pl.BlockSpec((RHS,n*K),lambda g:(0,LEAF//K))
    hbm=pl.BlockSpec(memory_space=HBM)
    return pl.pallas_call(far_kernel,
        out_shape=jax.ShapeDtypeStruct((n*RHS,K),f32),grid=(1,),
        in_specs=[pl.BlockSpec(memory_space=pltpu.SMEM),hbm,hbm,blk,blk,blk],
        out_specs=pl.BlockSpec((n*RHS,K),lambda g:(0,0)),
        scratch_shapes=[pltpu.VMEM((3*n,RHS,128),bf16)]*2+[pltpu.VMEM((n*64,128),f32),pltpu.SMEM((8,n),jnp.int32),
            pltpu.SemaphoreType.DMA((chunks,)),pltpu.SemaphoreType.DMA((1,))],
        compiler_params=pltpu.CompilerParams(vmem_limit_bytes=24<<20),name="far")(base,in_hbm(src.T),in_hbm(view),eb,eo,ea)

def down_kernel(base,csrc,pays,s0,s1,s2,s3,gcp,ccp,upt,tra,bas,lf,near_ref,out,gs,fs):
    nc=upt.shape[0]; ng=gcp.shape[0]
    n=lf.shape[0]//RHS
    devs=pays.shape[0]//24
    row=iota((K,128),0); col=lax.rem(iota((K,128),1),K)
    s4=onehot(col==lax.rem(row,8)*4+row//8)
    for q in range(8):
        fs[pl.ds(q*nc,nc),:]=upt[:,pl.ds(q*128,128)]
        gs[pl.ds(q*ng,ng),:]=gcp[:,pl.ds(q*128,128)]
    gv=[]
    for h in range(ng):
        t=(s0,s1,s2,s3)[h][...]
        gv.append(exact(jnp.concatenate([t[:,0:K],t[:,K:2*K]],axis=0),s4))
    gw=jnp.concatenate([gs[pl.ds(lax.rem(base[1]+ng-h,ng),8,stride=ng),:] for h in range(ng)],axis=1)
    gf=mul3(jnp.concatenate(gv,axis=1),masked4(gw))
    fw=jnp.concatenate([fs[pl.ds(u,8,stride=nc),:] for u in range(nc)],axis=1)
    wh,wl=masked4(fw)
    gh,gl=split(gf)
    down=dotnn(gh,wh)+dotnn(gl,wh)+dotnn(gh,wl)
    row=lax.rem(iota((128,K),0),K); col=iota((128,K),1)
    s5=onehot(row==lax.rem(col,8)*4+col//8)
    down=jnp.concatenate([down[:,u*128:(u+1)*128] for u in range(nc)],axis=0)
    down=exact(down,s5)
    row=lax.rem(iota((128,256),0),K); col=iota((128,256),1)
    p1=onehot(row==2*(lax.rem(col,128)//8)+col//128)
    row=iota((K,256),0); col=iota((K,256),1)
    nat=2*(lax.rem(col,128)//8)+col//128
    p2=onehot(row==lax.rem(nat,4)*8+nat//4)
    left=iota((RHS,128),1)<LEAF
    per=n//nc
    for u in range(nc):
        w=jnp.concatenate([ccp[pl.ds(u*64+j,8,stride=8),:] for j in range(8)],axis=1)
        vs=[]
        for j in range(8):
            s=csrc[u,j]
            place=lax.rem(s//nc,2)*(devs//2)+s//(2*nc)
            vs.append(spread4(pays[pl.ds(pl.multiple_of(place*24,8),RHS),:],lax.rem(s,nc)))
        cf=mul3(jnp.concatenate(vs,axis=1),masked4(w))+down[u*RHS:(u+1)*RHS]
        e=jnp.concatenate([tra[pl.ds(((u*per+i)//8)*64+(u*per+i)%8,8,stride=8),:] for i in range(per)],axis=1)
        eh,el=masked4(e)
        ch,cl=split(cf)
        d=dotnn(jnp.concatenate([ch,cl,ch],axis=1),jnp.concatenate([eh,eh,el],axis=0))
        d=jnp.concatenate([d[:,i*128:(i+1)*128] for i in range(per)],axis=0)
        q=exact(d,p1)+exact(lf[pl.ds(u*per*RHS,per*RHS),:],p2)
        for b in range(per//8):
            g=(u*per)//8+b
            z=q[b*128:(b+1)*128].reshape(8,RHS,256)
            z=jnp.stack([z[:,:,:128],z[:,:,128:]],axis=1).reshape(256,128)
            same=(iota((256,128),0)//32==lax.rem(iota((256,128),1),8))
            zh,zl=split(jnp.where(same,z,0.0))
            bh,bl=split(bas[pl.ds(g*128,128),:])
            o=(dotnn(zh,bh)+dotnn(zl,bh)+dotnn(zh,bl)).reshape(8,2,RHS,128)
            for m in range(4):
                a=jnp.where(left,o[2*m,0],o[2*m,1])
                c=jnp.where(left,o[2*m+1,0],o[2*m+1,1])
                r=jnp.where(left,a,c)+pltpu.roll(jnp.where(left,c,a),LEAF,1)
                at=pl.ds(g*512+m*128,128)
                out[:,at]=near_ref[:,at]+r

def down(base,csrc,pays,sums,gcp,ccp,upper,transfer,basis,lf,nearv):
    n=basis.shape[0]; nc=upper.shape[0]; ng=gcp.shape[0]
    bas=basis.reshape(n//8,8,16,128).transpose(0,2,1,3).reshape(n*16,128)
    tra=transfer.reshape(n//8,8,8,128).transpose(0,2,1,3).reshape(n*8,128)
    ccv=ccp.reshape(nc,8,8,128).transpose(0,2,1,3).reshape(nc*64,128)
    vm=pl.BlockSpec(memory_space=pltpu.VMEM)
    return pl.pallas_call(down_kernel,
        out_shape=jax.ShapeDtypeStruct((RHS,n*LEAF),f32),
        in_specs=[pl.BlockSpec(memory_space=pltpu.SMEM)]*2+[vm]*12,
        scratch_shapes=[pltpu.VMEM((8*ng,128),f32),pltpu.VMEM((8*nc,128),f32)],
        compiler_params=pltpu.CompilerParams(vmem_limit_bytes=24<<20),name="down")(base,csrc,pays,*sums,gcp,ccv,upper,tra,bas,lf,nearv)

def across(devs):
    return [[2*i+c for i in range(devs//2)] for c in range(2)]

def per_device(right_sides,near_blocks,near_source,near_count,basis,leaf_source,leaf_coupling,leaf_transfer,cluster_source,cluster_coupling,cluster_transfer,group_coupling):
    both=("group","leaf")
    leaves=near_blocks.shape[0]
    devs=lax.axis_size("leaf")
    every=lax.axis_size(both)
    ng=lax.axis_size("group")
    base=jnp.stack([(lax.axis_index(both)-1)*leaves,lax.axis_index("group")]).astype(jnp.int32)
    ext,rep=up(right_sides,basis,leaf_transfer,cluster_transfer,devs//2)
    some=lax.all_to_all(rep.reshape(devs//2,24,128),"leaf",0,0,tiled=True,axis_index_groups=across(devs))
    eb=lax.ppermute(ext,both,[(i,i+1) for i in range(every-1)])
    ea=lax.ppermute(ext,both,[(i+1,i) for i in range(every-1)])
    nearv=near(base,near_source,near_count,eb,ext,ea,near_blocks)
    some,nearv=lax.optimization_barrier((some,nearv))
    pays=lax.all_gather(some,"leaf",axis=0,tiled=True,axis_index_groups=[[2*i,2*i+1] for i in range(devs//2)])
    total=pays[:,RHS:,:].sum(axis=0)
    sums=[total]+[lax.ppermute(total,"group",[(i,(i+k)%ng) for i in range(ng)]) for k in range(1,ng)]
    base2,_=lax.optimization_barrier((base,total))
    lf=far(base2,leaf_source,eb,ext,ea,leaf_coupling)
    return down(base,cluster_source,pays.reshape(devs*24,128),sums,group_coupling.reshape(-1,1024),cluster_coupling,cluster_transfer,leaf_transfer,basis,lf,nearv)

def solution(mesh):
    both=("group","leaf")
    one=P(both)
    two=P(both,None)
    three=P(both,None,None)
    return jax.shard_map(per_device,mesh=mesh,
        in_specs=(P(None,both),three,two,one,two,two,three,two,two,three,two,P("group",None,None)),
        out_specs=P(None,both),check_vma=False)
```

```python
import functools

import jax
import jax.numpy as jnp
from jax import lax
from jax.experimental import pallas as pl
from jax.experimental.pallas import tpu as pltpu
from jax.sharding import PartitionSpec as P

LEAF=64;K=32;RHS=16
f32=jnp.float32; bf16=jnp.bfloat16
NT=(((1,),(1,)),((),()))
def split(a):
    h=a.astype(bf16)
    return h,(a-h.astype(f32)).astype(bf16)
def dotnt(a,b): return lax.dot_general(a,b,NT,preferred_element_type=f32)
def dotnn(a,b): return lax.dot_general(a,b,(((1,),(0,)),((),())),preferred_element_type=f32)

HBM=pltpu.HBM
def in_hbm(v): return pltpu.with_memory_space_constraint(v,HBM)

def point_table(x_ref, first, leaves, hi, lo):
    left=lax.broadcasted_iota(jnp.int32,(RHS,128),1)<LEAF
    def body(q,_):
        x=x_ref[:,pl.ds(pl.multiple_of(q*128,128),128)]
        y=pltpu.roll(x,LEAF,1)
        for n,(a,b) in enumerate(((x,y),(y,x))):
            h,l=split(jnp.where(left,a,b))
            hi[first+2*q+n]=h
            lo[first+2*q+n]=l
        return 0
    lax.fori_loop(0,leaves//2,body,0,unroll=4)

def near_kernel(var, base, src_h, cnt_h, nb_h, xb, xo, xa, out, hi, lo, weave, nb, src, cnt, sem, sem2):
    n=out.shape[1]//LEAF
    chunks=sem.shape[0]
    size=nb.shape[0]//chunks
    def chunk(c): return pltpu.make_async_copy(nb_h.at[pl.ds(c*size,size),:],nb.at[pl.ds(c*size,size),:],sem.at[c])
    ca=pltpu.make_async_copy(src_h,src,sem2.at[0]); cb=pltpu.make_async_copy(cnt_h,cnt,sem2.at[1])
    ca.start(); cb.start()
    for c in range(chunks): chunk(c).start()
    point_table(xo,n,n,hi,lo)
    point_table(xb,base[2]*n,n,hi,lo)
    point_table(xa,(2-base[2])*n,n,hi,lo)
    hi[3*n]=jnp.zeros((RHS,128),bf16)
    lo[3*n]=jnp.zeros((RHS,128),bf16)
    row=lax.broadcasted_iota(jnp.int32,(256,256),0)
    col=lax.broadcasted_iota(jnp.int32,(256,256),1)
    a=lax.rem(col,64)
    weave[...]=(row==col-a+lax.rem(a,2)*32+a//2).astype(f32).astype(bf16)
    ca.wait(); cb.wait()
    per=n//chunks
    first=base[0]
    left=lax.broadcasted_iota(jnp.int32,(RHS,128),1)<LEAF
    left32=lax.broadcasted_iota(jnp.int32,(32,128),1)<LEAF
    def join(table,at): return jnp.concatenate([jnp.where(left,table[at[2*p]],table[at[2*p+1]]) for p in range(4)],axis=1)
    def step(c,_):
        chunk(c).wait()
        for quad in range(per//4):
            parts=[]
            for m in range(4):
                t=c*per+quad*4+m
                off=pl.multiple_of(t*256,256)
                even=[];odd=[]
                for p in range(4):
                    a=nb[pl.ds(off+2*p,32,stride=8),:]
                    b=nb[pl.ds(off+2*p+1,32,stride=8),:]
                    if var=="f32":
                        even.append(jnp.where(left32,a,pltpu.roll(b,LEAF,1)))
                        odd.append(jnp.where(left32,pltpu.roll(a,LEAF,1),b))
                    else:
                        even.append((a,b))
                if var=="f32":
                    w=jnp.concatenate([jnp.concatenate(even,axis=1),jnp.concatenate(odd,axis=1)],axis=0)
                    ah,al=split(w)
                else:
                    res=[]
                    es=[(split(a),split(b)) for a,b in even]
                    for k in range(2):
                        e=jnp.concatenate([jnp.concatenate([a[k][:,:64],b[k][:,:64]],axis=1) for a,b in es],axis=1)
                        o=jnp.concatenate([jnp.concatenate([a[k][:,64:],b[k][:,64:]],axis=1) for a,b in es],axis=1)
                        res.append(jnp.concatenate([e,o],axis=0))
                    ah,al=res
                live=cnt[t]
                at=[jnp.where(j<live,src[j,t]-first,3*n) for j in range(8)]
                xh=join(hi,at); xl=join(lo,at)
                if var=="n128":
                    d=dotnt(jnp.concatenate([xh,xl],axis=0),jnp.concatenate([ah,al],axis=0))
                    parts.append(d[:RHS,:64]+d[RHS:,:64]+d[:RHS,64:])
                else:
                    d=dotnt(jnp.concatenate([xh,xl],axis=0),ah)
                    parts.append(d[:RHS]+d[RHS:]+dotnt(xh,al))
            h,l=split(jnp.concatenate(parts,axis=1))
            d=dotnn(jnp.concatenate([h,l],axis=0),weave[...])
            out[:,pl.ds(pl.multiple_of((c*per+quad*4)*LEAF,256),256)]=d[:RHS]+d[RHS:]
        return 0
    lax.fori_loop(0,chunks,step,0)

def near(base,src,cnt,xb,xo,xa,nb,chunks=4,var="f32"):
    leaves=nb.shape[0]
    view=nb.reshape(leaves,8,32,128).transpose(0,2,1,3).reshape(leaves*256,128)
    pts=leaves*LEAF
    blk=pl.BlockSpec((RHS,pts),lambda g:(0,0))
    hbm=pl.BlockSpec(memory_space=HBM)
    return pl.pallas_call(functools.partial(near_kernel,var),
        out_shape=jax.ShapeDtypeStruct((RHS,pts),f32),grid=(1,),
        in_specs=[pl.BlockSpec(memory_space=pltpu.SMEM),hbm,hbm,hbm,blk,blk,blk],
        out_specs=blk,
        scratch_shapes=[pltpu.VMEM((3*leaves+1,RHS,128),bf16)]*2+[pltpu.VMEM((256,256),bf16),pltpu.VMEM((leaves*256,128),f32),
            pltpu.SMEM((8,leaves),jnp.int32),pltpu.SMEM((leaves,),jnp.int32),pltpu.SemaphoreType.DMA((chunks,)),pltpu.SemaphoreType.DMA((2,))],
        cost_estimate=pl.CostEstimate(flops=10**11,bytes_accessed=10**7,transcendentals=0),
        compiler_params=pltpu.CompilerParams(vmem_limit_bytes=24<<20),
        name="near")(base,in_hbm(src.T),in_hbm(cnt),in_hbm(view),xb,xo,xa)

def iota(shape,d): return lax.broadcasted_iota(jnp.int32,shape,d)
def onehot(cond): return cond.astype(f32).astype(bf16)
def exact(v,m):
    h,l=split(v)
    return dotnn(h,m)+dotnn(l,m)
def spread4(tile,m):
    block=jnp.where(iota(tile.shape,1)//K==m,tile,0.0)
    block=block+pltpu.roll(block,64,1)
    return block+pltpu.roll(block,32,1)
def masked4(rows):
    n=rows.shape[1]//128
    lane=iota((16,128),1)//K
    half=iota((16,128),0)//8
    keep=[onehot(lane==half+2*p) for p in range(2)]
    h=rows.astype(bf16).astype(f32)
    out=[]
    for v in (h,rows-h):
        w=jnp.concatenate([v,v],axis=0).astype(bf16)
        out.append(jnp.concatenate([w*jnp.concatenate([m]*n,axis=1) for m in keep],axis=0))
    return out

def mul3(v,w):
    h,l=split(v)
    d=dotnt(jnp.concatenate([h,l],axis=0),w[0])
    return d[:RHS]+d[RHS:]+dotnt(h,w[1])

def up_kernel(x_h,bas_h,tra_h,upt_h,ext,tra,upt,x,bas,sem,sem2):
    chunks=sem.shape[0]-1
    size=bas.shape[0]//chunks
    first=pltpu.make_async_copy(x_h,x,sem.at[chunks])
    moves=[pltpu.make_async_copy(bas_h.at[pl.ds(c*size,size),:],bas.at[pl.ds(c*size,size),:],sem.at[c]) for c in range(chunks)]
    later=[pltpu.make_async_copy(tra_h,tra,sem2.at[0]),pltpu.make_async_copy(upt_h,upt,sem2.at[1])]
    first.start()
    for m in moves+later: m.start()
    pts=x.shape[1]
    n=pts//LEAF
    left=iota((RHS,128),1)<LEAF
    row=iota((256,256),0); col=iota((256,256),1)
    k2=lax.rem(row,128)//8
    s2=onehot(col==lax.rem(row,8)*32+2*k2+row//128)
    same=(iota((256,128),0)//32==lax.rem(iota((256,128),1),8))
    first.wait()
    ext[:,:pts]=x[...]
    for g in range(n//8):
        if g*128%size==0: moves[g*128//size].wait()
        blks=[]
        for q in range(4):
            t=x[:,pl.ds((g*4+q)*128,128)]
            y=pltpu.roll(t,LEAF,1)
            for a,b in ((t,y),(y,t)):
                blks+= [jnp.where(left,a,0.0),jnp.where(left,0.0,b)]
        xh,xl=split(jnp.concatenate(blks,axis=0))
        bh,bl=split(bas[pl.ds(g*128,128),:])
        d=dotnt(xh,bh)+dotnt(xl,bh)+dotnt(xh,bl)
        d=jnp.where(same,d,0.0).reshape(8,32,128).sum(axis=0)
        ext[:,pl.ds(pts+g*256,256)]=exact(jnp.concatenate([d[:RHS],d[RHS:]],axis=1),s2)
    for m in later: m.wait()

def up(x,basis,transfer,upper,chunks=2):
    n=basis.shape[0]
    tra=transfer.reshape(n//8,8,8,128).transpose(0,2,1,3).reshape(n*8,128)
    bas=basis.reshape(n//8,8,16,128).transpose(0,2,1,3).reshape(n*16,128)
    return pl.pallas_call(up_kernel,
        out_shape=(jax.ShapeDtypeStruct((RHS,n*(LEAF+K)),f32),jax.ShapeDtypeStruct(tra.shape,f32),jax.ShapeDtypeStruct(upper.shape,f32)),
        in_specs=[pl.BlockSpec(memory_space=HBM)]*4,
        scratch_shapes=[pltpu.VMEM(x.shape,f32),pltpu.VMEM(bas.shape,f32),pltpu.SemaphoreType.DMA((chunks+1,)),pltpu.SemaphoreType.DMA((2,))],
        compiler_params=pltpu.CompilerParams(vmem_limit_bytes=24<<20),name="up")(in_hbm(x),in_hbm(bas),in_hbm(tra),in_hbm(upper))

def lift_kernel(ext,tra,upt,rep,fs):
    nc=upt.shape[0]
    n=tra.shape[0]//8
    per=n//nc
    pts=n*LEAF
    outs=[]
    for u in range(nc):
        e=jnp.concatenate([tra[pl.ds(((u*per+i)//8)*64+(u*per+i)%8,8,stride=8),:] for i in range(per)],axis=1)
        v=[spread4(ext[:,pl.ds(pts+(u*per+i)//4*128,128)],i%4) for i in range(per)]
        outs.append(mul3(jnp.concatenate(v,axis=1),masked4(e)))
    row=iota((128,128),0); col=iota((128,128),1)
    s3=onehot(col==row//32*32+lax.rem(row,8)*4+lax.rem(row,32)//8)
    cc=exact(jnp.concatenate(outs,axis=1),s3)
    for q in range(8):
        fs[pl.ds(q*nc,nc),:]=upt[:,pl.ds(q*128,128)]
    f=jnp.concatenate([fs[pl.ds(u,8,stride=nc),:] for u in range(nc)],axis=1)
    pr=mul3(jnp.concatenate([spread4(cc,u) for u in range(nc)],axis=1),masked4(f))
    pay=jnp.concatenate([cc,jnp.concatenate([pr[0:8],pr[8:16],jnp.zeros((8,64),f32)],axis=1)],axis=0)
    for c in range(rep.shape[0]//24): rep[pl.ds(c*24,24),:]=pay

def lift(ext,tra,upper,copies):
    return pl.pallas_call(lift_kernel,
        out_shape=jax.ShapeDtypeStruct((copies*24,128),f32),
        in_specs=[pl.BlockSpec(memory_space=pltpu.VMEM)]*3,
        scratch_shapes=[pltpu.VMEM((8*upper.shape[0],128),f32)],
        compiler_params=pltpu.CompilerParams(vmem_limit_bytes=24<<20),name="lift")(ext,tra,upper)

def far_kernel(base,src_h,cpl_h,cb,co,ca,out,hi,lo,cpl,src,sem,sem2):
    tiles=co.shape[1]//128
    n=src.shape[1]
    chunks=sem.shape[0]
    size=cpl.shape[0]//chunks
    def chunk(c): return pltpu.make_async_copy(cpl_h.at[pl.ds(c*size,size),:],cpl.at[pl.ds(c*size,size),:],sem.at[c])
    idx=pltpu.make_async_copy(src_h,src,sem2.at[0])
    idx.start()
    for c in range(chunks): chunk(c).start()
    for w,ref in ((base[2],cb),(1,co),(2-base[2],ca)):
        def body(q,_):
            t=ref[:,pl.ds(pl.multiple_of(q*128,128),128)]
            for m in range(4):
                h,l=split(spread4(t,m))
                hi[(w*tiles+q)*4+m]=h
                lo[(w*tiles+q)*4+m]=l
            return 0
        lax.fori_loop(0,tiles,body,0,unroll=4)
    idx.wait()
    per=n//chunks
    first=base[0]
    def step(c,_):
        chunk(c).wait()
        for i in range(per):
            t=c*per+i
            off=pl.multiple_of(t*64,64)
            w=jnp.concatenate([cpl[pl.ds(off+j,8,stride=8),:] for j in range(8)],axis=1)
            wh,wl=masked4(w)
            at=[src[j,t]-first for j in range(8)]
            vh=jnp.concatenate([hi[s] for s in at],axis=1)
            vl=jnp.concatenate([lo[s] for s in at],axis=1)
            d=dotnt(jnp.concatenate([vh,vl],axis=0),wh)
            out[pl.ds(pl.multiple_of(t*RHS,RHS),RHS),:]=d[:RHS]+d[RHS:]+dotnt(vh,wl)
        return 0
    lax.fori_loop(0,chunks,step,0)

def far(base,src,eb,eo,ea,coupling,chunks=4):
    n=coupling.shape[0]
    view=coupling.reshape(n,8,8,128).transpose(0,2,1,3).reshape(n*64,128)
    blk=pl.BlockSpec((RHS,n*K),lambda g:(0,LEAF//K))
    hbm=pl.BlockSpec(memory_space=HBM)
    return pl.pallas_call(far_kernel,
        out_shape=jax.ShapeDtypeStruct((n*RHS,K),f32),grid=(1,),
        in_specs=[pl.BlockSpec(memory_space=pltpu.SMEM),hbm,hbm,blk,blk,blk],
        out_specs=pl.BlockSpec((n*RHS,K),lambda g:(0,0)),
        scratch_shapes=[pltpu.VMEM((3*n,RHS,128),bf16)]*2+[pltpu.VMEM((n*64,128),f32),pltpu.SMEM((8,n),jnp.int32),
            pltpu.SemaphoreType.DMA((chunks,)),pltpu.SemaphoreType.DMA((1,))],
        compiler_params=pltpu.CompilerParams(vmem_limit_bytes=24<<20),name="far")(base,in_hbm(src.T),in_hbm(view),eb,eo,ea)

def down_kernel(base,csrc,pays,s0,s1,s2,s3,gcp,ccp,upt,tra,bas,lf,near_ref,out,gs,fs):
    nc=upt.shape[0]; ng=gcp.shape[0]
    n=lf.shape[0]//RHS
    devs=pays.shape[0]//24
    row=iota((K,128),0); col=lax.rem(iota((K,128),1),K)
    s4=onehot(col==lax.rem(row,8)*4+row//8)
    for q in range(8):
        fs[pl.ds(q*nc,nc),:]=upt[:,pl.ds(q*128,128)]
        gs[pl.ds(q*ng,ng),:]=gcp[:,pl.ds(q*128,128)]
    gv=[]
    for h in range(ng):
        t=(s0,s1,s2,s3)[h][...]
        gv.append(exact(jnp.concatenate([t[:,0:K],t[:,K:2*K]],axis=0),s4))
    gw=jnp.concatenate([gs[pl.ds(lax.rem(base[1]+ng-h,ng),8,stride=ng),:] for h in range(ng)],axis=1)
    gf=mul3(jnp.concatenate(gv,axis=1),masked4(gw))
    fw=jnp.concatenate([fs[pl.ds(u,8,stride=nc),:] for u in range(nc)],axis=1)
    wh,wl=masked4(fw)
    gh,gl=split(gf)
    down=dotnn(gh,wh)+dotnn(gl,wh)+dotnn(gh,wl)
    row=lax.rem(iota((128,K),0),K); col=iota((128,K),1)
    s5=onehot(row==lax.rem(col,8)*4+col//8)
    down=jnp.concatenate([down[:,u*128:(u+1)*128] for u in range(nc)],axis=0)
    down=exact(down,s5)
    row=lax.rem(iota((128,256),0),K); col=iota((128,256),1)
    p1=onehot(row==2*(lax.rem(col,128)//8)+col//128)
    row=iota((K,256),0); col=iota((K,256),1)
    nat=2*(lax.rem(col,128)//8)+col//128
    p2=onehot(row==lax.rem(nat,4)*8+nat//4)
    left=iota((RHS,128),1)<LEAF
    per=n//nc
    for u in range(nc):
        w=jnp.concatenate([ccp[pl.ds(u*64+j,8,stride=8),:] for j in range(8)],axis=1)
        vs=[]
        for j in range(8):
            s=csrc[u,j]
            place=lax.rem(s//nc,2)*(devs//2)+s//(2*nc)
            vs.append(spread4(pays[pl.ds(pl.multiple_of(place*24,8),RHS),:],lax.rem(s,nc)))
        cf=mul3(jnp.concatenate(vs,axis=1),masked4(w))+down[u*RHS:(u+1)*RHS]
        e=jnp.concatenate([tra[pl.ds(((u*per+i)//8)*64+(u*per+i)%8,8,stride=8),:] for i in range(per)],axis=1)
        eh,el=masked4(e)
        ch,cl=split(cf)
        d=dotnn(jnp.concatenate([ch,cl,ch],axis=1),jnp.concatenate([eh,eh,el],axis=0))
        d=jnp.concatenate([d[:,i*128:(i+1)*128] for i in range(per)],axis=0)
        q=exact(d,p1)+exact(lf[pl.ds(u*per*RHS,per*RHS),:],p2)
        for b in range(per//8):
            g=(u*per)//8+b
            z=q[b*128:(b+1)*128].reshape(8,RHS,256)
            z=jnp.stack([z[:,:,:128],z[:,:,128:]],axis=1).reshape(256,128)
            same=(iota((256,128),0)//32==lax.rem(iota((256,128),1),8))
            zh,zl=split(jnp.where(same,z,0.0))
            bh,bl=split(bas[pl.ds(g*128,128),:])
            o=(dotnn(zh,bh)+dotnn(zl,bh)+dotnn(zh,bl)).reshape(8,2,RHS,128)
            for m in range(4):
                a=jnp.where(left,o[2*m,0],o[2*m,1])
                c=jnp.where(left,o[2*m+1,0],o[2*m+1,1])
                r=jnp.where(left,a,c)+pltpu.roll(jnp.where(left,c,a),LEAF,1)
                at=pl.ds(g*512+m*128,128)
                out[:,at]=near_ref[:,at]+r

def down(base,csrc,pays,sums,gcp,ccp,upper,tra,basis,lf,nearv):
    n=basis.shape[0]; nc=upper.shape[0]; ng=gcp.shape[0]
    bas=basis.reshape(n//8,8,16,128).transpose(0,2,1,3).reshape(n*16,128)
    ccv=ccp.reshape(nc,8,8,128).transpose(0,2,1,3).reshape(nc*64,128)
    vm=pl.BlockSpec(memory_space=pltpu.VMEM)
    return pl.pallas_call(down_kernel,
        out_shape=jax.ShapeDtypeStruct((RHS,n*LEAF),f32),
        in_specs=[pl.BlockSpec(memory_space=pltpu.SMEM)]*2+[vm]*12,
        scratch_shapes=[pltpu.VMEM((8*ng,128),f32),pltpu.VMEM((8*nc,128),f32)],
        compiler_params=pltpu.CompilerParams(vmem_limit_bytes=24<<20),name="down")(base,csrc,pays,*sums,gcp,ccv,upper,tra,bas,lf,nearv)

def across(devs):
    return [[2*i+c for i in range(devs//2)] for c in range(2)]

def per_device(right_sides,near_blocks,near_source,near_count,basis,leaf_source,leaf_coupling,leaf_transfer,cluster_source,cluster_coupling,cluster_transfer,group_coupling):
    both=("group","leaf")
    leaves=near_blocks.shape[0]
    devs=lax.axis_size("leaf")
    every=lax.axis_size(both)
    ng=lax.axis_size("group")
    base=jnp.stack([(lax.axis_index(both)-1)*leaves,lax.axis_index("group"),2*lax.rem(lax.axis_index("leaf")+1,2)]).astype(jnp.int32)
    ext,tra,upper=up(right_sides,basis,leaf_transfer,cluster_transfer)
    eb=lax.ppermute(ext,both,[(i,i^1) for i in range(every)])
    ea=lax.ppermute(ext,both,[p for i in range(1,every-1,2) for p in ((i,i+1),(i+1,i))])
    rep=lift(ext,tra,upper,devs//2)
    some=lax.all_to_all(rep.reshape(devs//2,24,128),"leaf",0,0,tiled=True,axis_index_groups=across(devs))
    nearv=near(base,near_source,near_count,eb,ext,ea,near_blocks)
    some,nearv=lax.optimization_barrier((some,nearv))
    pays=lax.all_gather(some,"leaf",axis=0,tiled=True,axis_index_groups=[[2*i,2*i+1] for i in range(devs//2)])
    total=pays[:,RHS:,:].sum(axis=0)
    sums=[total]+[lax.ppermute(total,"group",[(i,(i+k)%ng) for i in range(ng)]) for k in range(1,ng)]
    base2,_=lax.optimization_barrier((base,total))
    lf=far(base2,leaf_source,eb,ext,ea,leaf_coupling)
    return down(base,cluster_source,pays.reshape(devs*24,128),sums,group_coupling.reshape(-1,1024),cluster_coupling,upper,tra,basis,lf,nearv)

def solution(mesh):
    both=("group","leaf")
    one=P(both)
    two=P(both,None)
    three=P(both,None,None)
    return jax.shard_map(per_device,mesh=mesh,
        in_specs=(P(None,both),three,two,one,two,two,three,two,two,three,two,P("group",None,None)),
        out_specs=P(None,both),check_vma=False)
```

```python
import functools

import jax
import jax.numpy as jnp
from jax import lax
from jax.experimental import pallas as pl
from jax.experimental.pallas import tpu as pltpu
from jax.sharding import PartitionSpec as P

LEAF=64;K=32;RHS=16
f32=jnp.float32; bf16=jnp.bfloat16
NT=(((1,),(1,)),((),()))
def split(a):
    h=a.astype(bf16)
    return h,(a-h.astype(f32)).astype(bf16)
def dotnt(a,b): return lax.dot_general(a,b,NT,preferred_element_type=f32)
def dotnn(a,b): return lax.dot_general(a,b,(((1,),(0,)),((),())),preferred_element_type=f32)

HBM=pltpu.HBM
def in_hbm(v): return pltpu.with_memory_space_constraint(v,HBM)

def point_table(x_ref, first, leaves, hi, lo):
    left=lax.broadcasted_iota(jnp.int32,(RHS,128),1)<LEAF
    def body(q,_):
        x=x_ref[:,pl.ds(pl.multiple_of(q*128,128),128)]
        y=pltpu.roll(x,LEAF,1)
        for n,(a,b) in enumerate(((x,y),(y,x))):
            h,l=split(jnp.where(left,a,b))
            hi[first+2*q+n]=h
            lo[first+2*q+n]=l
        return 0
    lax.fori_loop(0,leaves//2,body,0,unroll=4)

def near_kernel(var, base, src_h, cnt_h, nb_h, xb, xo, xa, out, hi, lo, weave, nb, src, cnt, sem, sem2):
    n=out.shape[1]//LEAF
    chunks=sem.shape[0]
    size=nb.shape[0]//chunks
    def chunk(c): return pltpu.make_async_copy(nb_h.at[pl.ds(c*size,size),:],nb.at[pl.ds(c*size,size),:],sem.at[c])
    ca=pltpu.make_async_copy(src_h,src,sem2.at[0]); cb=pltpu.make_async_copy(cnt_h,cnt,sem2.at[1])
    ca.start(); cb.start()
    for c in range(chunks): chunk(c).start()
    point_table(xo,n,n,hi,lo)
    point_table(xb,base[2]*n,n,hi,lo)
    point_table(xa,(2-base[2])*n,n,hi,lo)
    hi[3*n]=jnp.zeros((RHS,128),bf16)
    lo[3*n]=jnp.zeros((RHS,128),bf16)
    row=lax.broadcasted_iota(jnp.int32,(256,256),0)
    col=lax.broadcasted_iota(jnp.int32,(256,256),1)
    a=lax.rem(col,64)
    weave[...]=(row==col-a+lax.rem(a,2)*32+a//2).astype(f32).astype(bf16)
    ca.wait(); cb.wait()
    per=n//chunks
    first=base[0]
    left=lax.broadcasted_iota(jnp.int32,(RHS,128),1)<LEAF
    left32=lax.broadcasted_iota(jnp.int32,(32,128),1)<LEAF
    def join(table,at): return jnp.concatenate([jnp.where(left,table[at[2*p]],table[at[2*p+1]]) for p in range(4)],axis=1)
    def step(c,_):
        chunk(c).wait()
        for quad in range(per//4):
            parts=[]
            for m in range(4):
                t=c*per+quad*4+m
                off=pl.multiple_of(t*256,256)
                even=[];odd=[]
                for p in range(4):
                    a=nb[pl.ds(off+2*p,32,stride=8),:]
                    b=nb[pl.ds(off+2*p+1,32,stride=8),:]
                    if var=="f32":
                        even.append(jnp.where(left32,a,pltpu.roll(b,LEAF,1)))
                        odd.append(jnp.where(left32,pltpu.roll(a,LEAF,1),b))
                    else:
                        even.append((a,b))
                if var=="f32":
                    w=jnp.concatenate([jnp.concatenate(even,axis=1),jnp.concatenate(odd,axis=1)],axis=0)
                    ah,al=split(w)
                else:
                    res=[]
                    es=[(split(a),split(b)) for a,b in even]
                    for k in range(2):
                        e=jnp.concatenate([jnp.concatenate([a[k][:,:64],b[k][:,:64]],axis=1) for a,b in es],axis=1)
                        o=jnp.concatenate([jnp.concatenate([a[k][:,64:],b[k][:,64:]],axis=1) for a,b in es],axis=1)
                        res.append(jnp.concatenate([e,o],axis=0))
                    ah,al=res
                live=cnt[t]
                at=[jnp.where(j<live,src[j,t]-first,3*n) for j in range(8)]
                xh=join(hi,at); xl=join(lo,at)
                if var=="n128":
                    d=dotnt(jnp.concatenate([xh,xl],axis=0),jnp.concatenate([ah,al],axis=0))
                    parts.append(d[:RHS,:64]+d[RHS:,:64]+d[:RHS,64:])
                else:
                    d=dotnt(jnp.concatenate([xh,xl],axis=0),ah)
                    parts.append(d[:RHS]+d[RHS:]+dotnt(xh,al))
            h,l=split(jnp.concatenate(parts,axis=1))
            d=dotnn(jnp.concatenate([h,l],axis=0),weave[...])
            out[:,pl.ds(pl.multiple_of((c*per+quad*4)*LEAF,256),256)]=d[:RHS]+d[RHS:]
        return 0
    lax.fori_loop(0,chunks,step,0)

def near(base,src,cnt,xb,xo,xa,nb,chunks=4,var="f32"):
    leaves=nb.shape[0]
    view=nb.reshape(leaves,8,32,128).transpose(0,2,1,3).reshape(leaves*256,128)
    pts=leaves*LEAF
    blk=pl.BlockSpec((RHS,pts),lambda g:(0,0))
    hbm=pl.BlockSpec(memory_space=HBM)
    return pl.pallas_call(functools.partial(near_kernel,var),
        out_shape=jax.ShapeDtypeStruct((RHS,pts),f32),grid=(1,),
        in_specs=[pl.BlockSpec(memory_space=pltpu.SMEM),hbm,hbm,hbm,blk,blk,blk],
        out_specs=blk,
        scratch_shapes=[pltpu.VMEM((3*leaves+1,RHS,128),bf16)]*2+[pltpu.VMEM((256,256),bf16),pltpu.VMEM((leaves*256,128),f32),
            pltpu.SMEM((8,leaves),jnp.int32),pltpu.SMEM((leaves,),jnp.int32),pltpu.SemaphoreType.DMA((chunks,)),pltpu.SemaphoreType.DMA((2,))],
        cost_estimate=pl.CostEstimate(flops=10**11,bytes_accessed=10**7,transcendentals=0),
        compiler_params=pltpu.CompilerParams(vmem_limit_bytes=24<<20),
        name="near")(base,in_hbm(src.T),in_hbm(cnt),in_hbm(view),xb,xo,xa)

def iota(shape,d): return lax.broadcasted_iota(jnp.int32,shape,d)
def onehot(cond): return cond.astype(f32).astype(bf16)
def exact(v,m):
    h,l=split(v)
    return dotnn(h,m)+dotnn(l,m)
def spread4(tile,m):
    block=jnp.where(iota(tile.shape,1)//K==m,tile,0.0)
    block=block+pltpu.roll(block,64,1)
    return block+pltpu.roll(block,32,1)
def masked4(rows):
    n=rows.shape[1]//128
    lane=iota((16,128),1)//K
    half=iota((16,128),0)//8
    keep=[onehot(lane==half+2*p) for p in range(2)]
    h=rows.astype(bf16).astype(f32)
    out=[]
    for v in (h,rows-h):
        w=jnp.concatenate([v,v],axis=0).astype(bf16)
        out.append(jnp.concatenate([w*jnp.concatenate([m]*n,axis=1) for m in keep],axis=0))
    return out

def mul3(v,w):
    h,l=split(v)
    d=dotnt(jnp.concatenate([h,l],axis=0),w[0])
    return d[:RHS]+d[RHS:]+dotnt(h,w[1])

def up_kernel(x_h,bas_h,tra_h,upt_h,ext,tra,upt,x,bas,sem,sem2):
    chunks=sem.shape[0]-1
    size=bas.shape[0]//chunks
    first=pltpu.make_async_copy(x_h,x,sem.at[chunks])
    moves=[pltpu.make_async_copy(bas_h.at[pl.ds(c*size,size),:],bas.at[pl.ds(c*size,size),:],sem.at[c]) for c in range(chunks)]
    later=[pltpu.make_async_copy(tra_h,tra,sem2.at[0]),pltpu.make_async_copy(upt_h,upt,sem2.at[1])]
    first.start()
    for m in moves+later: m.start()
    pts=x.shape[1]
    n=pts//LEAF
    left=iota((RHS,128),1)<LEAF
    row=iota((256,256),0); col=iota((256,256),1)
    k2=lax.rem(row,128)//8
    s2=onehot(col==lax.rem(row,8)*32+2*k2+row//128)
    same=(iota((256,128),0)//32==lax.rem(iota((256,128),1),8))
    first.wait()
    ext[:,:pts]=x[...]
    for g in range(n//8):
        if g*128%size==0: moves[g*128//size].wait()
        blks=[]
        for q in range(4):
            t=x[:,pl.ds((g*4+q)*128,128)]
            y=pltpu.roll(t,LEAF,1)
            for a,b in ((t,y),(y,t)):
                blks+= [jnp.where(left,a,0.0),jnp.where(left,0.0,b)]
        xh,xl=split(jnp.concatenate(blks,axis=0))
        bh,bl=split(bas[pl.ds(g*128,128),:])
        d=dotnt(xh,bh)+dotnt(xl,bh)+dotnt(xh,bl)
        d=jnp.where(same,d,0.0).reshape(8,32,128).sum(axis=0)
        ext[:,pl.ds(pts+g*256,256)]=exact(jnp.concatenate([d[:RHS],d[RHS:]],axis=1),s2)
    for m in later: m.wait()

def up(x,basis,transfer,upper,chunks=2):
    n=basis.shape[0]
    tra=transfer.reshape(n//8,8,8,128).transpose(0,2,1,3).reshape(n*8,128)
    bas=basis.reshape(n//8,8,16,128).transpose(0,2,1,3).reshape(n*16,128)
    return pl.pallas_call(up_kernel,
        out_shape=(jax.ShapeDtypeStruct((RHS,n*(LEAF+K)),f32),jax.ShapeDtypeStruct(tra.shape,f32),jax.ShapeDtypeStruct(upper.shape,f32)),
        in_specs=[pl.BlockSpec(memory_space=HBM)]*4,
        scratch_shapes=[pltpu.VMEM(x.shape,f32),pltpu.VMEM(bas.shape,f32),pltpu.SemaphoreType.DMA((chunks+1,)),pltpu.SemaphoreType.DMA((2,))],
        compiler_params=pltpu.CompilerParams(vmem_limit_bytes=24<<20),name="up")(in_hbm(x),in_hbm(bas),in_hbm(tra),in_hbm(upper))

def lift_kernel(ext,tra,upt,rep,fs):
    nc=upt.shape[0]
    n=tra.shape[0]//8
    per=n//nc
    pts=n*LEAF
    outs=[]
    for u in range(nc):
        e=jnp.concatenate([tra[pl.ds(((u*per+i)//8)*64+(u*per+i)%8,8,stride=8),:] for i in range(per)],axis=1)
        v=[spread4(ext[:,pl.ds(pts+(u*per+i)//4*128,128)],i%4) for i in range(per)]
        outs.append(mul3(jnp.concatenate(v,axis=1),masked4(e)))
    row=iota((128,128),0); col=iota((128,128),1)
    s3=onehot(col==row//32*32+lax.rem(row,8)*4+lax.rem(row,32)//8)
    cc=exact(jnp.concatenate(outs,axis=1),s3)
    for q in range(8):
        fs[pl.ds(q*nc,nc),:]=upt[:,pl.ds(q*128,128)]
    f=jnp.concatenate([fs[pl.ds(u,8,stride=nc),:] for u in range(nc)],axis=1)
    pr=mul3(jnp.concatenate([spread4(cc,u) for u in range(nc)],axis=1),masked4(f))
    pay=[cc[4*i:4*i+4] for i in range(4)]+[jnp.concatenate([pr[4*i:4*i+4] for i in range(4)],axis=1)]
    for c in range(rep.shape[0]):
        for i in range(5): rep[c,i]=pay[i]

def lift(ext,tra,upper,copies):
    return pl.pallas_call(lift_kernel,
        out_shape=jax.ShapeDtypeStruct((copies,5,4,128),f32),
        in_specs=[pl.BlockSpec(memory_space=pltpu.VMEM)]*3,
        scratch_shapes=[pltpu.VMEM((8*upper.shape[0],128),f32)],
        compiler_params=pltpu.CompilerParams(vmem_limit_bytes=24<<20),name="lift")(ext,tra,upper)

def far_kernel(base,src_h,cpl_h,cb,co,ca,out,hi,lo,cpl,src,sem,sem2):
    tiles=co.shape[1]//128
    n=src.shape[1]
    chunks=sem.shape[0]
    size=cpl.shape[0]//chunks
    def chunk(c): return pltpu.make_async_copy(cpl_h.at[pl.ds(c*size,size),:],cpl.at[pl.ds(c*size,size),:],sem.at[c])
    idx=pltpu.make_async_copy(src_h,src,sem2.at[0])
    idx.start()
    for c in range(chunks): chunk(c).start()
    for w,ref in ((base[2],cb),(1,co),(2-base[2],ca)):
        def body(q,_):
            t=ref[:,pl.ds(pl.multiple_of(q*128,128),128)]
            for m in range(4):
                h,l=split(spread4(t,m))
                hi[(w*tiles+q)*4+m]=h
                lo[(w*tiles+q)*4+m]=l
            return 0
        lax.fori_loop(0,tiles,body,0,unroll=4)
    idx.wait()
    per=n//chunks
    first=base[0]
    def step(c,_):
        chunk(c).wait()
        for i in range(per):
            t=c*per+i
            off=pl.multiple_of(t*64,64)
            w=jnp.concatenate([cpl[pl.ds(off+j,8,stride=8),:] for j in range(8)],axis=1)
            wh,wl=masked4(w)
            at=[src[j,t]-first for j in range(8)]
            vh=jnp.concatenate([hi[s] for s in at],axis=1)
            vl=jnp.concatenate([lo[s] for s in at],axis=1)
            d=dotnt(jnp.concatenate([vh,vl],axis=0),wh)
            out[pl.ds(pl.multiple_of(t*RHS,RHS),RHS),:]=d[:RHS]+d[RHS:]+dotnt(vh,wl)
        return 0
    lax.fori_loop(0,chunks,step,0)

def far(base,src,eb,eo,ea,coupling,chunks=4):
    n=coupling.shape[0]
    view=coupling.reshape(n,8,8,128).transpose(0,2,1,3).reshape(n*64,128)
    blk=pl.BlockSpec((RHS,n*K),lambda g:(0,LEAF//K))
    hbm=pl.BlockSpec(memory_space=HBM)
    return pl.pallas_call(far_kernel,
        out_shape=jax.ShapeDtypeStruct((n*RHS,K),f32),grid=(1,),
        in_specs=[pl.BlockSpec(memory_space=pltpu.SMEM),hbm,hbm,blk,blk,blk],
        out_specs=pl.BlockSpec((n*RHS,K),lambda g:(0,0)),
        scratch_shapes=[pltpu.VMEM((3*n,RHS,128),bf16)]*2+[pltpu.VMEM((n*64,128),f32),pltpu.SMEM((8,n),jnp.int32),
            pltpu.SemaphoreType.DMA((chunks,)),pltpu.SemaphoreType.DMA((1,))],
        compiler_params=pltpu.CompilerParams(vmem_limit_bytes=24<<20),name="far")(base,in_hbm(src.T),in_hbm(view),eb,eo,ea)

def gather_kernel(csrc,pays,ccp,out):
    nc=ccp.shape[0]//64
    devs=pays.shape[0]
    for u in range(nc):
        w=jnp.concatenate([ccp[pl.ds(u*64+j,8,stride=8),:] for j in range(8)],axis=1)
        vs=[]
        for j in range(8):
            s=csrc[u,j]
            place=lax.rem(s//nc,2)*(devs//2)+s//(2*nc)
            vs.append(spread4(jnp.concatenate([pays[place,i] for i in range(4)],axis=0),lax.rem(s,nc)))
        out[pl.ds(u*RHS,RHS),:]=mul3(jnp.concatenate(vs,axis=1),masked4(w))

def gather(csrc,pays,ccp):
    nc=ccp.shape[0]
    view=ccp.reshape(nc,8,8,128).transpose(0,2,1,3).reshape(nc*64,128)
    vm=pl.BlockSpec(memory_space=pltpu.VMEM)
    return pl.pallas_call(gather_kernel,
        out_shape=jax.ShapeDtypeStruct((nc*RHS,K),f32),
        in_specs=[pl.BlockSpec(memory_space=pltpu.SMEM),vm,vm],
        cost_estimate=pl.CostEstimate(flops=10**10,bytes_accessed=10**7,transcendentals=0),
        compiler_params=pltpu.CompilerParams(vmem_limit_bytes=24<<20),name="gather")(csrc,pays,view)

def down_kernel(base,s0,s1,s2,s3,cfar,gcp,upt,tra,bas,lf,near_ref,out,gs,fs):
    nc=upt.shape[0]; ng=gcp.shape[0]
    n=lf.shape[0]//RHS
    row=iota((K,128),0); col=lax.rem(iota((K,128),1),K)
    s4=onehot(col==lax.rem(row,8)*4+row//8)
    for q in range(8):
        fs[pl.ds(q*nc,nc),:]=upt[:,pl.ds(q*128,128)]
        gs[pl.ds(q*ng,ng),:]=gcp[:,pl.ds(q*128,128)]
    gv=[]
    for h in range(ng):
        t=(s0,s1,s2,s3)[h][...]
        gv.append(exact(jnp.concatenate([t[:,i*K:(i+1)*K] for i in range(4)],axis=0),s4))
    gw=jnp.concatenate([gs[pl.ds(lax.rem(base[1]+ng-h,ng),8,stride=ng),:] for h in range(ng)],axis=1)
    gf=mul3(jnp.concatenate(gv,axis=1),masked4(gw))
    fw=jnp.concatenate([fs[pl.ds(u,8,stride=nc),:] for u in range(nc)],axis=1)
    wh,wl=masked4(fw)
    gh,gl=split(gf)
    down=dotnn(gh,wh)+dotnn(gl,wh)+dotnn(gh,wl)
    row=lax.rem(iota((128,K),0),K); col=iota((128,K),1)
    s5=onehot(row==lax.rem(col,8)*4+col//8)
    down=jnp.concatenate([down[:,u*128:(u+1)*128] for u in range(nc)],axis=0)
    down=exact(down,s5)
    row=lax.rem(iota((128,256),0),K); col=iota((128,256),1)
    p1=onehot(row==2*(lax.rem(col,128)//8)+col//128)
    row=iota((K,256),0); col=iota((K,256),1)
    nat=2*(lax.rem(col,128)//8)+col//128
    p2=onehot(row==lax.rem(nat,4)*8+nat//4)
    left=iota((RHS,128),1)<LEAF
    per=n//nc
    for u in range(nc):
        cf=cfar[pl.ds(u*RHS,RHS),:]+down[u*RHS:(u+1)*RHS]
        e=jnp.concatenate([tra[pl.ds(((u*per+i)//8)*64+(u*per+i)%8,8,stride=8),:] for i in range(per)],axis=1)
        eh,el=masked4(e)
        ch,cl=split(cf)
        d=dotnn(jnp.concatenate([ch,cl,ch],axis=1),jnp.concatenate([eh,eh,el],axis=0))
        d=jnp.concatenate([d[:,i*128:(i+1)*128] for i in range(per)],axis=0)
        q=exact(d,p1)+exact(lf[pl.ds(u*per*RHS,per*RHS),:],p2)
        for b in range(per//8):
            g=(u*per)//8+b
            z=q[b*128:(b+1)*128].reshape(8,RHS,256)
            z=jnp.stack([z[:,:,:128],z[:,:,128:]],axis=1).reshape(256,128)
            same=(iota((256,128),0)//32==lax.rem(iota((256,128),1),8))
            zh,zl=split(jnp.where(same,z,0.0))
            bh,bl=split(bas[pl.ds(g*128,128),:])
            o=(dotnn(zh,bh)+dotnn(zl,bh)+dotnn(zh,bl)).reshape(8,2,RHS,128)
            for m in range(4):
                a=jnp.where(left,o[2*m,0],o[2*m,1])
                c=jnp.where(left,o[2*m+1,0],o[2*m+1,1])
                r=jnp.where(left,a,c)+pltpu.roll(jnp.where(left,c,a),LEAF,1)
                at=pl.ds(g*512+m*128,128)
                out[:,at]=near_ref[:,at]+r

def down(base,sums,cfar,gcp,upper,tra,basis,lf,nearv):
    n=basis.shape[0]; nc=upper.shape[0]; ng=gcp.shape[0]
    bas=basis.reshape(n//8,8,16,128).transpose(0,2,1,3).reshape(n*16,128)
    vm=pl.BlockSpec(memory_space=pltpu.VMEM)
    return pl.pallas_call(down_kernel,
        out_shape=jax.ShapeDtypeStruct((RHS,n*LEAF),f32),
        in_specs=[pl.BlockSpec(memory_space=pltpu.SMEM)]+[vm]*11,
        scratch_shapes=[pltpu.VMEM((8*ng,128),f32),pltpu.VMEM((8*nc,128),f32)],
        compiler_params=pltpu.CompilerParams(vmem_limit_bytes=24<<20),name="down")(base,*sums,cfar,gcp,upper,tra,bas,lf,nearv)

def across(devs):
    return [[2*i+c for i in range(devs//2)] for c in range(2)]

def per_device(right_sides,near_blocks,near_source,near_count,basis,leaf_source,leaf_coupling,leaf_transfer,cluster_source,cluster_coupling,cluster_transfer,group_coupling):
    both=("group","leaf")
    leaves=near_blocks.shape[0]
    devs=lax.axis_size("leaf")
    every=lax.axis_size(both)
    ng=lax.axis_size("group")
    base=jnp.stack([(lax.axis_index(both)-1)*leaves,lax.axis_index("group"),2*lax.rem(lax.axis_index("leaf")+1,2)]).astype(jnp.int32)
    ext,tra,upper=up(right_sides,basis,leaf_transfer,cluster_transfer)
    eb=lax.ppermute(ext,both,[(i,i^1) for i in range(every)])
    ea=lax.ppermute(ext,both,[p for i in range(1,every-1,2) for p in ((i,i+1),(i+1,i))])
    rep=lift(ext,tra,upper,devs//2)
    some=lax.all_to_all(rep,"leaf",0,0,tiled=True,axis_index_groups=across(devs))
    nearv=near(base,near_source,near_count,eb,ext,ea,near_blocks)
    lf=far(base,leaf_source,eb,ext,ea,leaf_coupling)
    some,nearv,lf=lax.optimization_barrier((some,nearv,lf))
    pays=lax.all_gather(some,"leaf",axis=0,tiled=True,axis_index_groups=[[2*i,2*i+1] for i in range(devs//2)])
    total=pays[:,4].sum(axis=0)
    sums=[total]+[lax.ppermute(total,"group",[(i,(i+k)%ng) for i in range(ng)]) for k in range(1,ng)]
    cfar=gather(cluster_source,pays,cluster_coupling)
    return down(base,sums,cfar,group_coupling.reshape(-1,1024),upper,tra,basis,lf,nearv)

def solution(mesh):
    both=("group","leaf")
    one=P(both)
    two=P(both,None)
    three=P(both,None,None)
    return jax.shard_map(per_device,mesh=mesh,
        in_specs=(P(None,both),three,two,one,two,two,three,two,two,three,two,P("group",None,None)),
        out_specs=P(None,both),check_vma=False)
```

```python
import functools

import jax
import jax.numpy as jnp
from jax import lax
from jax.experimental import pallas as pl
from jax.experimental.pallas import tpu as pltpu
from jax.sharding import PartitionSpec as P

LEAF=64;K=32;RHS=16
f32=jnp.float32; bf16=jnp.bfloat16
NT=(((1,),(1,)),((),()))
def split(a):
    h=a.astype(bf16)
    return h,(a-h.astype(f32)).astype(bf16)
def dotnt(a,b): return lax.dot_general(a,b,NT,preferred_element_type=f32)
def dotnn(a,b): return lax.dot_general(a,b,(((1,),(0,)),((),())),preferred_element_type=f32)

HBM=pltpu.HBM
def in_hbm(v): return pltpu.with_memory_space_constraint(v,HBM)

def point_table(x_ref, first, leaves, hi, lo):
    left=lax.broadcasted_iota(jnp.int32,(RHS,128),1)<LEAF
    def body(q,_):
        x=x_ref[:,pl.ds(pl.multiple_of(q*128,128),128)]
        y=pltpu.roll(x,LEAF,1)
        for n,(a,b) in enumerate(((x,y),(y,x))):
            h,l=split(jnp.where(left,a,b))
            hi[first+2*q+n]=h
            lo[first+2*q+n]=l
        return 0
    lax.fori_loop(0,leaves//2,body,0,unroll=4)

def near_kernel(base, src_h, cnt_h, nb_h, xb, xo, xa, out, hi, lo, weave, nb, src, cnt, sem, sem2):
    n=out.shape[1]//LEAF
    chunks=sem.shape[0]
    size=nb.shape[0]//chunks
    def chunk(c): return pltpu.make_async_copy(nb_h.at[pl.ds(c*size,size),:],nb.at[pl.ds(c*size,size),:],sem.at[c])
    ca=pltpu.make_async_copy(src_h,src,sem2.at[0]); cb=pltpu.make_async_copy(cnt_h,cnt,sem2.at[1])
    ca.start(); cb.start()
    for c in range(chunks): chunk(c).start()
    point_table(xo,n,n,hi,lo)
    point_table(xb,base[2]*n,n,hi,lo)
    point_table(xa,(2-base[2])*n,n,hi,lo)
    hi[3*n]=jnp.zeros((RHS,128),bf16)
    lo[3*n]=jnp.zeros((RHS,128),bf16)
    row=lax.broadcasted_iota(jnp.int32,(256,128),0)
    col=lax.broadcasted_iota(jnp.int32,(256,128),1)
    a=lax.rem(col,64)
    weave[...]=((row//128==col//64)&(lax.rem(row,64)==lax.rem(a,2)*32+a//2)).astype(f32).astype(bf16)
    ca.wait(); cb.wait()
    per=n//chunks
    first=base[0]
    left=lax.broadcasted_iota(jnp.int32,(RHS,128),1)<LEAF
    left32=lax.broadcasted_iota(jnp.int32,(32,128),1)<LEAF
    def join(table,at): return jnp.concatenate([jnp.where(left,table[at[2*p]],table[at[2*p+1]]) for p in range(4)],axis=1)
    def step(c,_):
        chunk(c).wait()
        for pair in range(per//2):
            parts=[]
            for m in range(2):
                t=c*per+pair*2+m
                off=pl.multiple_of(t*256,256)
                even=[];odd=[]
                for p in range(4):
                    a=nb[pl.ds(off+2*p,32,stride=8),:]
                    b=nb[pl.ds(off+2*p+1,32,stride=8),:]
                    even.append(jnp.where(left32,a,pltpu.roll(b,LEAF,1)))
                    odd.append(jnp.where(left32,pltpu.roll(a,LEAF,1),b))
                w=jnp.concatenate([jnp.concatenate(even,axis=1),jnp.concatenate(odd,axis=1)],axis=0)
                live=cnt[t]
                at=[jnp.where(j<live,src[j,t]-first,3*n) for j in range(8)]
                parts.append(dotnt(jnp.concatenate([join(hi,at),join(lo,at)],axis=0),jnp.concatenate(split(w),axis=0)))
            d=dotnn(jnp.concatenate(split(jnp.concatenate(parts,axis=1)),axis=0),weave[...])
            d=d[:2*RHS]+d[2*RHS:]
            out[:,pl.ds(pl.multiple_of((c*per+pair*2)*LEAF,128),128)]=d[:RHS]+d[RHS:]
        return 0
    lax.fori_loop(0,chunks,step,0)

def near(base,src,cnt,xb,xo,xa,nb,chunks=2):
    leaves=nb.shape[0]
    view=nb.reshape(leaves,8,32,128).transpose(0,2,1,3).reshape(leaves*256,128)
    pts=leaves*LEAF
    blk=pl.BlockSpec((RHS,pts),lambda g:(0,0))
    hbm=pl.BlockSpec(memory_space=HBM)
    return pl.pallas_call(near_kernel,
        out_shape=jax.ShapeDtypeStruct((RHS,pts),f32),grid=(1,),
        in_specs=[pl.BlockSpec(memory_space=pltpu.SMEM),hbm,hbm,hbm,blk,blk,blk],
        out_specs=blk,
        scratch_shapes=[pltpu.VMEM((3*leaves+1,RHS,128),bf16)]*2+[pltpu.VMEM((256,128),bf16),pltpu.VMEM((leaves*256,128),f32),
            pltpu.SMEM((8,leaves),jnp.int32),pltpu.SMEM((leaves,),jnp.int32),pltpu.SemaphoreType.DMA((chunks,)),pltpu.SemaphoreType.DMA((2,))],
        cost_estimate=pl.CostEstimate(flops=10**11,bytes_accessed=10**7,transcendentals=0),
        compiler_params=pltpu.CompilerParams(vmem_limit_bytes=24<<20),
        name="near")(base,in_hbm(src.T),in_hbm(cnt),in_hbm(view),xb,xo,xa)

def iota(shape,d): return lax.broadcasted_iota(jnp.int32,shape,d)
def onehot(cond): return cond.astype(f32).astype(bf16)
def exact(v,m):
    d=dotnn(jnp.concatenate(split(v),axis=0),m)
    return d[:v.shape[0]]+d[v.shape[0]:]
def wide(v,w):
    d=dotnt(jnp.concatenate(split(v),axis=0),jnp.concatenate(w,axis=0))
    return d[:RHS]+d[RHS:]
def spread4(tile,m):
    block=jnp.where(iota(tile.shape,1)//K==m,tile,0.0)
    block=block+pltpu.roll(block,64,1)
    return block+pltpu.roll(block,32,1)
def masked4(rows):
    n=rows.shape[1]//128
    lane=iota((16,128),1)//K
    half=iota((16,128),0)//8
    keep=[onehot(lane==half+2*p) for p in range(2)]
    h=rows.astype(bf16).astype(f32)
    out=[]
    for v in (h,rows-h):
        w=jnp.concatenate([v,v],axis=0).astype(bf16)
        out.append(jnp.concatenate([w*jnp.concatenate([m]*n,axis=1) for m in keep],axis=0))
    return out

def mul3(v,w):
    d=wide(v,w)
    n=w[0].shape[0]
    return d[:,:n]+d[:,n:]

def up_kernel(x_h,bas_h,tra_h,upt_h,ext,tra,upt,x,bas,sem,sem2):
    chunks=sem.shape[0]-1
    size=bas.shape[0]//chunks
    first=pltpu.make_async_copy(x_h,x,sem.at[chunks])
    moves=[pltpu.make_async_copy(bas_h.at[pl.ds(c*size,size),:],bas.at[pl.ds(c*size,size),:],sem.at[c]) for c in range(chunks)]
    later=[pltpu.make_async_copy(tra_h,tra,sem2.at[0]),pltpu.make_async_copy(upt_h,upt,sem2.at[1])]
    first.start()
    for m in moves+later: m.start()
    pts=x.shape[1]
    n=pts//LEAF
    left=iota((RHS,128),1)<LEAF
    row=iota((256,256),0); col=iota((256,256),1)
    k2=lax.rem(row,128)//8
    s2=onehot(col==lax.rem(row,8)*32+2*k2+row//128)
    same=(iota((256,128),0)//32==lax.rem(iota((256,128),1),8))
    first.wait()
    ext[:,:pts]=x[...]
    for g in range(n//8):
        if g*128%size==0: moves[g*128//size].wait()
        blks=[]
        for q in range(4):
            t=x[:,pl.ds((g*4+q)*128,128)]
            y=pltpu.roll(t,LEAF,1)
            for a,b in ((t,y),(y,t)):
                blks+= [jnp.where(left,a,0.0),jnp.where(left,0.0,b)]
        xh,xl=split(jnp.concatenate(blks,axis=0))
        bh,bl=split(bas[pl.ds(g*128,128),:])
        d=dotnt(jnp.concatenate([xh,xl],axis=1),jnp.concatenate([jnp.concatenate([bh,bh],axis=1),jnp.concatenate([bl,jnp.zeros_like(bl)],axis=1)],axis=0))
        d=jnp.where(same,d[:,:128]+d[:,128:],0.0).reshape(8,32,128).sum(axis=0)
        ext[:,pl.ds(pts+g*256,256)]=exact(jnp.concatenate([d[:RHS],d[RHS:]],axis=1),s2)
    for m in later: m.wait()

def up(x,basis,transfer,upper,chunks=2):
    n=basis.shape[0]
    tra=transfer.reshape(n//8,8,8,128).transpose(0,2,1,3).reshape(n*8,128)
    bas=basis.reshape(n//8,8,16,128).transpose(0,2,1,3).reshape(n*16,128)
    return pl.pallas_call(up_kernel,
        out_shape=(jax.ShapeDtypeStruct((RHS,n*(LEAF+K)),f32),jax.ShapeDtypeStruct(tra.shape,f32),jax.ShapeDtypeStruct(upper.shape,f32)),
        in_specs=[pl.BlockSpec(memory_space=HBM)]*4,
        scratch_shapes=[pltpu.VMEM(x.shape,f32),pltpu.VMEM(bas.shape,f32),pltpu.SemaphoreType.DMA((chunks+1,)),pltpu.SemaphoreType.DMA((2,))],
        compiler_params=pltpu.CompilerParams(vmem_limit_bytes=24<<20),name="up")(in_hbm(x),in_hbm(bas),in_hbm(tra),in_hbm(upper))

def lift_kernel(ext,tra,upt,rep,fs):
    nc=upt.shape[0]
    n=tra.shape[0]//8
    per=n//nc
    pts=n*LEAF
    outs=[]
    for u in range(nc):
        e=jnp.concatenate([tra[pl.ds(((u*per+i)//8)*64+(u*per+i)%8,8,stride=8),:] for i in range(per)],axis=1)
        v=[spread4(ext[:,pl.ds(pts+(u*per+i)//4*128,128)],i%4) for i in range(per)]
        outs.append(mul3(jnp.concatenate(v,axis=1),masked4(e)))
    row=iota((128,128),0); col=iota((128,128),1)
    s3=onehot(col==row//32*32+lax.rem(row,8)*4+lax.rem(row,32)//8)
    cc=exact(jnp.concatenate(outs,axis=1),s3)
    for q in range(8):
        fs[pl.ds(q*nc,nc),:]=upt[:,pl.ds(q*128,128)]
    f=jnp.concatenate([fs[pl.ds(u,8,stride=nc),:] for u in range(nc)],axis=1)
    pr=mul3(jnp.concatenate([spread4(cc,u) for u in range(nc)],axis=1),masked4(f))
    pay=[cc[4*i:4*i+4] for i in range(4)]+[jnp.concatenate([pr[4*i:4*i+4] for i in range(4)],axis=1)]
    for c in range(rep.shape[0]):
        for i in range(5): rep[c,i]=pay[i]

def lift(ext,tra,upper,copies):
    return pl.pallas_call(lift_kernel,
        out_shape=jax.ShapeDtypeStruct((copies,5,4,128),f32),
        in_specs=[pl.BlockSpec(memory_space=pltpu.VMEM)]*3,
        scratch_shapes=[pltpu.VMEM((8*upper.shape[0],128),f32)],
        compiler_params=pltpu.CompilerParams(vmem_limit_bytes=24<<20),name="lift")(ext,tra,upper)

def far_kernel(base,src_h,cpl_h,cb,co,ca,out,table,cpl,src,sem,sem2):
    tiles=co.shape[1]//128
    n=src.shape[1]
    chunks=sem.shape[0]
    size=cpl.shape[0]//chunks
    def chunk(c): return pltpu.make_async_copy(cpl_h.at[pl.ds(c*size,size),:],cpl.at[pl.ds(c*size,size),:],sem.at[c])
    idx=pltpu.make_async_copy(src_h,src,sem2.at[0])
    idx.start()
    for c in range(chunks): chunk(c).start()
    for w,ref in ((base[2],cb),(1,co),(2-base[2],ca)):
        def body(q,_):
            t=ref[:,pl.ds(pl.multiple_of(q*128,128),128)]
            for m in range(4): table[(w*tiles+q)*4+m]=jnp.concatenate(split(spread4(t,m)),axis=0)
            return 0
        lax.fori_loop(0,tiles,body,0,unroll=4)
    idx.wait()
    per=n//chunks
    first=base[0]
    block=iota((8,128),1)//K
    block32=iota((2*RHS,128),1)//K
    def pick(where,four):
        return jnp.where(where<2,jnp.where(where<1,four[0],four[1]),jnp.where(where<3,four[2],four[3]))
    def step(c,_):
        chunk(c).wait()
        for i in range(per):
            t=c*per+i
            off=pl.multiple_of(t*64,64)
            cs=[cpl[pl.ds(off+j,8,stride=8),:] for j in range(8)]
            w=[[pick(block,[pltpu.roll(cs[4*h+p],(p-km)%4*K,1) if p!=km else cs[4*h+p] for p in range(4)]) for h in range(2)] for km in range(4)]
            w=jnp.concatenate([jnp.concatenate(v,axis=1) for v in w],axis=0)
            at=[src[j,t]-first for j in range(8)]
            v=jnp.concatenate([pick(block32,[table[at[4*h+p]] for p in range(4)]) for h in range(2)],axis=1)
            d=dotnt(v,jnp.concatenate(split(w),axis=0))
            out[pl.ds(pl.multiple_of(t*RHS,RHS),RHS),:]=d[:RHS]+d[RHS:]
        return 0
    lax.fori_loop(0,chunks,step,0)

def far(base,src,eb,eo,ea,coupling,chunks=2):
    n=coupling.shape[0]
    view=coupling.reshape(n,8,8,128).transpose(0,2,1,3).reshape(n*64,128)
    blk=pl.BlockSpec((RHS,n*K),lambda g:(0,LEAF//K))
    hbm=pl.BlockSpec(memory_space=HBM)
    return pl.pallas_call(far_kernel,
        out_shape=jax.ShapeDtypeStruct((n*RHS,2*K),f32),grid=(1,),
        in_specs=[pl.BlockSpec(memory_space=pltpu.SMEM),hbm,hbm,blk,blk,blk],
        out_specs=pl.BlockSpec((n*RHS,2*K),lambda g:(0,0)),
        scratch_shapes=[pltpu.VMEM((3*n,2*RHS,128),bf16),pltpu.VMEM((n*64,128),f32),pltpu.SMEM((8,n),jnp.int32),
            pltpu.SemaphoreType.DMA((chunks,)),pltpu.SemaphoreType.DMA((1,))],
        compiler_params=pltpu.CompilerParams(vmem_limit_bytes=24<<20),name="far")(base,in_hbm(src.T),in_hbm(view),eb,eo,ea)

def gather_kernel(csrc,pays,ccp,out):
    nc=ccp.shape[0]//64
    devs=pays.shape[0]
    for u in range(nc):
        w=jnp.concatenate([ccp[pl.ds(u*64+j,8,stride=8),:] for j in range(8)],axis=1)
        vs=[]
        for j in range(8):
            s=csrc[u,j]
            place=lax.rem(s//nc,2)*(devs//2)+s//(2*nc)
            vs.append(spread4(jnp.concatenate([pays[place,i] for i in range(4)],axis=0),lax.rem(s,nc)))
        out[pl.ds(u*RHS,RHS),:]=mul3(jnp.concatenate(vs,axis=1),masked4(w))

def gather(csrc,pays,ccp):
    nc=ccp.shape[0]
    view=ccp.reshape(nc,8,8,128).transpose(0,2,1,3).reshape(nc*64,128)
    vm=pl.BlockSpec(memory_space=pltpu.VMEM)
    return pl.pallas_call(gather_kernel,
        out_shape=jax.ShapeDtypeStruct((nc*RHS,K),f32),
        in_specs=[pl.BlockSpec(memory_space=pltpu.SMEM),vm,vm],
        cost_estimate=pl.CostEstimate(flops=10**10,bytes_accessed=10**7,transcendentals=0),
        compiler_params=pltpu.CompilerParams(vmem_limit_bytes=24<<20),name="gather")(csrc,pays,view)

def down_kernel(base,s0,s1,s2,s3,cfar,gcp,upt,tra,bas,lf,near_ref,out,gs,fs):
    nc=upt.shape[0]; ng=gcp.shape[0]
    n=lf.shape[0]//RHS
    row=iota((K,128),0); col=lax.rem(iota((K,128),1),K)
    s4=onehot(col==lax.rem(row,8)*4+row//8)
    for q in range(8):
        fs[pl.ds(q*nc,nc),:]=upt[:,pl.ds(q*128,128)]
        gs[pl.ds(q*ng,ng),:]=gcp[:,pl.ds(q*128,128)]
    gv=exact(jnp.concatenate([s[:,i*K:(i+1)*K] for s in (s0,s1,s2,s3) for i in range(4)],axis=0),s4)
    gv=[gv[h*RHS:(h+1)*RHS] for h in range(ng)]
    gw=jnp.concatenate([gs[pl.ds(lax.rem(base[1]+ng-h,ng),8,stride=ng),:] for h in range(ng)],axis=1)
    gf=mul3(jnp.concatenate(gv,axis=1),masked4(gw))
    fw=jnp.concatenate([fs[pl.ds(u,8,stride=nc),:] for u in range(nc)],axis=1)
    wh,wl=masked4(fw)
    gh,gl=split(gf)
    down=dotnn(gh,wh)+dotnn(gl,wh)+dotnn(gh,wl)
    row=lax.rem(iota((128,K),0),K); col=iota((128,K),1)
    s5=onehot(row==lax.rem(col,8)*4+col//8)
    down=jnp.concatenate([down[:,u*128:(u+1)*128] for u in range(nc)],axis=0)
    down=exact(down,s5)
    row=lax.rem(iota((128,256),0),K); col=iota((128,256),1)
    p1=onehot(row==2*(lax.rem(col,128)//8)+col//128)
    row=lax.rem(iota((2*K,256),0),K); col=iota((2*K,256),1)
    nat=2*(lax.rem(col,128)//8)+col//128
    p2=onehot(row==lax.rem(nat,4)*8+nat//4)
    p12=jnp.concatenate([p1,p1,p2,p2],axis=0)
    left=iota((RHS,128),1)<LEAF
    per=n//nc
    for u in range(nc):
        cf=cfar[pl.ds(u*RHS,RHS),:]+down[u*RHS:(u+1)*RHS]
        e=jnp.concatenate([tra[pl.ds(((u*per+i)//8)*64+(u*per+i)%8,8,stride=8),:] for i in range(per)],axis=1)
        eh,el=masked4(e)
        ch,cl=split(cf)
        d=dotnn(jnp.concatenate([ch,cl,ch],axis=1),jnp.concatenate([eh,eh,el],axis=0))
        d=jnp.concatenate([d[:,i*128:(i+1)*128] for i in range(per)],axis=0)
        q=dotnn(jnp.concatenate([*split(d),*split(lf[pl.ds(u*per*RHS,per*RHS),:])],axis=1),p12)
        for b in range(per//8):
            g=(u*per)//8+b
            z=q[b*128:(b+1)*128].reshape(8,RHS,256)
            z=jnp.stack([z[:,:,:128],z[:,:,128:]],axis=1).reshape(256,128)
            same=(iota((256,128),0)//32==lax.rem(iota((256,128),1),8))
            zh,zl=split(jnp.where(same,z,0.0))
            bh,bl=split(bas[pl.ds(g*128,128),:])
            o=dotnn(jnp.concatenate([zh,zl],axis=1),jnp.concatenate([jnp.concatenate([bh,bl],axis=1),jnp.concatenate([bh,jnp.zeros_like(bl)],axis=1)],axis=0))
            o=(o[:,:128]+o[:,128:]).reshape(8,2,RHS,128)
            for m in range(4):
                a=jnp.where(left,o[2*m,0],o[2*m,1])
                c=jnp.where(left,o[2*m+1,0],o[2*m+1,1])
                r=jnp.where(left,a,c)+pltpu.roll(jnp.where(left,c,a),LEAF,1)
                at=pl.ds(g*512+m*128,128)
                out[:,at]=near_ref[:,at]+r

def down(base,sums,cfar,gcp,upper,tra,basis,lf,nearv):
    n=basis.shape[0]; nc=upper.shape[0]; ng=gcp.shape[0]
    bas=basis.reshape(n//8,8,16,128).transpose(0,2,1,3).reshape(n*16,128)
    vm=pl.BlockSpec(memory_space=pltpu.VMEM)
    return pl.pallas_call(down_kernel,
        out_shape=jax.ShapeDtypeStruct((RHS,n*LEAF),f32),
        in_specs=[pl.BlockSpec(memory_space=pltpu.SMEM)]+[vm]*11,
        scratch_shapes=[pltpu.VMEM((8*ng,128),f32),pltpu.VMEM((8*nc,128),f32)],
        compiler_params=pltpu.CompilerParams(vmem_limit_bytes=24<<20),name="down")(base,*sums,cfar,gcp,upper,tra,bas,lf,nearv)

def across(devs):
    return [[2*i+c for i in range(devs//2)] for c in range(2)]

def per_device(right_sides,near_blocks,near_source,near_count,basis,leaf_source,leaf_coupling,leaf_transfer,cluster_source,cluster_coupling,cluster_transfer,group_coupling):
    both=("group","leaf")
    leaves=near_blocks.shape[0]
    devs=lax.axis_size("leaf")
    every=lax.axis_size(both)
    ng=lax.axis_size("group")
    base=jnp.stack([(lax.axis_index(both)-1)*leaves,lax.axis_index("group"),2*lax.rem(lax.axis_index("leaf")+1,2)]).astype(jnp.int32)
    ext,tra,upper=up(right_sides,basis,leaf_transfer,cluster_transfer)
    eb=lax.ppermute(ext,both,[(i,i^1) for i in range(every)])
    ea=lax.ppermute(ext,both,[p for i in range(1,every-1,2) for p in ((i,i+1),(i+1,i))])
    rep=lift(ext,tra,upper,devs//2)
    some=lax.all_to_all(rep,"leaf",0,0,tiled=True,axis_index_groups=across(devs))
    nearv=near(base,near_source,near_count,eb,ext,ea,near_blocks)
    lf=far(base,leaf_source,eb,ext,ea,leaf_coupling)
    some,nearv,lf=lax.optimization_barrier((some,nearv,lf))
    pays=lax.all_gather(some,"leaf",axis=0,tiled=True,axis_index_groups=[[2*i,2*i+1] for i in range(devs//2)])
    total=pays[:,4].sum(axis=0)
    sums=[total]+[lax.ppermute(total,"group",[(i,(i+k)%ng) for i in range(ng)]) for k in range(1,ng)]
    cfar=gather(cluster_source,pays,cluster_coupling)
    return down(base,sums,cfar,group_coupling.reshape(-1,1024),upper,tra,basis,lf,nearv)

def solution(mesh):
    both=("group","leaf")
    one=P(both)
    two=P(both,None)
    three=P(both,None,None)
    return jax.shard_map(per_device,mesh=mesh,
        in_specs=(P(None,both),three,two,one,two,two,three,two,two,three,two,P("group",None,None)),
        out_specs=P(None,both),check_vma=False)
```

```python
import functools

import jax
import jax.numpy as jnp
from jax import lax
from jax.experimental import pallas as pl
from jax.experimental.pallas import tpu as pltpu
from jax.sharding import PartitionSpec as P

LEAF=64;K=32;RHS=16
f32=jnp.float32; bf16=jnp.bfloat16
NT=(((1,),(1,)),((),()))
def split(a):
    h=a.astype(bf16)
    return h,(a-h.astype(f32)).astype(bf16)
def dotnt(a,b): return lax.dot_general(a,b,NT,preferred_element_type=f32)
def dotnn(a,b): return lax.dot_general(a,b,(((1,),(0,)),((),())),preferred_element_type=f32)

HBM=pltpu.HBM
def in_hbm(v): return pltpu.with_memory_space_constraint(v,HBM)

def point_table(x_ref, first, leaves, hi, lo):
    left=lax.broadcasted_iota(jnp.int32,(RHS,128),1)<LEAF
    def body(q,_):
        x=x_ref[:,pl.ds(pl.multiple_of(q*128,128),128)]
        y=pltpu.roll(x,LEAF,1)
        for n,(a,b) in enumerate(((x,y),(y,x))):
            h,l=split(jnp.where(left,a,b))
            hi[first+2*q+n]=h
            lo[first+2*q+n]=l
        return 0
    lax.fori_loop(0,leaves//2,body,0,unroll=4)

def near_kernel(base, src_h, cnt_h, nb_h, xb, xo, xa, out, hi, lo, weave, acc, nb, src, cnt, sem, sem2):
    n=out.shape[1]//LEAF
    chunks=sem.shape[0]
    size=nb.shape[0]//chunks
    def chunk(c): return pltpu.make_async_copy(nb_h.at[pl.ds(c*size,size),:],nb.at[pl.ds(c*size,size),:],sem.at[c])
    ca=pltpu.make_async_copy(src_h,src,sem2.at[0]); cb=pltpu.make_async_copy(cnt_h,cnt,sem2.at[1])
    ca.start(); cb.start()
    for c in range(chunks): chunk(c).start()
    point_table(xo,n,n,hi,lo)
    point_table(xb,base[2]*n,n,hi,lo)
    point_table(xa,(2-base[2])*n,n,hi,lo)
    hi[3*n]=jnp.zeros((RHS,128),bf16)
    lo[3*n]=jnp.zeros((RHS,128),bf16)
    row=lax.broadcasted_iota(jnp.int32,(256,128),0)
    col=lax.broadcasted_iota(jnp.int32,(256,128),1)
    a=lax.rem(col,64)
    weave[...]=((row//128==col//64)&(lax.rem(row,64)==lax.rem(a,2)*32+a//2)).astype(f32).astype(bf16)
    ca.wait(); cb.wait()
    per=n//chunks
    first=base[0]
    left=lax.broadcasted_iota(jnp.int32,(RHS,128),1)<LEAF
    left32=lax.broadcasted_iota(jnp.int32,(32,128),1)<LEAF
    def join(table,at): return jnp.concatenate([jnp.where(left,table[at[2*p]],table[at[2*p+1]]) for p in range(4)],axis=1)
    def step(c,_):
        chunk(c).wait()
        for pair in range(per//2):
            for m in range(2):
                t=c*per+pair*2+m
                off=pl.multiple_of(t*256,256)
                even=[];odd=[]
                for p in range(4):
                    a=nb[pl.ds(off+2*p,32,stride=8),:]
                    b=nb[pl.ds(off+2*p+1,32,stride=8),:]
                    even.append(jnp.where(left32,a,pltpu.roll(b,LEAF,1)))
                    odd.append(jnp.where(left32,pltpu.roll(a,LEAF,1),b))
                w=jnp.concatenate([jnp.concatenate(even,axis=1),jnp.concatenate(odd,axis=1)],axis=0)
                live=cnt[t]
                at=[jnp.where(j<live,src[j,t]-first,3*n) for j in range(8)]
                d=dotnt(jnp.concatenate([join(hi,at),join(lo,at)],axis=0),jnp.concatenate(split(w),axis=0))
                acc[pl.ds(pl.multiple_of((c*per+pair*2)*(RHS//2),RHS),RHS),m*128:(m+1)*128]=d[:RHS]+d[RHS:]
        return 0
    lax.fori_loop(0,chunks,step,0)
    d=dotnn(jnp.concatenate(split(acc[...]),axis=0),weave[...])
    d=d[:n*RHS//2]+d[n*RHS//2:]
    for q in range(n//2): out[:,q*128:(q+1)*128]=d[q*RHS:(q+1)*RHS]

def near(base,src,cnt,xb,xo,xa,nb,chunks=4):
    leaves=nb.shape[0]
    view=nb.reshape(leaves,8,32,128).transpose(0,2,1,3).reshape(leaves*256,128)
    hbm=pl.BlockSpec(memory_space=HBM)
    vm=pl.BlockSpec(memory_space=pltpu.VMEM)
    return pl.pallas_call(near_kernel,
        out_shape=jax.ShapeDtypeStruct((RHS,leaves*LEAF),f32),
        in_specs=[pl.BlockSpec(memory_space=pltpu.SMEM),hbm,hbm,hbm,vm,vm,vm],
        out_specs=vm,
        scratch_shapes=[pltpu.VMEM((3*leaves+1,RHS,128),bf16)]*2+[pltpu.VMEM((256,128),bf16),pltpu.VMEM((leaves//2*RHS,256),f32),pltpu.VMEM((leaves*256,128),f32),
            pltpu.SMEM((8,leaves),jnp.int32),pltpu.SMEM((leaves,),jnp.int32),pltpu.SemaphoreType.DMA((chunks,)),pltpu.SemaphoreType.DMA((2,))],
        cost_estimate=pl.CostEstimate(flops=10**11,bytes_accessed=10**7,transcendentals=0),
        compiler_params=pltpu.CompilerParams(vmem_limit_bytes=24<<20),
        name="near")(base,in_hbm(src.T),in_hbm(cnt),in_hbm(view),xb,xo,xa)

def iota(shape,d): return lax.broadcasted_iota(jnp.int32,shape,d)
def onehot(cond): return cond.astype(f32).astype(bf16)
def exact(v,m):
    d=dotnn(jnp.concatenate(split(v),axis=0),m)
    return d[:v.shape[0]]+d[v.shape[0]:]
def wide(v,w):
    d=dotnt(jnp.concatenate(split(v),axis=0),jnp.concatenate(w,axis=0))
    return d[:RHS]+d[RHS:]
def spread4(tile,m):
    block=jnp.where(iota(tile.shape,1)//K==m,tile,0.0)
    block=block+pltpu.roll(block,64,1)
    return block+pltpu.roll(block,32,1)
def masked4(rows):
    n=rows.shape[1]//128
    lane=iota((16,128),1)//K
    half=iota((16,128),0)//8
    keep=[onehot(lane==half+2*p) for p in range(2)]
    h=rows.astype(bf16).astype(f32)
    out=[]
    for v in (h,rows-h):
        w=jnp.concatenate([v,v],axis=0).astype(bf16)
        out.append(jnp.concatenate([w*jnp.concatenate([m]*n,axis=1) for m in keep],axis=0))
    return out

def mul3(v,w):
    d=wide(v,w)
    n=w[0].shape[0]
    return d[:,:n]+d[:,n:]

def up_kernel(x_h,bas_h,tra_h,upt_h,ext,tra,upt,x,bas,sem,sem2):
    chunks=sem.shape[0]-1
    size=bas.shape[0]//chunks
    first=pltpu.make_async_copy(x_h,x,sem.at[chunks])
    moves=[pltpu.make_async_copy(bas_h.at[pl.ds(c*size,size),:],bas.at[pl.ds(c*size,size),:],sem.at[c]) for c in range(chunks)]
    later=[pltpu.make_async_copy(tra_h,tra,sem2.at[0]),pltpu.make_async_copy(upt_h,upt,sem2.at[1])]
    first.start()
    for m in moves+later: m.start()
    pts=x.shape[1]
    n=pts//LEAF
    left=iota((RHS,128),1)<LEAF
    row=iota((256,256),0); col=iota((256,256),1)
    k2=lax.rem(row,128)//8
    s2=onehot(col==lax.rem(row,8)*32+2*k2+row//128)
    same=(iota((256,128),0)//32==lax.rem(iota((256,128),1),8))
    first.wait()
    ext[:,:pts]=x[...]
    rows=[]
    for g in range(n//8):
        if g*128%size==0: moves[g*128//size].wait()
        blks=[]
        for q in range(4):
            t=x[:,pl.ds((g*4+q)*128,128)]
            y=pltpu.roll(t,LEAF,1)
            for a,b in ((t,y),(y,t)):
                blks+= [jnp.where(left,a,0.0),jnp.where(left,0.0,b)]
        xh,xl=split(jnp.concatenate(blks,axis=0))
        bh,bl=split(bas[pl.ds(g*128,128),:])
        d=dotnt(jnp.concatenate([xh,xl],axis=1),jnp.concatenate([jnp.concatenate([bh,bh],axis=1),jnp.concatenate([bl,jnp.zeros_like(bl)],axis=1)],axis=0))
        d=jnp.where(same,d[:,:128]+d[:,128:],0.0).reshape(8,32,128).sum(axis=0)
        rows.append(jnp.concatenate([d[:RHS],d[RHS:]],axis=1))
    d=exact(jnp.concatenate(rows,axis=0),s2)
    for g in range(n//8): ext[:,pl.ds(pts+g*256,256)]=d[g*RHS:(g+1)*RHS]
    for m in later: m.wait()

def up(x,basis,transfer,upper,chunks=2):
    n=basis.shape[0]
    tra=transfer.reshape(n//8,8,8,128).transpose(0,2,1,3).reshape(n*8,128)
    bas=basis.reshape(n//8,8,16,128).transpose(0,2,1,3).reshape(n*16,128)
    return pl.pallas_call(up_kernel,
        out_shape=(jax.ShapeDtypeStruct((RHS,n*(LEAF+K)),f32),jax.ShapeDtypeStruct(tra.shape,f32),jax.ShapeDtypeStruct(upper.shape,f32)),
        in_specs=[pl.BlockSpec(memory_space=HBM)]*4,
        scratch_shapes=[pltpu.VMEM(x.shape,f32),pltpu.VMEM(bas.shape,f32),pltpu.SemaphoreType.DMA((chunks+1,)),pltpu.SemaphoreType.DMA((2,))],
        compiler_params=pltpu.CompilerParams(vmem_limit_bytes=24<<20),name="up")(in_hbm(x),in_hbm(bas),in_hbm(tra),in_hbm(upper))

def lift_kernel(ext,tra,upt,rep,fs):
    nc=upt.shape[0]
    n=tra.shape[0]//8
    per=n//nc
    pts=n*LEAF
    outs=[]
    for u in range(nc):
        e=jnp.concatenate([tra[pl.ds(((u*per+i)//8)*64+(u*per+i)%8,8,stride=8),:] for i in range(per)],axis=1)
        v=[spread4(ext[:,pl.ds(pts+(u*per+i)//4*128,128)],i%4) for i in range(per)]
        outs.append(mul3(jnp.concatenate(v,axis=1),masked4(e)))
    row=iota((128,128),0); col=iota((128,128),1)
    s3=onehot(col==row//32*32+lax.rem(row,8)*4+lax.rem(row,32)//8)
    cc=exact(jnp.concatenate(outs,axis=1),s3)
    for q in range(8):
        fs[pl.ds(q*nc,nc),:]=upt[:,pl.ds(q*128,128)]
    f=jnp.concatenate([fs[pl.ds(u,8,stride=nc),:] for u in range(nc)],axis=1)
    pr=mul3(jnp.concatenate([spread4(cc,u) for u in range(nc)],axis=1),masked4(f))
    pay=[cc[4*i:4*i+4] for i in range(4)]+[jnp.concatenate([pr[4*i:4*i+4] for i in range(4)],axis=1)]
    for c in range(rep.shape[0]):
        for i in range(5): rep[c,i]=pay[i]

def lift(ext,tra,upper,copies):
    return pl.pallas_call(lift_kernel,
        out_shape=jax.ShapeDtypeStruct((copies,5,4,128),f32),
        in_specs=[pl.BlockSpec(memory_space=pltpu.VMEM)]*3,
        scratch_shapes=[pltpu.VMEM((8*upper.shape[0],128),f32)],
        compiler_params=pltpu.CompilerParams(vmem_limit_bytes=24<<20),name="lift")(ext,tra,upper)

def far_kernel(base,src_h,cpl_h,cb,co,ca,out,table,cpl,src,sem,sem2):
    n=src.shape[1]
    tiles=n*K//128
    skip=n*LEAF
    chunks=sem.shape[0]
    size=cpl.shape[0]//chunks
    def chunk(c): return pltpu.make_async_copy(cpl_h.at[pl.ds(c*size,size),:],cpl.at[pl.ds(c*size,size),:],sem.at[c])
    idx=pltpu.make_async_copy(src_h,src,sem2.at[0])
    idx.start()
    for c in range(chunks): chunk(c).start()
    for w,ref in ((base[2],cb),(1,co),(2-base[2],ca)):
        def body(q,_):
            t=ref[:,pl.ds(pl.multiple_of(skip+q*128,128),128)]
            for m in range(4): table[(w*tiles+q)*4+m]=jnp.concatenate(split(spread4(t,m)),axis=0)
            return 0
        lax.fori_loop(0,tiles,body,0,unroll=8)
    idx.wait()
    per=n//chunks
    first=base[0]
    block=iota((8,128),1)//K
    block32=iota((2*RHS,128),1)//K
    def pick(where,four):
        return jnp.where(where<2,jnp.where(where<1,four[0],four[1]),jnp.where(where<3,four[2],four[3]))
    def step(c,_):
        chunk(c).wait()
        for i in range(per):
            t=c*per+i
            off=pl.multiple_of(t*64,64)
            cs=[cpl[pl.ds(off+j,8,stride=8),:] for j in range(8)]
            w=[[pick(block,[pltpu.roll(cs[4*h+p],(p-km)%4*K,1) if p!=km else cs[4*h+p] for p in range(4)]) for h in range(2)] for km in range(4)]
            w=jnp.concatenate([jnp.concatenate(v,axis=1) for v in w],axis=0)
            at=[src[j,t]-first for j in range(8)]
            v=jnp.concatenate([pick(block32,[table[at[4*h+p]] for p in range(4)]) for h in range(2)],axis=1)
            d=dotnt(v,jnp.concatenate(split(w),axis=0))
            out[pl.ds(pl.multiple_of(t*RHS,RHS),RHS),:]=d[:RHS]+d[RHS:]
        return 0
    lax.fori_loop(0,chunks,step,0)

def far(base,src,eb,eo,ea,coupling,chunks=2):
    n=coupling.shape[0]
    view=coupling.reshape(n,8,8,128).transpose(0,2,1,3).reshape(n*64,128)
    vm=pl.BlockSpec(memory_space=pltpu.VMEM)
    hbm=pl.BlockSpec(memory_space=HBM)
    return pl.pallas_call(far_kernel,
        out_shape=jax.ShapeDtypeStruct((n*RHS,2*K),f32),
        in_specs=[pl.BlockSpec(memory_space=pltpu.SMEM),hbm,hbm,vm,vm,vm],
        out_specs=vm,
        scratch_shapes=[pltpu.VMEM((3*n,2*RHS,128),bf16),pltpu.VMEM((n*64,128),f32),pltpu.SMEM((8,n),jnp.int32),
            pltpu.SemaphoreType.DMA((chunks,)),pltpu.SemaphoreType.DMA((1,))],
        compiler_params=pltpu.CompilerParams(vmem_limit_bytes=24<<20),name="far")(base,in_hbm(src.T),in_hbm(view),eb,eo,ea)

def gather_kernel(csrc,pays,ccp,out):
    nc=ccp.shape[0]//64
    devs=pays.shape[0]
    for u in range(nc):
        w=jnp.concatenate([ccp[pl.ds(u*64+j,8,stride=8),:] for j in range(8)],axis=1)
        vs=[]
        for j in range(8):
            s=csrc[u,j]
            place=lax.rem(s//nc,2)*(devs//2)+s//(2*nc)
            vs.append(spread4(jnp.concatenate([pays[place,i] for i in range(4)],axis=0),lax.rem(s,nc)))
        out[pl.ds(u*RHS,RHS),:]=mul3(jnp.concatenate(vs,axis=1),masked4(w))

def gather(csrc,pays,ccp):
    nc=ccp.shape[0]
    view=ccp.reshape(nc,8,8,128).transpose(0,2,1,3).reshape(nc*64,128)
    vm=pl.BlockSpec(memory_space=pltpu.VMEM)
    return pl.pallas_call(gather_kernel,
        out_shape=jax.ShapeDtypeStruct((nc*RHS,K),f32),
        in_specs=[pl.BlockSpec(memory_space=pltpu.SMEM),vm,vm],
        cost_estimate=pl.CostEstimate(flops=10**10,bytes_accessed=10**7,transcendentals=0),
        compiler_params=pltpu.CompilerParams(vmem_limit_bytes=24<<20),name="gather")(csrc,pays,view)

def down_kernel(base,s0,s1,s2,s3,cfar,gcp,upt,tra,bas,lf,near_ref,out,gs,fs):
    nc=upt.shape[0]; ng=gcp.shape[0]
    n=lf.shape[0]//RHS
    row=iota((K,128),0); col=lax.rem(iota((K,128),1),K)
    s4=onehot(col==lax.rem(row,8)*4+row//8)
    for q in range(8):
        fs[pl.ds(q*nc,nc),:]=upt[:,pl.ds(q*128,128)]
        gs[pl.ds(q*ng,ng),:]=gcp[:,pl.ds(q*128,128)]
    gv=exact(jnp.concatenate([s[:,i*K:(i+1)*K] for s in (s0,s1,s2,s3) for i in range(4)],axis=0),s4)
    gv=[gv[h*RHS:(h+1)*RHS] for h in range(ng)]
    gw=jnp.concatenate([gs[pl.ds(lax.rem(base[1]+ng-h,ng),8,stride=ng),:] for h in range(ng)],axis=1)
    gf=mul3(jnp.concatenate(gv,axis=1),masked4(gw))
    fw=jnp.concatenate([fs[pl.ds(u,8,stride=nc),:] for u in range(nc)],axis=1)
    wh,wl=masked4(fw)
    gh,gl=split(gf)
    down=dotnn(gh,wh)+dotnn(gl,wh)+dotnn(gh,wl)
    row=lax.rem(iota((128,K),0),K); col=iota((128,K),1)
    s5=onehot(row==lax.rem(col,8)*4+col//8)
    down=jnp.concatenate([down[:,u*128:(u+1)*128] for u in range(nc)],axis=0)
    down=exact(down,s5)
    row=lax.rem(iota((128,256),0),K); col=iota((128,256),1)
    p1=onehot(row==2*(lax.rem(col,128)//8)+col//128)
    row=lax.rem(iota((2*K,256),0),K); col=iota((2*K,256),1)
    nat=2*(lax.rem(col,128)//8)+col//128
    p2=onehot(row==lax.rem(nat,4)*8+nat//4)
    p12=jnp.concatenate([p1,p1,p2,p2],axis=0)
    left=iota((RHS,128),1)<LEAF
    per=n//nc
    ds=[]
    for u in range(nc):
        cf=cfar[pl.ds(u*RHS,RHS),:]+down[u*RHS:(u+1)*RHS]
        e=jnp.concatenate([tra[pl.ds(((u*per+i)//8)*64+(u*per+i)%8,8,stride=8),:] for i in range(per)],axis=1)
        eh,el=masked4(e)
        ch,cl=split(cf)
        d=dotnn(jnp.concatenate([ch,cl,ch],axis=1),jnp.concatenate([eh,eh,el],axis=0))
        ds+=[d[:,i*128:(i+1)*128] for i in range(per)]
    q=dotnn(jnp.concatenate([*split(jnp.concatenate(ds,axis=0)),*split(lf[...])],axis=1),p12)
    same=(iota((256,128),0)//32==lax.rem(iota((256,128),1),8))
    for g in range(n//8):
        z=q[g*128:(g+1)*128].reshape(8,RHS,256)
        z=jnp.stack([z[:,:,:128],z[:,:,128:]],axis=1).reshape(256,128)
        zh,zl=split(jnp.where(same,z,0.0))
        bh,bl=split(bas[pl.ds(g*128,128),:])
        o=dotnn(jnp.concatenate([zh,zl],axis=1),jnp.concatenate([jnp.concatenate([bh,bl],axis=1),jnp.concatenate([bh,jnp.zeros_like(bl)],axis=1)],axis=0))
        o=(o[:,:128]+o[:,128:]).reshape(8,2,RHS,128)
        for m in range(4):
            a=jnp.where(left,o[2*m,0],o[2*m,1])
            c=jnp.where(left,o[2*m+1,0],o[2*m+1,1])
            r=jnp.where(left,a,c)+pltpu.roll(jnp.where(left,c,a),LEAF,1)
            at=pl.ds(g*512+m*128,128)
            out[:,at]=near_ref[:,at]+r

def down(base,sums,cfar,gcp,upper,tra,basis,lf,nearv):
    n=basis.shape[0]; nc=upper.shape[0]; ng=gcp.shape[0]
    bas=basis.reshape(n//8,8,16,128).transpose(0,2,1,3).reshape(n*16,128)
    vm=pl.BlockSpec(memory_space=pltpu.VMEM)
    return pl.pallas_call(down_kernel,
        out_shape=jax.ShapeDtypeStruct((RHS,n*LEAF),f32),
        in_specs=[pl.BlockSpec(memory_space=pltpu.SMEM)]+[vm]*11,
        scratch_shapes=[pltpu.VMEM((8*ng,128),f32),pltpu.VMEM((8*nc,128),f32)],
        compiler_params=pltpu.CompilerParams(vmem_limit_bytes=24<<20),name="down")(base,*sums,cfar,gcp,upper,tra,bas,lf,nearv)

def across(devs):
    return [[2*i+c for i in range(devs//2)] for c in range(2)]

def per_device(right_sides,near_blocks,near_source,near_count,basis,leaf_source,leaf_coupling,leaf_transfer,cluster_source,cluster_coupling,cluster_transfer,group_coupling):
    both=("group","leaf")
    leaves=near_blocks.shape[0]
    devs=lax.axis_size("leaf")
    every=lax.axis_size(both)
    ng=lax.axis_size("group")
    base=jnp.stack([(lax.axis_index(both)-1)*leaves,lax.axis_index("group"),2*lax.rem(lax.axis_index("leaf")+1,2)]).astype(jnp.int32)
    ext,tra,upper=up(right_sides,basis,leaf_transfer,cluster_transfer)
    eb=lax.ppermute(ext,both,[(i,i^1) for i in range(every)])
    ea=lax.ppermute(ext,both,[p for i in range(1,every-1,2) for p in ((i,i+1),(i+1,i))])
    rep=lift(ext,tra,upper,devs//2)
    some=lax.all_to_all(rep,"leaf",0,0,tiled=True,axis_index_groups=across(devs))
    nearv=near(base,near_source,near_count,eb,ext,ea,near_blocks)
    lf=far(base,leaf_source,eb,ext,ea,leaf_coupling)
    some,nearv,lf=lax.optimization_barrier((some,nearv,lf))
    pays=lax.all_gather(some,"leaf",axis=0,tiled=True,axis_index_groups=[[2*i,2*i+1] for i in range(devs//2)])
    total=pays[:,4].sum(axis=0)
    sums=[total]+[lax.ppermute(total,"group",[(i,(i+k)%ng) for i in range(ng)]) for k in range(1,ng)]
    cfar=gather(cluster_source,pays,cluster_coupling)
    return down(base,sums,cfar,group_coupling.reshape(-1,1024),upper,tra,basis,lf,nearv)

def solution(mesh):
    both=("group","leaf")
    one=P(both)
    two=P(both,None)
    three=P(both,None,None)
    return jax.shard_map(per_device,mesh=mesh,
        in_specs=(P(None,both),three,two,one,two,two,three,two,two,three,two,P("group",None,None)),
        out_specs=P(None,both),check_vma=False)
```

```python
import functools

import jax
import jax.numpy as jnp
from jax import lax
from jax.experimental import pallas as pl
from jax.experimental.pallas import tpu as pltpu
from jax.sharding import PartitionSpec as P

LEAF=64;K=32;RHS=16
f32=jnp.float32; bf16=jnp.bfloat16
NT=(((1,),(1,)),((),()))
def split(a):
    h=a.astype(bf16)
    return h,(a-h.astype(f32)).astype(bf16)
def dotnt(a,b): return lax.dot_general(a,b,NT,preferred_element_type=f32)
def dotnn(a,b): return lax.dot_general(a,b,(((1,),(0,)),((),())),preferred_element_type=f32)

HBM=pltpu.HBM
def in_hbm(v): return pltpu.with_memory_space_constraint(v,HBM)

def point_table(x_ref, first, leaves, hi, lo):
    left=lax.broadcasted_iota(jnp.int32,(RHS,128),1)<LEAF
    def body(q,_):
        x=x_ref[:,pl.ds(pl.multiple_of(q*128,128),128)]
        y=pltpu.roll(x,LEAF,1)
        for n,(a,b) in enumerate(((x,y),(y,x))):
            h,l=split(jnp.where(left,a,b))
            hi[first+2*q+n]=h
            lo[first+2*q+n]=l
        return 0
    lax.fori_loop(0,leaves//2,body,0,unroll=4)

def near_kernel(base, src_h, cnt_h, nb_h, xb, xo, xa, out, hi, lo, weave, acc, nb, src, cnt, sem, sem2):
    n=out.shape[1]//LEAF
    chunks=sem.shape[0]
    size=nb.shape[0]//chunks
    def chunk(c): return pltpu.make_async_copy(nb_h.at[pl.ds(c*size,size),:],nb.at[pl.ds(c*size,size),:],sem.at[c])
    ca=pltpu.make_async_copy(src_h,src,sem2.at[0]); cb=pltpu.make_async_copy(cnt_h,cnt,sem2.at[1])
    ca.start(); cb.start()
    for c in range(chunks): chunk(c).start()
    point_table(xo,n,n,hi,lo)
    point_table(xb,base[2]*n,n,hi,lo)
    point_table(xa,(2-base[2])*n,n,hi,lo)
    hi[3*n]=jnp.zeros((RHS,128),bf16)
    lo[3*n]=jnp.zeros((RHS,128),bf16)
    row=lax.broadcasted_iota(jnp.int32,(256,128),0)
    col=lax.broadcasted_iota(jnp.int32,(256,128),1)
    a=lax.rem(col,64)
    weave[...]=((row//128==col//64)&(lax.rem(row,64)==lax.rem(a,2)*32+a//2)).astype(f32).astype(bf16)
    ca.wait(); cb.wait()
    per=n//chunks
    first=base[0]
    left=lax.broadcasted_iota(jnp.int32,(RHS,128),1)<LEAF
    left32=lax.broadcasted_iota(jnp.int32,(32,128),1)<LEAF
    def join(table,at): return jnp.concatenate([jnp.where(left,table[at[2*p]],table[at[2*p+1]]) for p in range(4)],axis=1)
    def step(c,_):
        chunk(c).wait()
        for pair in range(per//2):
            for m in range(2):
                t=c*per+pair*2+m
                off=pl.multiple_of(t*256,256)
                even=[];odd=[]
                for p in range(4):
                    a=nb[pl.ds(off+2*p,32,stride=8),:]
                    b=nb[pl.ds(off+2*p+1,32,stride=8),:]
                    even.append(jnp.where(left32,a,pltpu.roll(b,LEAF,1)))
                    odd.append(jnp.where(left32,pltpu.roll(a,LEAF,1),b))
                w=jnp.concatenate([jnp.concatenate(even,axis=1),jnp.concatenate(odd,axis=1)],axis=0)
                live=cnt[t]
                at=[jnp.where(j<live,src[j,t]-first,3*n) for j in range(8)]
                d=dotnt(jnp.concatenate([join(hi,at),join(lo,at)],axis=0),jnp.concatenate(split(w),axis=0))
                acc[pl.ds(pl.multiple_of((c*per+pair*2)*(RHS//2),RHS),RHS),m*128:(m+1)*128]=d[:RHS]+d[RHS:]
        return 0
    lax.fori_loop(0,chunks,step,0)
    d=dotnn(jnp.concatenate(split(acc[...]),axis=0),weave[...])
    d=d[:n*RHS//2]+d[n*RHS//2:]
    for q in range(n//2): out[:,q*128:(q+1)*128]=d[q*RHS:(q+1)*RHS]

def near(base,src,cnt,xb,xo,xa,nb,chunks=4):
    leaves=nb.shape[0]
    view=nb.reshape(leaves,8,32,128).transpose(0,2,1,3).reshape(leaves*256,128)
    hbm=pl.BlockSpec(memory_space=HBM)
    vm=pl.BlockSpec(memory_space=pltpu.VMEM)
    return pl.pallas_call(near_kernel,
        out_shape=jax.ShapeDtypeStruct((RHS,leaves*LEAF),f32),
        in_specs=[pl.BlockSpec(memory_space=pltpu.SMEM),hbm,hbm,hbm,vm,vm,vm],
        out_specs=vm,
        scratch_shapes=[pltpu.VMEM((3*leaves+1,RHS,128),bf16)]*2+[pltpu.VMEM((256,128),bf16),pltpu.VMEM((leaves//2*RHS,256),f32),pltpu.VMEM((leaves*256,128),f32),
            pltpu.SMEM((8,leaves),jnp.int32),pltpu.SMEM((leaves,),jnp.int32),pltpu.SemaphoreType.DMA((chunks,)),pltpu.SemaphoreType.DMA((2,))],
        cost_estimate=pl.CostEstimate(flops=10**11,bytes_accessed=10**7,transcendentals=0),
        compiler_params=pltpu.CompilerParams(vmem_limit_bytes=24<<20),
        name="near")(base,in_hbm(src.T),in_hbm(cnt),in_hbm(view),xb,xo,xa)

def iota(shape,d): return lax.broadcasted_iota(jnp.int32,shape,d)
def onehot(cond): return cond.astype(f32).astype(bf16)
def exact(v,m):
    d=dotnn(jnp.concatenate(split(v),axis=0),m)
    return d[:v.shape[0]]+d[v.shape[0]:]
def wide(v,w):
    d=dotnt(jnp.concatenate(split(v),axis=0),jnp.concatenate(w,axis=0))
    return d[:RHS]+d[RHS:]
def spread4(tile,m):
    block=jnp.where(iota(tile.shape,1)//K==m,tile,0.0)
    block=block+pltpu.roll(block,64,1)
    return block+pltpu.roll(block,32,1)
def masked4(rows):
    n=rows.shape[1]//128
    lane=iota((16,128),1)//K
    half=iota((16,128),0)//8
    keep=[onehot(lane==half+2*p) for p in range(2)]
    h=rows.astype(bf16).astype(f32)
    out=[]
    for v in (h,rows-h):
        w=jnp.concatenate([v,v],axis=0).astype(bf16)
        out.append(jnp.concatenate([w*jnp.concatenate([m]*n,axis=1) for m in keep],axis=0))
    return out

def mul3(v,w):
    d=wide(v,w)
    n=w[0].shape[0]
    return d[:,:n]+d[:,n:]

def up_kernel(x_h,bas_h,tra_h,upt_h,ext,tra,upt,x,bas,sem,sem2):
    chunks=sem.shape[0]-1
    size=bas.shape[0]//chunks
    first=pltpu.make_async_copy(x_h,x,sem.at[chunks])
    moves=[pltpu.make_async_copy(bas_h.at[pl.ds(c*size,size),:],bas.at[pl.ds(c*size,size),:],sem.at[c]) for c in range(chunks)]
    later=[pltpu.make_async_copy(tra_h,tra,sem2.at[0]),pltpu.make_async_copy(upt_h,upt,sem2.at[1])]
    first.start()
    for m in moves+later: m.start()
    pts=x.shape[1]
    n=pts//LEAF
    left=iota((RHS,128),1)<LEAF
    row=iota((256,256),0); col=iota((256,256),1)
    k2=lax.rem(row,128)//8
    s2=onehot(col==lax.rem(row,8)*32+2*k2+row//128)
    same=(iota((256,128),0)//32==lax.rem(iota((256,128),1),8))
    first.wait()
    ext[:,:pts]=x[...]
    rows=[]
    for g in range(n//8):
        if g*128%size==0: moves[g*128//size].wait()
        blks=[]
        for q in range(4):
            t=x[:,pl.ds((g*4+q)*128,128)]
            y=pltpu.roll(t,LEAF,1)
            for a,b in ((t,y),(y,t)):
                blks+= [jnp.where(left,a,0.0),jnp.where(left,0.0,b)]
        xh,xl=split(jnp.concatenate(blks,axis=0))
        bh,bl=split(bas[pl.ds(g*128,128),:])
        d=dotnt(jnp.concatenate([xh,xl],axis=1),jnp.concatenate([jnp.concatenate([bh,bh],axis=1),jnp.concatenate([bl,jnp.zeros_like(bl)],axis=1)],axis=0))
        d=jnp.where(same,d[:,:128]+d[:,128:],0.0).reshape(8,32,128).sum(axis=0)
        rows.append(jnp.concatenate([d[:RHS],d[RHS:]],axis=1))
    d=exact(jnp.concatenate(rows,axis=0),s2)
    for g in range(n//8): ext[:,pl.ds(pts+g*256,256)]=d[g*RHS:(g+1)*RHS]
    for m in later: m.wait()

def up(x,basis,transfer,upper,chunks=2):
    n=basis.shape[0]
    tra=transfer.reshape(n//8,8,8,128).transpose(0,2,1,3).reshape(n*8,128)
    bas=basis.reshape(n//8,8,16,128).transpose(0,2,1,3).reshape(n*16,128)
    return pl.pallas_call(up_kernel,
        out_shape=(jax.ShapeDtypeStruct((RHS,n*(LEAF+K)),f32),jax.ShapeDtypeStruct(tra.shape,f32),jax.ShapeDtypeStruct(upper.shape,f32)),
        in_specs=[pl.BlockSpec(memory_space=HBM)]*4,
        scratch_shapes=[pltpu.VMEM(x.shape,f32),pltpu.VMEM(bas.shape,f32),pltpu.SemaphoreType.DMA((chunks+1,)),pltpu.SemaphoreType.DMA((2,))],
        compiler_params=pltpu.CompilerParams(vmem_limit_bytes=24<<20),name="up")(in_hbm(x),in_hbm(bas),in_hbm(tra),in_hbm(upper))

def lift_kernel(turn,base,ext,tra,upt,*rest):
    out,fs,rep,sem=rest[-4:]
    @pl.when(base[3]==turn)
    def _():
        nc=upt.shape[0]
        n=tra.shape[0]//8
        per=n//nc
        pts=n*LEAF
        outs=[]
        for u in range(nc):
            e=jnp.concatenate([tra[pl.ds(((u*per+i)//8)*64+(u*per+i)%8,8,stride=8),:] for i in range(per)],axis=1)
            v=[spread4(ext[:,pl.ds(pts+(u*per+i)//4*128,128)],i%4) for i in range(per)]
            outs.append(mul3(jnp.concatenate(v,axis=1),masked4(e)))
        row=iota((128,128),0); col=iota((128,128),1)
        s3=onehot(col==row//32*32+lax.rem(row,8)*4+lax.rem(row,32)//8)
        cc=exact(jnp.concatenate(outs,axis=1),s3)
        for q in range(8):
            fs[pl.ds(q*nc,nc),:]=upt[:,pl.ds(q*128,128)]
        f=jnp.concatenate([fs[pl.ds(u,8,stride=nc),:] for u in range(nc)],axis=1)
        pr=mul3(jnp.concatenate([spread4(cc,u) for u in range(nc)],axis=1),masked4(f))
        pay=[cc[4*i:4*i+4] for i in range(4)]+[jnp.concatenate([pr[4*i:4*i+4] for i in range(4)],axis=1)]
        for c in range(rep.shape[0]):
            for i in range(5): rep[c,i]=pay[i]
        move=pltpu.make_async_copy(rep,out,sem)
        move.start()
        move.wait()

def lift(turn,base,ext,tra,upper,copies,given=None):
    vm=pl.BlockSpec(memory_space=pltpu.VMEM)
    hbm=pl.BlockSpec(memory_space=HBM)
    more=[] if given is None else [given]
    shape=(copies,5,4,128)
    return pl.pallas_call(functools.partial(lift_kernel,turn),
        out_shape=jax.ShapeDtypeStruct(shape,f32),
        in_specs=[pl.BlockSpec(memory_space=pltpu.SMEM)]+[vm]*3+[hbm]*len(more),
        out_specs=hbm,
        input_output_aliases={4:0} if more else {},
        scratch_shapes=[pltpu.VMEM((8*upper.shape[0],128),f32),pltpu.VMEM(shape,f32),pltpu.SemaphoreType.DMA],
        compiler_params=pltpu.CompilerParams(vmem_limit_bytes=24<<20),name="lift")(base,ext,tra,upper,*more)

def far_kernel(base,src_h,cpl_h,cb,co,ca,out,table,cpl,src,sem,sem2):
    n=src.shape[1]
    tiles=n*K//128
    skip=n*LEAF
    chunks=sem.shape[0]
    size=cpl.shape[0]//chunks
    def chunk(c): return pltpu.make_async_copy(cpl_h.at[pl.ds(c*size,size),:],cpl.at[pl.ds(c*size,size),:],sem.at[c])
    idx=pltpu.make_async_copy(src_h,src,sem2.at[0])
    idx.start()
    for c in range(chunks): chunk(c).start()
    for w,ref in ((base[2],cb),(1,co),(2-base[2],ca)):
        def body(q,_):
            t=ref[:,pl.ds(pl.multiple_of(skip+q*128,128),128)]
            for m in range(4): table[(w*tiles+q)*4+m]=jnp.concatenate(split(spread4(t,m)),axis=0)
            return 0
        lax.fori_loop(0,tiles,body,0,unroll=8)
    idx.wait()
    per=n//chunks
    first=base[0]
    block=iota((8,128),1)//K
    block32=iota((2*RHS,128),1)//K
    def pick(where,four):
        return jnp.where(where<2,jnp.where(where<1,four[0],four[1]),jnp.where(where<3,four[2],four[3]))
    def step(c,_):
        chunk(c).wait()
        for i in range(per):
            t=c*per+i
            off=pl.multiple_of(t*64,64)
            cs=[cpl[pl.ds(off+j,8,stride=8),:] for j in range(8)]
            w=[[pick(block,[pltpu.roll(cs[4*h+p],(p-km)%4*K,1) if p!=km else cs[4*h+p] for p in range(4)]) for h in range(2)] for km in range(4)]
            w=jnp.concatenate([jnp.concatenate(v,axis=1) for v in w],axis=0)
            at=[src[j,t]-first for j in range(8)]
            v=jnp.concatenate([pick(block32,[table[at[4*h+p]] for p in range(4)]) for h in range(2)],axis=1)
            d=dotnt(v,jnp.concatenate(split(w),axis=0))
            out[pl.ds(pl.multiple_of(t*RHS,RHS),RHS),:]=d[:RHS]+d[RHS:]
        return 0
    lax.fori_loop(0,chunks,step,0)

def far(base,src,eb,eo,ea,coupling,chunks=2):
    n=coupling.shape[0]
    view=coupling.reshape(n,8,8,128).transpose(0,2,1,3).reshape(n*64,128)
    vm=pl.BlockSpec(memory_space=pltpu.VMEM)
    hbm=pl.BlockSpec(memory_space=HBM)
    return pl.pallas_call(far_kernel,
        out_shape=jax.ShapeDtypeStruct((n*RHS,2*K),f32),
        in_specs=[pl.BlockSpec(memory_space=pltpu.SMEM),hbm,hbm,vm,vm,vm],
        out_specs=vm,
        scratch_shapes=[pltpu.VMEM((3*n,2*RHS,128),bf16),pltpu.VMEM((n*64,128),f32),pltpu.SMEM((8,n),jnp.int32),
            pltpu.SemaphoreType.DMA((chunks,)),pltpu.SemaphoreType.DMA((1,))],
        compiler_params=pltpu.CompilerParams(vmem_limit_bytes=24<<20),name="far")(base,in_hbm(src.T),in_hbm(view),eb,eo,ea)

def gather_kernel(csrc,pays,ccp,out):
    nc=ccp.shape[0]//64
    devs=pays.shape[0]
    for u in range(nc):
        w=jnp.concatenate([ccp[pl.ds(u*64+j,8,stride=8),:] for j in range(8)],axis=1)
        vs=[]
        for j in range(8):
            s=csrc[u,j]
            place=lax.rem(s//nc,2)*(devs//2)+s//(2*nc)
            vs.append(spread4(jnp.concatenate([pays[place,i] for i in range(4)],axis=0),lax.rem(s,nc)))
        out[pl.ds(u*RHS,RHS),:]=mul3(jnp.concatenate(vs,axis=1),masked4(w))

def gather(csrc,pays,ccp):
    nc=ccp.shape[0]
    view=ccp.reshape(nc,8,8,128).transpose(0,2,1,3).reshape(nc*64,128)
    vm=pl.BlockSpec(memory_space=pltpu.VMEM)
    return pl.pallas_call(gather_kernel,
        out_shape=jax.ShapeDtypeStruct((nc*RHS,K),f32),
        in_specs=[pl.BlockSpec(memory_space=pltpu.SMEM),vm,vm],
        cost_estimate=pl.CostEstimate(flops=10**10,bytes_accessed=10**7,transcendentals=0),
        compiler_params=pltpu.CompilerParams(vmem_limit_bytes=24<<20),name="gather")(csrc,pays,view)

def down_kernel(base,s0,s1,s2,s3,cfar,gcp,upt,tra,bas,lf,near_ref,out,gs,fs):
    nc=upt.shape[0]; ng=gcp.shape[0]
    n=lf.shape[0]//RHS
    row=iota((K,128),0); col=lax.rem(iota((K,128),1),K)
    s4=onehot(col==lax.rem(row,8)*4+row//8)
    for q in range(8):
        fs[pl.ds(q*nc,nc),:]=upt[:,pl.ds(q*128,128)]
        gs[pl.ds(q*ng,ng),:]=gcp[:,pl.ds(q*128,128)]
    gv=exact(jnp.concatenate([s[:,i*K:(i+1)*K] for s in (s0,s1,s2,s3) for i in range(4)],axis=0),s4)
    gv=[gv[h*RHS:(h+1)*RHS] for h in range(ng)]
    gw=jnp.concatenate([gs[pl.ds(lax.rem(base[1]+ng-h,ng),8,stride=ng),:] for h in range(ng)],axis=1)
    gf=mul3(jnp.concatenate(gv,axis=1),masked4(gw))
    fw=jnp.concatenate([fs[pl.ds(u,8,stride=nc),:] for u in range(nc)],axis=1)
    wh,wl=masked4(fw)
    gh,gl=split(gf)
    down=dotnn(gh,wh)+dotnn(gl,wh)+dotnn(gh,wl)
    row=lax.rem(iota((128,K),0),K); col=iota((128,K),1)
    s5=onehot(row==lax.rem(col,8)*4+col//8)
    down=jnp.concatenate([down[:,u*128:(u+1)*128] for u in range(nc)],axis=0)
    down=exact(down,s5)
    row=lax.rem(iota((128,256),0),K); col=iota((128,256),1)
    p1=onehot(row==2*(lax.rem(col,128)//8)+col//128)
    row=lax.rem(iota((2*K,256),0),K); col=iota((2*K,256),1)
    nat=2*(lax.rem(col,128)//8)+col//128
    p2=onehot(row==lax.rem(nat,4)*8+nat//4)
    p12=jnp.concatenate([p1,p1,p2,p2],axis=0)
    left=iota((RHS,128),1)<LEAF
    per=n//nc
    ds=[]
    for u in range(nc):
        cf=cfar[pl.ds(u*RHS,RHS),:]+down[u*RHS:(u+1)*RHS]
        e=jnp.concatenate([tra[pl.ds(((u*per+i)//8)*64+(u*per+i)%8,8,stride=8),:] for i in range(per)],axis=1)
        eh,el=masked4(e)
        ch,cl=split(cf)
        d=dotnn(jnp.concatenate([ch,cl,ch],axis=1),jnp.concatenate([eh,eh,el],axis=0))
        ds+=[d[:,i*128:(i+1)*128] for i in range(per)]
    q=dotnn(jnp.concatenate([*split(jnp.concatenate(ds,axis=0)),*split(lf[...])],axis=1),p12)
    same=(iota((256,128),0)//32==lax.rem(iota((256,128),1),8))
    for g in range(n//8):
        z=q[g*128:(g+1)*128].reshape(8,RHS,256)
        z=jnp.stack([z[:,:,:128],z[:,:,128:]],axis=1).reshape(256,128)
        zh,zl=split(jnp.where(same,z,0.0))
        bh,bl=split(bas[pl.ds(g*128,128),:])
        o=dotnn(jnp.concatenate([zh,zl],axis=1),jnp.concatenate([jnp.concatenate([bh,bl],axis=1),jnp.concatenate([bh,jnp.zeros_like(bl)],axis=1)],axis=0))
        o=(o[:,:128]+o[:,128:]).reshape(8,2,RHS,128)
        for m in range(4):
            a=jnp.where(left,o[2*m,0],o[2*m,1])
            c=jnp.where(left,o[2*m+1,0],o[2*m+1,1])
            r=jnp.where(left,a,c)+pltpu.roll(jnp.where(left,c,a),LEAF,1)
            at=pl.ds(g*512+m*128,128)
            out[:,at]=near_ref[:,at]+r

def down(base,sums,cfar,gcp,upper,tra,basis,lf,nearv):
    n=basis.shape[0]; nc=upper.shape[0]; ng=gcp.shape[0]
    bas=basis.reshape(n//8,8,16,128).transpose(0,2,1,3).reshape(n*16,128)
    vm=pl.BlockSpec(memory_space=pltpu.VMEM)
    return pl.pallas_call(down_kernel,
        out_shape=jax.ShapeDtypeStruct((RHS,n*LEAF),f32),
        in_specs=[pl.BlockSpec(memory_space=pltpu.SMEM)]+[vm]*11,
        scratch_shapes=[pltpu.VMEM((8*ng,128),f32),pltpu.VMEM((8*nc,128),f32)],
        compiler_params=pltpu.CompilerParams(vmem_limit_bytes=24<<20),name="down")(base,*sums,cfar,gcp,upper,tra,bas,lf,nearv)

def across(devs):
    return [[2*i+c for i in range(devs//2)] for c in range(2)]

def per_device(right_sides,near_blocks,near_source,near_count,basis,leaf_source,leaf_coupling,leaf_transfer,cluster_source,cluster_coupling,cluster_transfer,group_coupling):
    both=("group","leaf")
    leaves=near_blocks.shape[0]
    devs=lax.axis_size("leaf")
    every=lax.axis_size(both)
    ng=lax.axis_size("group")
    base=jnp.stack([(lax.axis_index(both)-1)*leaves,lax.axis_index("group"),2*lax.rem(lax.axis_index("leaf")+1,2),lax.axis_index("leaf")//(devs-1)]).astype(jnp.int32)
    ext,tra,upper=up(right_sides,basis,leaf_transfer,cluster_transfer)
    eb=lax.ppermute(ext,both,[(i,i^1) for i in range(every)])
    rep=lift(0,base,ext,tra,upper,devs//2)
    ext2,rep=lax.optimization_barrier((ext,rep))
    ea=lax.ppermute(ext2,both,[p for i in range(1,every-1,2) for p in ((i,i+1),(i+1,i))])
    rep=lift(1,base,ext,tra,upper,devs//2,rep)
    some=lax.all_to_all(rep,"leaf",0,0,tiled=True,axis_index_groups=across(devs))
    nearv=near(base,near_source,near_count,eb,ext,ea,near_blocks)
    lf=far(base,leaf_source,eb,ext,ea,leaf_coupling)
    some,nearv,lf=lax.optimization_barrier((some,nearv,lf))
    pays=lax.all_gather(some,"leaf",axis=0,tiled=True,axis_index_groups=[[2*i,2*i+1] for i in range(devs//2)])
    total=pays[:,4].sum(axis=0)
    sums=[total]+[lax.ppermute(total,"group",[(i,(i+k)%ng) for i in range(ng)]) for k in range(1,ng)]
    cfar=gather(cluster_source,pays,cluster_coupling)
    return down(base,sums,cfar,group_coupling.reshape(-1,1024),upper,tra,basis,lf,nearv)

def solution(mesh):
    both=("group","leaf")
    one=P(both)
    two=P(both,None)
    three=P(both,None,None)
    return jax.shard_map(per_device,mesh=mesh,
        in_specs=(P(None,both),three,two,one,two,two,three,two,two,three,two,P("group",None,None)),
        out_specs=P(None,both),check_vma=False)
```

```python
import functools

import jax
import jax.numpy as jnp
from jax import lax
from jax.experimental import pallas as pl
from jax.experimental.pallas import tpu as pltpu
from jax.sharding import PartitionSpec as P

LEAF=64;K=32;RHS=16
f32=jnp.float32; bf16=jnp.bfloat16
NT=(((1,),(1,)),((),()))
def split(a):
    h=a.astype(bf16)
    return h,(a-h.astype(f32)).astype(bf16)
def dotnt(a,b): return lax.dot_general(a,b,NT,preferred_element_type=f32)
def dotnn(a,b): return lax.dot_general(a,b,(((1,),(0,)),((),())),preferred_element_type=f32)

HBM=pltpu.HBM
def in_hbm(v): return pltpu.with_memory_space_constraint(v,HBM)

def point_table(x_ref, first, leaves, hi, lo):
    left=lax.broadcasted_iota(jnp.int32,(RHS,128),1)<LEAF
    def body(q,_):
        x=x_ref[:,pl.ds(pl.multiple_of(q*128,128),128)]
        y=pltpu.roll(x,LEAF,1)
        for n,(a,b) in enumerate(((x,y),(y,x))):
            h,l=split(jnp.where(left,a,b))
            hi[first+2*q+n]=h
            lo[first+2*q+n]=l
        return 0
    lax.fori_loop(0,leaves//2,body,0,unroll=4)

def near_kernel(base, src_h, cnt_h, nb_h, xb, xo, xa, out, hi, lo, weave, acc, nb, src, cnt, sem, sem2):
    n=out.shape[1]//LEAF
    chunks=sem.shape[0]
    size=nb.shape[0]//chunks
    def chunk(c): return pltpu.make_async_copy(nb_h.at[pl.ds(c*size,size),:],nb.at[pl.ds(c*size,size),:],sem.at[c])
    ca=pltpu.make_async_copy(src_h,src,sem2.at[0]); cb=pltpu.make_async_copy(cnt_h,cnt,sem2.at[1])
    ca.start(); cb.start()
    for c in range(chunks): chunk(c).start()
    point_table(xo,n,n,hi,lo)
    point_table(xb,base[2]*n,n,hi,lo)
    point_table(xa,(2-base[2])*n,n,hi,lo)
    hi[3*n]=jnp.zeros((RHS,128),bf16)
    lo[3*n]=jnp.zeros((RHS,128),bf16)
    row=lax.broadcasted_iota(jnp.int32,(256,128),0)
    col=lax.broadcasted_iota(jnp.int32,(256,128),1)
    a=lax.rem(col,64)
    weave[...]=((row//128==col//64)&(lax.rem(row,64)==lax.rem(a,2)*32+a//2)).astype(f32).astype(bf16)
    ca.wait(); cb.wait()
    per=n//chunks
    first=base[0]
    left=lax.broadcasted_iota(jnp.int32,(RHS,128),1)<LEAF
    left32=lax.broadcasted_iota(jnp.int32,(32,128),1)<LEAF
    def join(table,at): return jnp.concatenate([jnp.where(left,table[at[2*p]],table[at[2*p+1]]) for p in range(4)],axis=1)
    def step(c,_):
        chunk(c).wait()
        for pair in range(per//2):
            for m in range(2):
                t=c*per+pair*2+m
                off=pl.multiple_of(t*256,256)
                even=[];odd=[]
                for p in range(4):
                    a=nb[pl.ds(off+2*p,32,stride=8),:]
                    b=nb[pl.ds(off+2*p+1,32,stride=8),:]
                    even.append(jnp.where(left32,a,pltpu.roll(b,LEAF,1)))
                    odd.append(jnp.where(left32,pltpu.roll(a,LEAF,1),b))
                w=jnp.concatenate([jnp.concatenate(even,axis=1),jnp.concatenate(odd,axis=1)],axis=0)
                live=cnt[t]
                at=[jnp.where(j<live,src[j,t]-first,3*n) for j in range(8)]
                d=dotnt(jnp.concatenate([join(hi,at),join(lo,at)],axis=0),jnp.concatenate(split(w),axis=0))
                acc[pl.ds(pl.multiple_of((c*per+pair*2)*(RHS//2),RHS),RHS),m*128:(m+1)*128]=d[:RHS]+d[RHS:]
        return 0
    lax.fori_loop(0,chunks,step,0)
    d=dotnn(jnp.concatenate(split(acc[...]),axis=0),weave[...])
    d=d[:n*RHS//2]+d[n*RHS//2:]
    for q in range(n//2): out[:,q*128:(q+1)*128]=d[q*RHS:(q+1)*RHS]

def near(base,src,cnt,xb,xo,xa,nb,chunks=4):
    leaves=nb.shape[0]
    view=nb.reshape(leaves,8,32,128).transpose(0,2,1,3).reshape(leaves*256,128)
    hbm=pl.BlockSpec(memory_space=HBM)
    vm=pl.BlockSpec(memory_space=pltpu.VMEM)
    return pl.pallas_call(near_kernel,
        out_shape=jax.ShapeDtypeStruct((RHS,leaves*LEAF),f32),
        in_specs=[pl.BlockSpec(memory_space=pltpu.SMEM),hbm,hbm,hbm,vm,vm,vm],
        out_specs=vm,
        scratch_shapes=[pltpu.VMEM((3*leaves+1,RHS,128),bf16)]*2+[pltpu.VMEM((256,128),bf16),pltpu.VMEM((leaves//2*RHS,256),f32),pltpu.VMEM((leaves*256,128),f32),
            pltpu.SMEM((8,leaves),jnp.int32),pltpu.SMEM((leaves,),jnp.int32),pltpu.SemaphoreType.DMA((chunks,)),pltpu.SemaphoreType.DMA((2,))],
        cost_estimate=pl.CostEstimate(flops=10**11,bytes_accessed=10**7,transcendentals=0),
        compiler_params=pltpu.CompilerParams(vmem_limit_bytes=24<<20),
        name="near")(base,in_hbm(src.T),in_hbm(cnt),in_hbm(view),xb,xo,xa)

def iota(shape,d): return lax.broadcasted_iota(jnp.int32,shape,d)
def onehot(cond): return cond.astype(f32).astype(bf16)
def exact(v,m):
    d=dotnn(jnp.concatenate(split(v),axis=0),m)
    return d[:v.shape[0]]+d[v.shape[0]:]
def wide(v,w):
    d=dotnt(jnp.concatenate(split(v),axis=0),jnp.concatenate(w,axis=0))
    return d[:RHS]+d[RHS:]
def spread4(tile,m):
    block=jnp.where(iota(tile.shape,1)//K==m,tile,0.0)
    block=block+pltpu.roll(block,64,1)
    return block+pltpu.roll(block,32,1)
def masked4(rows):
    n=rows.shape[1]//128
    lane=iota((16,128),1)//K
    half=iota((16,128),0)//8
    keep=[onehot(lane==half+2*p) for p in range(2)]
    h=rows.astype(bf16).astype(f32)
    out=[]
    for v in (h,rows-h):
        w=jnp.concatenate([v,v],axis=0).astype(bf16)
        out.append(jnp.concatenate([w*jnp.concatenate([m]*n,axis=1) for m in keep],axis=0))
    return out

def pick(where,four):
    return jnp.where(where<2,jnp.where(where<1,four[0],four[1]),jnp.where(where<3,four[2],four[3]))
def join4(four):
    block=iota((8,128),1)//K
    return jnp.concatenate([pick(block,[pltpu.roll(c,(p-km)%4*K,1) if p!=km else c for p,c in enumerate(four)]) for km in range(4)],axis=0)
def natural():
    row=iota((128,128),0); col=iota((128,128),1)
    return onehot(col==row//32*32+lax.rem(row,8)*4+lax.rem(row,32)//8)

def mul3(v,w):
    d=wide(v,w)
    n=w[0].shape[0]
    return d[:,:n]+d[:,n:]

def up_kernel(x_h,bas_h,tra_h,upt_h,ext,tra,upt,x,bas,sem,sem2):
    chunks=sem.shape[0]-1
    size=bas.shape[0]//chunks
    first=pltpu.make_async_copy(x_h,x,sem.at[chunks])
    moves=[pltpu.make_async_copy(bas_h.at[pl.ds(c*size,size),:],bas.at[pl.ds(c*size,size),:],sem.at[c]) for c in range(chunks)]
    later=[pltpu.make_async_copy(tra_h,tra,sem2.at[0]),pltpu.make_async_copy(upt_h,upt,sem2.at[1])]
    first.start()
    for m in moves+later: m.start()
    pts=x.shape[1]
    n=pts//LEAF
    left=iota((RHS,128),1)<LEAF
    row=iota((256,256),0); col=iota((256,256),1)
    k2=lax.rem(row,128)//8
    s2=onehot(col==lax.rem(row,8)*32+2*k2+row//128)
    same=(iota((256,128),0)//32==lax.rem(iota((256,128),1),8))
    first.wait()
    ext[:,:pts]=x[...]
    rows=[]
    for g in range(n//8):
        if g*128%size==0: moves[g*128//size].wait()
        blks=[]
        for q in range(4):
            t=x[:,pl.ds((g*4+q)*128,128)]
            y=pltpu.roll(t,LEAF,1)
            for a,b in ((t,y),(y,t)):
                blks+= [jnp.where(left,a,0.0),jnp.where(left,0.0,b)]
        xh,xl=split(jnp.concatenate(blks,axis=0))
        bh,bl=split(bas[pl.ds(g*128,128),:])
        d=dotnt(jnp.concatenate([xh,xl],axis=1),jnp.concatenate([jnp.concatenate([bh,bh],axis=1),jnp.concatenate([bl,jnp.zeros_like(bl)],axis=1)],axis=0))
        d=jnp.where(same,d[:,:128]+d[:,128:],0.0).reshape(8,32,128).sum(axis=0)
        rows.append(jnp.concatenate([d[:RHS],d[RHS:]],axis=1))
    d=exact(jnp.concatenate(rows,axis=0),s2)
    for g in range(n//8): ext[:,pl.ds(pts+g*256,256)]=d[g*RHS:(g+1)*RHS]
    for m in later: m.wait()

def up(x,basis,transfer,upper,chunks=2):
    n=basis.shape[0]
    tra=transfer.reshape(n//8,8,8,128).transpose(0,2,1,3).reshape(n*8,128)
    bas=basis.reshape(n//8,8,16,128).transpose(0,2,1,3).reshape(n*16,128)
    return pl.pallas_call(up_kernel,
        out_shape=(jax.ShapeDtypeStruct((RHS,n*(LEAF+K)),f32),jax.ShapeDtypeStruct(tra.shape,f32),jax.ShapeDtypeStruct(upper.shape,f32)),
        in_specs=[pl.BlockSpec(memory_space=HBM)]*4,
        scratch_shapes=[pltpu.VMEM(x.shape,f32),pltpu.VMEM(bas.shape,f32),pltpu.SemaphoreType.DMA((chunks+1,)),pltpu.SemaphoreType.DMA((2,))],
        compiler_params=pltpu.CompilerParams(vmem_limit_bytes=24<<20),name="up")(in_hbm(x),in_hbm(bas),in_hbm(tra),in_hbm(upper))

def lift_kernel(ext,tra,upt,rep,ejh,ejl,fs):
    nc=upt.shape[0]
    n=tra.shape[0]//8
    per=n//nc
    pts=n*LEAF
    outs=[]
    for u in range(nc):
        es=[tra[pl.ds(((u*per+i)//8)*64+(u*per+i)%8,8,stride=8),:] for i in range(per)]
        w=split(jnp.concatenate([join4(es[i:i+4]) for i in range(0,per,4)],axis=1))
        ejh[pl.ds(u*K,K),:]=w[0]
        ejl[pl.ds(u*K,K),:]=w[1]
        outs.append(mul3(ext[:,pl.ds(pts+u*per*K,per*K)],w))
    cc=exact(jnp.concatenate(outs,axis=1),natural())
    for q in range(8):
        fs[pl.ds(q*nc,nc),:]=upt[:,pl.ds(q*128,128)]
    pr=mul3(cc,split(join4([fs[pl.ds(u,8,stride=nc),:] for u in range(nc)])))
    pay=[cc[4*i:4*i+4] for i in range(4)]+[jnp.concatenate([pr[4*i:4*i+4] for i in range(4)],axis=1)]
    for c in range(rep.shape[0]):
        for i in range(5): rep[c,i]=pay[i]

def lift(ext,tra,upper,copies):
    vm=pl.BlockSpec(memory_space=pltpu.VMEM)
    nc=upper.shape[0]
    join=jax.ShapeDtypeStruct((nc*K,tra.shape[0]//8//nc*K),bf16)
    return pl.pallas_call(lift_kernel,
        out_shape=(jax.ShapeDtypeStruct((copies,5,4,128),f32),join,join),
        in_specs=[vm]*3,out_specs=(vm,)*3,
        scratch_shapes=[pltpu.VMEM((8*nc,128),f32)],
        compiler_params=pltpu.CompilerParams(vmem_limit_bytes=24<<20),name="lift")(ext,tra,upper)

def far_kernel(base,src_h,cpl_h,cb,co,ca,out,table,cpl,src,sem,sem2):
    n=src.shape[1]
    tiles=n*K//128
    skip=n*LEAF
    chunks=sem.shape[0]
    size=cpl.shape[0]//chunks
    def chunk(c): return pltpu.make_async_copy(cpl_h.at[pl.ds(c*size,size),:],cpl.at[pl.ds(c*size,size),:],sem.at[c])
    idx=pltpu.make_async_copy(src_h,src,sem2.at[0])
    idx.start()
    for c in range(chunks): chunk(c).start()
    for w,ref in ((base[2],cb),(1,co),(2-base[2],ca)):
        def body(q,_):
            t=ref[:,pl.ds(pl.multiple_of(skip+q*128,128),128)]
            for m in range(4): table[(w*tiles+q)*4+m]=jnp.concatenate(split(spread4(t,m)),axis=0)
            return 0
        lax.fori_loop(0,tiles,body,0,unroll=8)
    idx.wait()
    per=n//chunks
    first=base[0]
    block32=iota((2*RHS,128),1)//K
    def step(c,_):
        chunk(c).wait()
        for i in range(per):
            t=c*per+i
            off=pl.multiple_of(t*64,64)
            cs=[cpl[pl.ds(off+j,8,stride=8),:] for j in range(8)]
            w=jnp.concatenate([join4(cs[:4]),join4(cs[4:])],axis=1)
            at=[src[j,t]-first for j in range(8)]
            v=jnp.concatenate([pick(block32,[table[at[4*h+p]] for p in range(4)]) for h in range(2)],axis=1)
            d=dotnt(v,jnp.concatenate(split(w),axis=0))
            out[pl.ds(pl.multiple_of(t*RHS,RHS),RHS),:]=d[:RHS]+d[RHS:]
        return 0
    lax.fori_loop(0,chunks,step,0)

def far(base,src,eb,eo,ea,coupling,chunks=2):
    n=coupling.shape[0]
    view=coupling.reshape(n,8,8,128).transpose(0,2,1,3).reshape(n*64,128)
    vm=pl.BlockSpec(memory_space=pltpu.VMEM)
    hbm=pl.BlockSpec(memory_space=HBM)
    return pl.pallas_call(far_kernel,
        out_shape=jax.ShapeDtypeStruct((n*RHS,2*K),f32),
        in_specs=[pl.BlockSpec(memory_space=pltpu.SMEM),hbm,hbm,vm,vm,vm],
        out_specs=vm,
        scratch_shapes=[pltpu.VMEM((3*n,2*RHS,128),bf16),pltpu.VMEM((n*64,128),f32),pltpu.SMEM((8,n),jnp.int32),
            pltpu.SemaphoreType.DMA((chunks,)),pltpu.SemaphoreType.DMA((1,))],
        compiler_params=pltpu.CompilerParams(vmem_limit_bytes=24<<20),name="far")(base,in_hbm(src.T),in_hbm(view),eb,eo,ea)

def gather_kernel(csrc,pays,ccp,out):
    nc=ccp.shape[0]//64
    devs=pays.shape[0]
    block=iota((RHS,128),1)//K
    for u in range(nc):
        cs=[ccp[pl.ds(u*64+j,8,stride=8),:] for j in range(8)]
        vs=[]
        for j in range(8):
            s=csrc[u,j]
            place=lax.rem(s//nc,2)*(devs//2)+s//(2*nc)
            v=jnp.concatenate([pays[place,i] for i in range(4)],axis=0)
            vs.append(pltpu.roll(v,lax.rem(nc+j%4-lax.rem(s,nc),nc)*K,1))
        v=jnp.concatenate([pick(block,vs[:4]),pick(block,vs[4:])],axis=1)
        out[pl.ds(u*RHS,RHS),:]=mul3(v,split(jnp.concatenate([join4(cs[:4]),join4(cs[4:])],axis=1)))

def gather(csrc,pays,ccp):
    nc=ccp.shape[0]
    view=ccp.reshape(nc,8,8,128).transpose(0,2,1,3).reshape(nc*64,128)
    vm=pl.BlockSpec(memory_space=pltpu.VMEM)
    return pl.pallas_call(gather_kernel,
        out_shape=jax.ShapeDtypeStruct((nc*RHS,K),f32),
        in_specs=[pl.BlockSpec(memory_space=pltpu.SMEM),vm,vm],
        cost_estimate=pl.CostEstimate(flops=10**10,bytes_accessed=10**7,transcendentals=0),
        compiler_params=pltpu.CompilerParams(vmem_limit_bytes=24<<20),name="gather")(csrc,pays,view)

def down_kernel(base,s0,s1,s2,s3,cfar,gcp,upt,ejh,ejl,bas,lf,near_ref,out,gs,fs):
    nc=upt.shape[0]; ng=gcp.shape[0]
    n=lf.shape[0]//RHS
    for q in range(8):
        fs[pl.ds(q*nc,nc),:]=upt[:,pl.ds(q*128,128)]
        gs[pl.ds(q*ng,ng),:]=gcp[:,pl.ds(q*128,128)]
    gv=jnp.concatenate([jnp.concatenate([s[:,i*K:(i+1)*K] for i in range(4)],axis=0) for s in (s0,s1,s2,s3)],axis=1)
    gw=join4([gs[pl.ds(lax.rem(base[1]+ng-h,ng),8,stride=ng),:] for h in range(ng)])
    gf=mul3(exact(gv,natural()),split(gw))
    wh,wl=split(join4([fs[pl.ds(u,8,stride=nc),:] for u in range(nc)]))
    gh,gl=split(gf)
    down=dotnn(jnp.concatenate([gh,gl,gh],axis=1),jnp.concatenate([wh,wh,wl],axis=0))
    row=iota((128,128),0); col=iota((128,128),1)
    down=exact(down,onehot(col==row//32*32+lax.rem(row,4)*8+lax.rem(row,32)//4))
    row=lax.rem(iota((128,256),0),K); col=iota((128,256),1)
    p1=onehot(row==2*(lax.rem(col,128)//8)+col//128)
    row=lax.rem(iota((2*K,256),0),K); col=iota((2*K,256),1)
    nat=2*(lax.rem(col,128)//8)+col//128
    p2=onehot(row==lax.rem(nat,4)*8+nat//4)
    p12=jnp.concatenate([p1,p1,p2,p2],axis=0)
    left=iota((RHS,128),1)<LEAF
    per=n//nc
    ds=[]
    block=iota((RHS,128),1)//K
    for u in range(nc):
        cf=cfar[pl.ds(u*RHS,RHS),:]+down[:,u*K:(u+1)*K]
        ch,cl=split(cf)
        eh=ejh[pl.ds(u*K,K),:]
        d=dotnn(jnp.concatenate([ch,cl,ch],axis=1),jnp.concatenate([eh,eh,ejl[pl.ds(u*K,K),:]],axis=0))
        ds+=[jnp.where(block==i%4,d[:,i//4*128:i//4*128+128],0.0) for i in range(per)]
    q=dotnn(jnp.concatenate([*split(jnp.concatenate(ds,axis=0)),*split(lf[...])],axis=1),p12)
    same=(iota((256,128),0)//32==lax.rem(iota((256,128),1),8))
    for g in range(n//8):
        z=q[g*128:(g+1)*128].reshape(8,RHS,256)
        z=jnp.stack([z[:,:,:128],z[:,:,128:]],axis=1).reshape(256,128)
        zh,zl=split(jnp.where(same,z,0.0))
        bh,bl=split(bas[pl.ds(g*128,128),:])
        o=dotnn(jnp.concatenate([zh,zl],axis=1),jnp.concatenate([jnp.concatenate([bh,bl],axis=1),jnp.concatenate([bh,jnp.zeros_like(bl)],axis=1)],axis=0))
        o=(o[:,:128]+o[:,128:]).reshape(8,2,RHS,128)
        for m in range(4):
            a=jnp.where(left,o[2*m,0],o[2*m,1])
            c=jnp.where(left,o[2*m+1,0],o[2*m+1,1])
            r=jnp.where(left,a,c)+pltpu.roll(jnp.where(left,c,a),LEAF,1)
            at=pl.ds(g*512+m*128,128)
            out[:,at]=near_ref[:,at]+r

def down(base,sums,cfar,gcp,upper,ejh,ejl,basis,lf,nearv):
    n=basis.shape[0]; nc=upper.shape[0]; ng=gcp.shape[0]
    bas=basis.reshape(n//8,8,16,128).transpose(0,2,1,3).reshape(n*16,128)
    vm=pl.BlockSpec(memory_space=pltpu.VMEM)
    return pl.pallas_call(down_kernel,
        out_shape=jax.ShapeDtypeStruct((RHS,n*LEAF),f32),
        in_specs=[pl.BlockSpec(memory_space=pltpu.SMEM)]+[vm]*12,
        scratch_shapes=[pltpu.VMEM((8*ng,128),f32),pltpu.VMEM((8*nc,128),f32)],
        compiler_params=pltpu.CompilerParams(vmem_limit_bytes=24<<20),name="down")(base,*sums,cfar,gcp,upper,ejh,ejl,bas,lf,nearv)

def across(devs):
    return [[2*i+c for i in range(devs//2)] for c in range(2)]

def per_device(right_sides,near_blocks,near_source,near_count,basis,leaf_source,leaf_coupling,leaf_transfer,cluster_source,cluster_coupling,cluster_transfer,group_coupling):
    both=("group","leaf")
    leaves=near_blocks.shape[0]
    devs=lax.axis_size("leaf")
    every=lax.axis_size(both)
    ng=lax.axis_size("group")
    base=jnp.stack([(lax.axis_index(both)-1)*leaves,lax.axis_index("group"),2*lax.rem(lax.axis_index("leaf")+1,2)]).astype(jnp.int32)
    ext,tra,upper=up(right_sides,basis,leaf_transfer,cluster_transfer)
    eb=lax.ppermute(ext,both,[(i,i^1) for i in range(every)])
    ea=lax.ppermute(ext,both,[p for i in range(1,every-1,2) for p in ((i,i+1),(i+1,i))])
    rep,ejh,ejl=lift(ext,tra,upper,devs//2)
    some=lax.all_to_all(rep,"leaf",0,0,tiled=True,axis_index_groups=across(devs))
    nearv=near(base,near_source,near_count,eb,ext,ea,near_blocks)
    lf=far(base,leaf_source,eb,ext,ea,leaf_coupling)
    some,nearv,lf=lax.optimization_barrier((some,nearv,lf))
    pays=lax.all_gather(some,"leaf",axis=0,tiled=True,axis_index_groups=[[2*i,2*i+1] for i in range(devs//2)])
    total=pays[:,4].sum(axis=0)
    sums=[total]+[lax.ppermute(total,"group",[(i,(i+k)%ng) for i in range(ng)]) for k in range(1,ng)]
    cfar=gather(cluster_source,pays,cluster_coupling)
    return down(base,sums,cfar,group_coupling.reshape(-1,1024),upper,ejh,ejl,basis,lf,nearv)

def solution(mesh):
    both=("group","leaf")
    one=P(both)
    two=P(both,None)
    three=P(both,None,None)
    return jax.shard_map(per_device,mesh=mesh,
        in_specs=(P(None,both),three,two,one,two,two,three,two,two,three,two,P("group",None,None)),
        out_specs=P(None,both),check_vma=False)
```

```python
import functools

import jax
import jax.numpy as jnp
from jax import lax
from jax.experimental import pallas as pl
from jax.experimental.pallas import tpu as pltpu
from jax.sharding import PartitionSpec as P

LEAF=64;K=32;RHS=16
f32=jnp.float32; bf16=jnp.bfloat16
NT=(((1,),(1,)),((),()))
def split(a):
    h=a.astype(bf16)
    return h,(a-h.astype(f32)).astype(bf16)
def dotnt(a,b): return lax.dot_general(a,b,NT,preferred_element_type=f32)
def dotnn(a,b): return lax.dot_general(a,b,(((1,),(0,)),((),())),preferred_element_type=f32)

HBM=pltpu.HBM
def in_hbm(v): return pltpu.with_memory_space_constraint(v,HBM)

def point_table(x_ref, first, leaves, hi, lo):
    left=lax.broadcasted_iota(jnp.int32,(RHS,128),1)<LEAF
    def body(q,_):
        x=x_ref[:,pl.ds(pl.multiple_of(q*128,128),128)]
        y=pltpu.roll(x,LEAF,1)
        for n,(a,b) in enumerate(((x,y),(y,x))):
            h,l=split(jnp.where(left,a,b))
            hi[first+2*q+n]=h
            lo[first+2*q+n]=l
        return 0
    lax.fori_loop(0,leaves//2,body,0,unroll=4)

def near_kernel(base, src_h, cnt_h, nb_h, xb, xo, xa, out, hi, lo, weave, acc, nb, src, cnt, sem, sem2):
    n=out.shape[1]//LEAF
    chunks=sem.shape[0]
    size=nb.shape[0]//chunks
    def chunk(c): return pltpu.make_async_copy(nb_h.at[pl.ds(c*size,size),:],nb.at[pl.ds(c*size,size),:],sem.at[c])
    ca=pltpu.make_async_copy(src_h,src,sem2.at[0]); cb=pltpu.make_async_copy(cnt_h,cnt,sem2.at[1])
    ca.start(); cb.start()
    for c in range(chunks): chunk(c).start()
    point_table(xo,n,n,hi,lo)
    point_table(xb,base[2]*n,n,hi,lo)
    point_table(xa,(2-base[2])*n,n,hi,lo)
    hi[3*n]=jnp.zeros((RHS,128),bf16)
    lo[3*n]=jnp.zeros((RHS,128),bf16)
    row=lax.broadcasted_iota(jnp.int32,(256,128),0)
    col=lax.broadcasted_iota(jnp.int32,(256,128),1)
    a=lax.rem(col,64)
    weave[...]=((row//128==col//64)&(lax.rem(row,64)==lax.rem(a,2)*32+a//2)).astype(f32).astype(bf16)
    ca.wait(); cb.wait()
    per=n//chunks
    first=base[0]
    left=lax.broadcasted_iota(jnp.int32,(RHS,128),1)<LEAF
    left32=lax.broadcasted_iota(jnp.int32,(32,128),1)<LEAF
    def join(table,at): return jnp.concatenate([jnp.where(left,table[at[2*p]],table[at[2*p+1]]) for p in range(4)],axis=1)
    def step(c,_):
        chunk(c).wait()
        for pair in range(per//2):
            for m in range(2):
                t=c*per+pair*2+m
                off=pl.multiple_of(t*256,256)
                even=[];odd=[]
                for p in range(4):
                    a=nb[pl.ds(off+2*p,32,stride=8),:]
                    b=nb[pl.ds(off+2*p+1,32,stride=8),:]
                    even.append(jnp.where(left32,a,pltpu.roll(b,LEAF,1)))
                    odd.append(jnp.where(left32,pltpu.roll(a,LEAF,1),b))
                w=jnp.concatenate([jnp.concatenate(even,axis=1),jnp.concatenate(odd,axis=1)],axis=0)
                live=cnt[t]
                at=[jnp.where(j<live,src[j,t]-first,3*n) for j in range(8)]
                d=dotnt(jnp.concatenate([join(hi,at),join(lo,at)],axis=0),jnp.concatenate(split(w),axis=0))
                acc[pl.ds(pl.multiple_of((c*per+pair*2)*(RHS//2),RHS),RHS),m*128:(m+1)*128]=d[:RHS]+d[RHS:]
        return 0
    lax.fori_loop(0,chunks,step,0)
    d=dotnn(jnp.concatenate(split(acc[...]),axis=0),weave[...])
    d=d[:n*RHS//2]+d[n*RHS//2:]
    for q in range(n//2): out[:,q*128:(q+1)*128]=d[q*RHS:(q+1)*RHS]

def near(base,src,cnt,xb,xo,xa,nb,chunks=4):
    leaves=nb.shape[0]
    view=nb.reshape(leaves,8,32,128).transpose(0,2,1,3).reshape(leaves*256,128)
    hbm=pl.BlockSpec(memory_space=HBM)
    vm=pl.BlockSpec(memory_space=pltpu.VMEM)
    return pl.pallas_call(near_kernel,
        out_shape=jax.ShapeDtypeStruct((RHS,leaves*LEAF),f32),
        in_specs=[pl.BlockSpec(memory_space=pltpu.SMEM),hbm,hbm,hbm,vm,vm,vm],
        out_specs=vm,
        scratch_shapes=[pltpu.VMEM((3*leaves+1,RHS,128),bf16)]*2+[pltpu.VMEM((256,128),bf16),pltpu.VMEM((leaves//2*RHS,256),f32),pltpu.VMEM((leaves*256,128),f32),
            pltpu.SMEM((8,leaves),jnp.int32),pltpu.SMEM((leaves,),jnp.int32),pltpu.SemaphoreType.DMA((chunks,)),pltpu.SemaphoreType.DMA((2,))],
        cost_estimate=pl.CostEstimate(flops=10**11,bytes_accessed=10**7,transcendentals=0),
        compiler_params=pltpu.CompilerParams(vmem_limit_bytes=24<<20),
        name="near")(base,in_hbm(src.T),in_hbm(cnt),in_hbm(view),xb,xo,xa)

def iota(shape,d): return lax.broadcasted_iota(jnp.int32,shape,d)
def onehot(cond): return cond.astype(f32).astype(bf16)
def exact(v,m):
    d=dotnn(jnp.concatenate(split(v),axis=0),m)
    return d[:v.shape[0]]+d[v.shape[0]:]
def wide(v,w):
    d=dotnt(jnp.concatenate(split(v),axis=0),jnp.concatenate(w,axis=0))
    return d[:RHS]+d[RHS:]
def spread4(tile,m):
    block=jnp.where(iota(tile.shape,1)//K==m,tile,0.0)
    block=block+pltpu.roll(block,64,1)
    return block+pltpu.roll(block,32,1)
def masked4(rows):
    n=rows.shape[1]//128
    lane=iota((16,128),1)//K
    half=iota((16,128),0)//8
    keep=[onehot(lane==half+2*p) for p in range(2)]
    h=rows.astype(bf16).astype(f32)
    out=[]
    for v in (h,rows-h):
        w=jnp.concatenate([v,v],axis=0).astype(bf16)
        out.append(jnp.concatenate([w*jnp.concatenate([m]*n,axis=1) for m in keep],axis=0))
    return out

def pick(where,four):
    return jnp.where(where<2,jnp.where(where<1,four[0],four[1]),jnp.where(where<3,four[2],four[3]))
def join4(four):
    block=iota((8,128),1)//K
    return jnp.concatenate([pick(block,[pltpu.roll(c,(p-km)%4*K,1) if p!=km else c for p,c in enumerate(four)]) for km in range(4)],axis=0)
def natural():
    row=iota((128,128),0); col=iota((128,128),1)
    return onehot(col==row//32*32+lax.rem(row,8)*4+lax.rem(row,32)//8)

def mul3(v,w):
    d=wide(v,w)
    n=w[0].shape[0]
    return d[:,:n]+d[:,n:]

def up_kernel(x_h,bas_h,tra_h,upt_h,ext,tra,upt,x,bas,sem,sem2):
    chunks=sem.shape[0]-1
    size=bas.shape[0]//chunks
    first=pltpu.make_async_copy(x_h,x,sem.at[chunks])
    moves=[pltpu.make_async_copy(bas_h.at[pl.ds(c*size,size),:],bas.at[pl.ds(c*size,size),:],sem.at[c]) for c in range(chunks)]
    later=[pltpu.make_async_copy(tra_h,tra,sem2.at[0]),pltpu.make_async_copy(upt_h,upt,sem2.at[1])]
    first.start()
    for m in moves+later: m.start()
    pts=x.shape[1]
    n=pts//LEAF
    left=iota((RHS,128),1)<LEAF
    row=iota((256,256),0); col=iota((256,256),1)
    k2=lax.rem(row,128)//8
    s2=onehot(col==lax.rem(row,8)*32+2*k2+row//128)
    same=(iota((256,128),0)//32==lax.rem(iota((256,128),1),8))
    first.wait()
    ext[:,:pts]=x[...]
    rows=[]
    for g in range(n//8):
        if g*128%size==0: moves[g*128//size].wait()
        blks=[]
        for q in range(4):
            t=x[:,pl.ds((g*4+q)*128,128)]
            y=pltpu.roll(t,LEAF,1)
            for a,b in ((t,y),(y,t)):
                blks+= [jnp.where(left,a,0.0),jnp.where(left,0.0,b)]
        xh,xl=split(jnp.concatenate(blks,axis=0))
        bh,bl=split(bas[pl.ds(g*128,128),:])
        d=dotnt(jnp.concatenate([xh,xl],axis=1),jnp.concatenate([jnp.concatenate([bh,bh],axis=1),jnp.concatenate([bl,jnp.zeros_like(bl)],axis=1)],axis=0))
        d=jnp.where(same,d[:,:128]+d[:,128:],0.0).reshape(8,32,128).sum(axis=0)
        rows.append(jnp.concatenate([d[:RHS],d[RHS:]],axis=1))
    d=exact(jnp.concatenate(rows,axis=0),s2)
    for g in range(n//8): ext[:,pl.ds(pts+g*256,256)]=d[g*RHS:(g+1)*RHS]
    for m in later: m.wait()

def up(x,basis,transfer,upper,chunks=2):
    n=basis.shape[0]
    tra=transfer.reshape(n//8,8,8,128).transpose(0,2,1,3).reshape(n*8,128)
    bas=basis.reshape(n//8,8,16,128).transpose(0,2,1,3).reshape(n*16,128)
    return pl.pallas_call(up_kernel,
        out_shape=(jax.ShapeDtypeStruct((RHS,n*(LEAF+K)),f32),jax.ShapeDtypeStruct(tra.shape,f32),jax.ShapeDtypeStruct(upper.shape,f32)),
        in_specs=[pl.BlockSpec(memory_space=HBM)]*4,
        scratch_shapes=[pltpu.VMEM(x.shape,f32),pltpu.VMEM(bas.shape,f32),pltpu.SemaphoreType.DMA((chunks+1,)),pltpu.SemaphoreType.DMA((2,))],
        compiler_params=pltpu.CompilerParams(vmem_limit_bytes=24<<20),name="up")(in_hbm(x),in_hbm(bas),in_hbm(tra),in_hbm(upper))

def lift_kernel(ext,tra,upt,rep,ejh,ejl,fs):
    nc=upt.shape[0]
    n=tra.shape[0]//8
    per=n//nc
    pts=n*LEAF
    outs=[]
    for u in range(nc):
        es=[tra[pl.ds(((u*per+i)//8)*64+(u*per+i)%8,8,stride=8),:] for i in range(per)]
        w=split(jnp.concatenate([join4(es[i:i+4]) for i in range(0,per,4)],axis=1))
        ejh[pl.ds(u*K,K),:]=w[0]
        ejl[pl.ds(u*K,K),:]=w[1]
        outs.append(mul3(ext[:,pl.ds(pts+u*per*K,per*K)],w))
    cc=exact(jnp.concatenate(outs,axis=1),natural())
    for q in range(8):
        fs[pl.ds(q*nc,nc),:]=upt[:,pl.ds(q*128,128)]
    pr=mul3(cc,split(join4([fs[pl.ds(u,8,stride=nc),:] for u in range(nc)])))
    pay=[cc[4*i:4*i+4] for i in range(4)]+[jnp.concatenate([pr[4*i:4*i+4] for i in range(4)],axis=1)]
    for c in range(rep.shape[0]):
        for i in range(5): rep[c,i]=pay[i]

def lift(ext,tra,upper,copies):
    vm=pl.BlockSpec(memory_space=pltpu.VMEM)
    nc=upper.shape[0]
    join=jax.ShapeDtypeStruct((nc*K,tra.shape[0]//8//nc*K),bf16)
    return pl.pallas_call(lift_kernel,
        out_shape=(jax.ShapeDtypeStruct((copies,5,4,128),f32),join,join),
        in_specs=[vm]*3,out_specs=(vm,)*3,
        scratch_shapes=[pltpu.VMEM((8*nc,128),f32)],
        compiler_params=pltpu.CompilerParams(vmem_limit_bytes=24<<20),name="lift")(ext,tra,upper)

def far_kernel(base,src_h,cpl_h,cb,co,ca,out,table,cpl,src,sem,sem2):
    n=src.shape[1]
    tiles=n*K//128
    skip=n*LEAF
    chunks=sem.shape[0]
    size=cpl.shape[0]//chunks
    def chunk(c): return pltpu.make_async_copy(cpl_h.at[pl.ds(c*size,size),:],cpl.at[pl.ds(c*size,size),:],sem.at[c])
    idx=pltpu.make_async_copy(src_h,src,sem2.at[0])
    idx.start()
    for c in range(chunks): chunk(c).start()
    for w,ref in ((base[2],cb),(1,co),(2-base[2],ca)):
        def body(q,_):
            t=ref[:,pl.ds(pl.multiple_of(skip+q*128,128),128)]
            for m in range(4): table[(w*tiles+q)*4+m]=jnp.concatenate(split(spread4(t,m)),axis=0)
            return 0
        lax.fori_loop(0,tiles,body,0,unroll=8)
    idx.wait()
    per=n//chunks
    first=base[0]
    block32=iota((2*RHS,128),1)//K
    def step(c,_):
        chunk(c).wait()
        for i in range(per):
            t=c*per+i
            off=pl.multiple_of(t*64,64)
            cs=[cpl[pl.ds(off+j,8,stride=8),:] for j in range(8)]
            w=jnp.concatenate([join4(cs[:4]),join4(cs[4:])],axis=1)
            at=[src[j,t]-first for j in range(8)]
            v=jnp.concatenate([pick(block32,[table[at[4*h+p]] for p in range(4)]) for h in range(2)],axis=1)
            d=dotnt(v,jnp.concatenate(split(w),axis=0))
            out[pl.ds(pl.multiple_of(t*RHS,RHS),RHS),:]=d[:RHS]+d[RHS:]
        return 0
    lax.fori_loop(0,chunks,step,0)

def far(base,src,eb,eo,ea,coupling,chunks=2):
    n=coupling.shape[0]
    view=coupling.reshape(n,8,8,128).transpose(0,2,1,3).reshape(n*64,128)
    vm=pl.BlockSpec(memory_space=pltpu.VMEM)
    hbm=pl.BlockSpec(memory_space=HBM)
    return pl.pallas_call(far_kernel,
        out_shape=jax.ShapeDtypeStruct((n*RHS,2*K),f32),
        in_specs=[pl.BlockSpec(memory_space=pltpu.SMEM),hbm,hbm,vm,vm,vm],
        out_specs=vm,
        scratch_shapes=[pltpu.VMEM((3*n,2*RHS,128),bf16),pltpu.VMEM((n*64,128),f32),pltpu.SMEM((8,n),jnp.int32),
            pltpu.SemaphoreType.DMA((chunks,)),pltpu.SemaphoreType.DMA((1,))],
        compiler_params=pltpu.CompilerParams(vmem_limit_bytes=24<<20),name="far")(base,in_hbm(src.T),in_hbm(view),eb,eo,ea)

def gather_kernel(base,csrc,own,other,ccp,out):
    nc=ccp.shape[0]//64
    mine=1-base[2]//2
    block=iota((RHS,128),1)//K
    for u in range(nc):
        cs=[ccp[pl.ds(u*64+j,8,stride=8),:] for j in range(8)]
        vs=[]
        for j in range(8):
            s=csrc[u,j]
            here=lax.rem(s//nc,2)==mine
            place=s//(2*nc)
            v=jnp.concatenate([jnp.where(here,own[place,i],other[place,i]) for i in range(4)],axis=0)
            vs.append(pltpu.roll(v,lax.rem(nc+j%4-lax.rem(s,nc),nc)*K,1))
        v=jnp.concatenate([pick(block,vs[:4]),pick(block,vs[4:])],axis=1)
        out[pl.ds(u*RHS,RHS),:]=mul3(v,split(jnp.concatenate([join4(cs[:4]),join4(cs[4:])],axis=1)))

def gather(base,csrc,own,other,ccp):
    nc=ccp.shape[0]
    view=ccp.reshape(nc,8,8,128).transpose(0,2,1,3).reshape(nc*64,128)
    vm=pl.BlockSpec(memory_space=pltpu.VMEM)
    return pl.pallas_call(gather_kernel,
        out_shape=jax.ShapeDtypeStruct((nc*RHS,K),f32),
        in_specs=[pl.BlockSpec(memory_space=pltpu.SMEM)]*2+[vm]*3,
        cost_estimate=pl.CostEstimate(flops=10**10,bytes_accessed=10**7,transcendentals=0),
        compiler_params=pltpu.CompilerParams(vmem_limit_bytes=24<<20),name="gather")(base,csrc,own,other,view)

def down_kernel(base,s0,s1,s2,s3,cfar,gcp,upt,ejh,ejl,bas,lf,near_ref,out,gs,fs):
    nc=upt.shape[0]; ng=gcp.shape[0]
    n=lf.shape[0]//RHS
    for q in range(8):
        fs[pl.ds(q*nc,nc),:]=upt[:,pl.ds(q*128,128)]
        gs[pl.ds(q*ng,ng),:]=gcp[:,pl.ds(q*128,128)]
    gv=jnp.concatenate([jnp.concatenate([s[:,i*K:(i+1)*K] for i in range(4)],axis=0) for s in (s0,s1,s2,s3)],axis=1)
    gw=join4([gs[pl.ds(jnp.bitwise_xor(base[1],h),8,stride=ng),:] for h in range(ng)])
    gf=mul3(exact(gv,natural()),split(gw))
    wh,wl=split(join4([fs[pl.ds(u,8,stride=nc),:] for u in range(nc)]))
    gh,gl=split(gf)
    down=dotnn(jnp.concatenate([gh,gl,gh],axis=1),jnp.concatenate([wh,wh,wl],axis=0))
    row=iota((128,128),0); col=iota((128,128),1)
    down=exact(down,onehot(col==row//32*32+lax.rem(row,4)*8+lax.rem(row,32)//4))
    row=lax.rem(iota((128,256),0),K); col=iota((128,256),1)
    p1=onehot(row==2*(lax.rem(col,128)//8)+col//128)
    row=lax.rem(iota((2*K,256),0),K); col=iota((2*K,256),1)
    nat=2*(lax.rem(col,128)//8)+col//128
    p2=onehot(row==lax.rem(nat,4)*8+nat//4)
    p12=jnp.concatenate([p1,p1,p2,p2],axis=0)
    left=iota((RHS,128),1)<LEAF
    per=n//nc
    ds=[]
    block=iota((RHS,128),1)//K
    for u in range(nc):
        cf=cfar[pl.ds(u*RHS,RHS),:]+down[:,u*K:(u+1)*K]
        ch,cl=split(cf)
        eh=ejh[pl.ds(u*K,K),:]
        d=dotnn(jnp.concatenate([ch,cl,ch],axis=1),jnp.concatenate([eh,eh,ejl[pl.ds(u*K,K),:]],axis=0))
        ds+=[jnp.where(block==i%4,d[:,i//4*128:i//4*128+128],0.0) for i in range(per)]
    q=dotnn(jnp.concatenate([*split(jnp.concatenate(ds,axis=0)),*split(lf[...])],axis=1),p12)
    same=(iota((256,128),0)//32==lax.rem(iota((256,128),1),8))
    for g in range(n//8):
        z=q[g*128:(g+1)*128].reshape(8,RHS,256)
        z=jnp.stack([z[:,:,:128],z[:,:,128:]],axis=1).reshape(256,128)
        zh,zl=split(jnp.where(same,z,0.0))
        bh,bl=split(bas[pl.ds(g*128,128),:])
        o=dotnn(jnp.concatenate([zh,zl],axis=1),jnp.concatenate([jnp.concatenate([bh,bl],axis=1),jnp.concatenate([bh,jnp.zeros_like(bl)],axis=1)],axis=0))
        o=(o[:,:128]+o[:,128:]).reshape(8,2,RHS,128)
        for m in range(4):
            a=jnp.where(left,o[2*m,0],o[2*m,1])
            c=jnp.where(left,o[2*m+1,0],o[2*m+1,1])
            r=jnp.where(left,a,c)+pltpu.roll(jnp.where(left,c,a),LEAF,1)
            at=pl.ds(g*512+m*128,128)
            out[:,at]=near_ref[:,at]+r

def down(base,sums,cfar,gcp,upper,ejh,ejl,basis,lf,nearv):
    n=basis.shape[0]; nc=upper.shape[0]; ng=gcp.shape[0]
    bas=basis.reshape(n//8,8,16,128).transpose(0,2,1,3).reshape(n*16,128)
    vm=pl.BlockSpec(memory_space=pltpu.VMEM)
    return pl.pallas_call(down_kernel,
        out_shape=jax.ShapeDtypeStruct((RHS,n*LEAF),f32),
        in_specs=[pl.BlockSpec(memory_space=pltpu.SMEM)]+[vm]*12,
        scratch_shapes=[pltpu.VMEM((8*ng,128),f32),pltpu.VMEM((8*nc,128),f32)],
        compiler_params=pltpu.CompilerParams(vmem_limit_bytes=24<<20),name="down")(base,*sums,cfar,gcp,upper,ejh,ejl,bas,lf,nearv)

def across(devs):
    return [[2*i+c for i in range(devs//2)] for c in range(2)]

def per_device(right_sides,near_blocks,near_source,near_count,basis,leaf_source,leaf_coupling,leaf_transfer,cluster_source,cluster_coupling,cluster_transfer,group_coupling):
    both=("group","leaf")
    leaves=near_blocks.shape[0]
    devs=lax.axis_size("leaf")
    every=lax.axis_size(both)
    ng=lax.axis_size("group")
    base=jnp.stack([(lax.axis_index(both)-1)*leaves,lax.axis_index("group"),2*lax.rem(lax.axis_index("leaf")+1,2)]).astype(jnp.int32)
    ext,tra,upper=up(right_sides,basis,leaf_transfer,cluster_transfer)
    eb=lax.ppermute(ext,both,[(i,i^1) for i in range(every)])
    ea=lax.ppermute(ext,both,[p for i in range(1,every-1,2) for p in ((i,i+1),(i+1,i))])
    rep,ejh,ejl=lift(ext,tra,upper,devs//2)
    some=lax.all_to_all(rep,"leaf",0,0,tiled=True,axis_index_groups=across(devs))
    nearv=near(base,near_source,near_count,eb,ext,ea,near_blocks)
    lf=far(base,leaf_source,eb,ext,ea,leaf_coupling)
    some,nearv,lf=lax.optimization_barrier((some,nearv,lf))
    other=lax.ppermute(some,"leaf",[(i,i^1) for i in range(devs)])
    total=some[:,4].sum(axis=0)+other[:,4].sum(axis=0)
    sums=[total]+[lax.ppermute(total,"group",[(i,i^k) for i in range(ng)]) for k in range(1,ng)]
    cfar=gather(base,cluster_source,some,other,cluster_coupling)
    return down(base,sums,cfar,group_coupling.reshape(-1,1024),upper,ejh,ejl,basis,lf,nearv)

def solution(mesh):
    both=("group","leaf")
    one=P(both)
    two=P(both,None)
    three=P(both,None,None)
    return jax.shard_map(per_device,mesh=mesh,
        in_specs=(P(None,both),three,two,one,two,two,three,two,two,three,two,P("group",None,None)),
        out_specs=P(None,both),check_vma=False)
```
